32 devices in a mesh: cells: 8 (over z, y), modes: 4 (over x, core).
Axes of the slice: x: 2, y: 2, z: 4, core: 2. Of those that a mesh axis runs over, the one named last changes fastest.
Arguments:
- theta: float32 [8192, 32], P('modes'), may hold values from -6 to 6
- basis: bfloat16 [16384, 8192], P('cells', 'modes'), may hold values from -0.0625 to 0.0625
- mean_logk: float32 [16384], P('cells'), may hold values from -3 to 3
- face_mult: float32 [3, 16384], P(None, 'cells'), may hold values from 0.3 to 3
- storage: float32 [16384], P('cells'), may hold values from 0.05 to 0.5
- sources: float32 [16384], P('cells'), may hold values from -6 to 6
- obs_data: float32 [16384], P('cells'), may hold values from -6 to 6
- obs_weight: float32 [16384], P('cells'), may hold values from 0.1 to 1
- fault_pairs: int32 [2048, 2], P('cells'), may hold values from 0 to 2047, as said below
- fault_mult: float32 [2048], P('cells'), may hold values from 0.1 to 1
- noise: float32 [8192, 32], P('modes'), may hold values from -6 to 6
Outputs:
- theta_next: float32 [8192, 32], P('modes')
- grad: float32 [8192, 32], P('modes')
- pressure: float32 [32, 16384], P('modes', 'cells')
The draws below stay inside these ranges and needn't reach their ends.
Inputs may be any that keep to these rules, and one draw needn't show every extreme that they name: `fault_pairs`: each block of 256 slots lists its live connections first; each joins a cell (x, y, z) of the block with (x, y+1, z+s), 1 <= s <= 3; the remaining slots pair a cell with itself. Some block is full in every draw.
All inputs are finite; a program needn't handle non-finite values.
Results may differ from the reference program's by a relative error of at most 0.0047.
Values may be sent and summed in bfloat16 or wider, within the bound.
A program may use at most 64 MiB of HBM per device.

```python
import math
import jax
import jax.numpy as jnp
from jax import lax

SX = 1
NY = 32
NZ = 64
MODES = 8192
CHAINS = 32
SWEEPS = 6
THROW = 3
NNC_DEV = 256
C_DEV = 2048
NX = 8
CELLS = 16384
NNC_TOT = 2048
N_CELLS = 8


def draw_fault_pairs(key, part):
    keys = jax.random.split(key, 6)
    total = NNC_DEV * N_CELLS
    layer_x = jax.random.randint(keys[0], (total,), 0, SX)
    layer_y = jax.random.randint(keys[1], (total,), 0, NY - 1)
    layer_z = jax.random.randint(keys[2], (total,), 0, NZ - THROW)
    throw_z = jax.random.randint(keys[3], (total,), 1, THROW + 1)
    slot = jnp.arange(total) % NNC_DEV
    block = jnp.arange(total) // NNC_DEV
    layer_x = jnp.where(slot == 0, 0, jnp.where(slot == 1, SX - 1, layer_x))
    layer_y = jnp.where(slot == 0, 0, jnp.where(slot == 1, NY - 2, layer_y))
    layer_z = jnp.where(slot == 0, 0, jnp.where(slot == 1, NZ - 1 - THROW, layer_z))
    throw_z = jnp.where(slot < 2, THROW, throw_z)
    near_cell = (layer_x * NY + layer_y) * NZ + layer_z
    far_cell = (layer_x * NY + layer_y + 1) * NZ + layer_z + throw_z
    live_count = jax.random.randint(keys[4], (N_CELLS,), NNC_DEV // 4, NNC_DEV + 1)
    full_block = jax.random.randint(keys[5], (), 0, N_CELLS)
    live_count = jnp.where(jnp.arange(N_CELLS) == full_block, NNC_DEV, live_count)
    keep = slot < live_count[block]
    far_cell = jnp.where(keep, far_cell, near_cell)
    return jnp.stack([near_cell, far_cell], 1).astype(jnp.int32)


def block_levels(stream_key, shape, shards, low, high):
    level, own = 1.0, jax.random.fold_in(stream_key, 6)
    for dim, parts in shards:
        steps = jnp.exp(jax.random.uniform(jax.random.fold_in(own, dim), (parts,), jnp.float32, low / len(shards), high / len(shards)))
        level = level * jnp.repeat(steps, shape[dim] // parts).reshape([-1 if axis == dim else 1 for axis in range(len(shape))])
    return level


def centred(rng, extent, spread, limit, cuts=(), held_as=jnp.bfloat16):
    factor_of = block_levels(rng, extent, cuts, -0.22, 0.18) if cuts else 1.0
    values = jax.random.normal(rng, extent, jnp.float32) * spread * factor_of
    return jnp.minimum(jnp.maximum(values, -limit), limit).astype(held_as)


def setup_inputs(seed: int = 0) -> dict:
    streams_of = jax.random.split(jax.random.key(seed), 12)
    theta = centred(streams_of[0], (MODES, CHAINS), 1.0, 6.0, ((0, 4),), jnp.float32)
    basis = centred(streams_of[1], (CELLS, MODES), MODES ** -0.5, 0.0625, ((0, 8), (1, 4)))
    mean_logk = centred(streams_of[2], (CELLS,), 0.5, 3.0, ((0, 8),), jnp.float32)
    face_mult = jnp.clip(jnp.exp(math.log(3.0) - 2.3025851 * jax.random.uniform(streams_of[3], (3, CELLS), jnp.float32) ** block_levels(streams_of[3], (3, CELLS), ((1, 8),), -0.2, 0.2)), 0.3, 3.0)
    storage = jnp.clip(jnp.exp(math.log(0.5) - 2.3025851 * jax.random.uniform(streams_of[4], (CELLS,), jnp.float32) ** block_levels(streams_of[4], (CELLS,), ((0, 8),), -0.2, 0.2)), 0.05, 0.5)
    sources = centred(streams_of[5], (CELLS,), 1.0, 6.0, ((0, 8),), jnp.float32)
    obs_data = centred(streams_of[6], (CELLS,), 1.0, 6.0, ((0, 8),), jnp.float32)
    obs_weight = jnp.clip(jnp.exp(math.log(1.0) - 2.3025851 * jax.random.uniform(streams_of[7], (CELLS,), jnp.float32) ** block_levels(streams_of[7], (CELLS,), ((0, 8),), -0.2, 0.2)), 0.1, 1.0)
    fault_pairs = draw_fault_pairs(jax.random.fold_in(streams_of[11], 71), 0)
    fault_mult = jnp.clip(jnp.exp(math.log(1.0) - 2.3025851 * jax.random.uniform(streams_of[9], (NNC_TOT,), jnp.float32) ** block_levels(streams_of[9], (NNC_TOT,), ((0, 8),), -0.2, 0.2)), 0.1, 1.0)
    noise = centred(streams_of[10], (MODES, CHAINS), 1.0, 6.0, ((0, 4),), jnp.float32)
    return dict(theta=theta, basis=basis, mean_logk=mean_logk, face_mult=face_mult, storage=storage, sources=sources, obs_data=obs_data, obs_weight=obs_weight, fault_pairs=fault_pairs, fault_mult=fault_mult, noise=noise)


LOW_EIG = 0.1
HIGH_EIG = 1.9
STEP_SIZE = 0.01

def harmonic(left, right):
    return 2.0 * left * right / (left + right)

def pad_axis(array, axis, before, after):
    widths = [(0, 0)] * array.ndim
    widths[axis] = (before, after)
    return jnp.pad(array, widths)

def transmit(perm_ext, mult_ext, mult_y, mult_z, near_cell, far_cell, fault_mult, depth_y, depth_z):
    chains_n = perm_ext.shape[0]
    layers = perm_ext.shape[1] - 2
    trans_x = harmonic(perm_ext[:, :-1], perm_ext[:, 1:]) * mult_ext[:, :-1]
    perm = perm_ext[:, 1:-1].reshape(chains_n, layers, depth_y, depth_z)
    trans_y = harmonic(perm[:, :, :-1], perm[:, :, 1:]) * mult_y.reshape(1, layers, depth_y, depth_z)[:, :, :-1]
    trans_z = harmonic(perm[..., :-1], perm[..., 1:]) * mult_z.reshape(1, layers, depth_y, depth_z)[..., :-1]
    flat = perm.reshape(chains_n, -1)
    live = fault_mult * (near_cell != far_cell).astype(fault_mult.dtype)
    trans_n = harmonic(flat[:, near_cell], flat[:, far_cell]) * live[None]
    return (trans_x, trans_y, trans_z, trans_n)

def diagonal_of(trans, storage, near_cell, far_cell, depth_y, depth_z):
    trans_x, trans_y, trans_z, trans_n = trans
    chains_n = trans_x.shape[0]
    layers = trans_x.shape[1] - 1
    total = (trans_x[:, 1:] + trans_x[:, :-1]).reshape(chains_n, layers, depth_y, depth_z)
    total = total + pad_axis(trans_y, 2, 0, 1) + pad_axis(trans_y, 2, 1, 0)
    total = total + pad_axis(trans_z, 3, 0, 1) + pad_axis(trans_z, 3, 1, 0)
    total = total.reshape(chains_n, -1)
    total = total.at[:, near_cell].add(trans_n).at[:, far_cell].add(trans_n)
    return total + storage[None]

def operate(field_ext, trans, storage, near_cell, far_cell, depth_y, depth_z):
    trans_x, trans_y, trans_z, trans_n = trans
    chains_n = field_ext.shape[0]
    layers = field_ext.shape[1] - 2
    flux_x = trans_x * (field_ext[:, :-1] - field_ext[:, 1:])
    result = (flux_x[:, 1:] - flux_x[:, :-1]).reshape(chains_n, layers, depth_y, depth_z)
    field = field_ext[:, 1:-1].reshape(chains_n, layers, depth_y, depth_z)
    flux_y = trans_y * (field[:, :, :-1] - field[:, :, 1:])
    result = result + pad_axis(flux_y, 2, 0, 1) - pad_axis(flux_y, 2, 1, 0)
    flux_z = trans_z * (field[..., :-1] - field[..., 1:])
    result = result + pad_axis(flux_z, 3, 0, 1) - pad_axis(flux_z, 3, 1, 0)
    result = result.reshape(chains_n, -1)
    flat = field.reshape(chains_n, -1)
    flux_n = trans_n * (flat[:, near_cell] - flat[:, far_cell])
    result = result.at[:, near_cell].add(flux_n).at[:, far_cell].add(-flux_n)
    return result + storage[None] * flat

def solve(rhs, apply_fn, diag):
    center = 0.5 * (HIGH_EIG + LOW_EIG)
    half = 0.5 * (HIGH_EIG - LOW_EIG)
    sigma = center / half
    resid = rhs / diag
    direction = resid / center
    iterate = jnp.zeros_like(rhs)
    rho = jnp.asarray(1.0 / sigma, dtype=rhs.dtype)

    def sweep_step(sweep, carry):
        iterate, resid, direction, rho = carry
        iterate = iterate + direction
        resid = resid - apply_fn(direction) / diag
        rho_next = 1.0 / (2.0 * sigma - rho)
        direction = rho_next * rho * direction + 2.0 * rho_next / half * resid
        return (iterate, resid, direction, rho_next)
    iterate, resid, direction, rho = lax.fori_loop(0, SWEEPS, sweep_step, (iterate, resid, direction, rho))
    return iterate + direction

def gradient_of(pres_ext, adj_ext, perm_ext, trans, near_cell, far_cell, depth_y, depth_z):
    trans_x, trans_y, trans_z, trans_n = trans
    chains_n = perm_ext.shape[0]
    layers = perm_ext.shape[1] - 2
    coef_x = -(adj_ext[:, :-1] - adj_ext[:, 1:]) * (pres_ext[:, :-1] - pres_ext[:, 1:]) * trans_x / (perm_ext[:, :-1] + perm_ext[:, 1:])
    result = coef_x[:, 1:] * perm_ext[:, 2:] + coef_x[:, :-1] * perm_ext[:, :-2]
    result = result.reshape(chains_n, layers, depth_y, depth_z)
    shape4 = (chains_n, layers, depth_y, depth_z)
    perm = perm_ext[:, 1:-1].reshape(shape4)
    pres = pres_ext[:, 1:-1].reshape(shape4)
    adj = adj_ext[:, 1:-1].reshape(shape4)
    coef_y = -(adj[:, :, :-1] - adj[:, :, 1:]) * (pres[:, :, :-1] - pres[:, :, 1:]) * trans_y / (perm[:, :, :-1] + perm[:, :, 1:])
    result = result + pad_axis(coef_y * perm[:, :, 1:], 2, 0, 1) + pad_axis(coef_y * perm[:, :, :-1], 2, 1, 0)
    coef_z = -(adj[..., :-1] - adj[..., 1:]) * (pres[..., :-1] - pres[..., 1:]) * trans_z / (perm[..., :-1] + perm[..., 1:])
    result = result + pad_axis(coef_z * perm[..., 1:], 3, 0, 1) + pad_axis(coef_z * perm[..., :-1], 3, 1, 0)
    result = result.reshape(chains_n, -1)
    perm_f = perm.reshape(chains_n, -1)
    pres_f = pres.reshape(chains_n, -1)
    adj_f = adj.reshape(chains_n, -1)
    perm_a = perm_f[:, near_cell]
    perm_b = perm_f[:, far_cell]
    coef_n = -(adj_f[:, near_cell] - adj_f[:, far_cell]) * (pres_f[:, near_cell] - pres_f[:, far_cell]) * trans_n / (perm_a + perm_b)
    return result.at[:, near_cell].add(coef_n * perm_b).at[:, far_cell].add(coef_n * perm_a)

def extend_zero(array):
    return jnp.pad(array, ((0, 0), (1, 1), (0, 0)))

def reference(theta, basis, mean_logk, face_mult, storage, sources, obs_data, obs_weight, fault_pairs, fault_mult, noise):
    theta_b = theta.astype(jnp.bfloat16)
    theta_w = theta_b.astype(jnp.float32)
    blocks = basis.reshape(N_CELLS, C_DEV, MODES)

    def field_block(block):
        return jnp.dot(block.astype(jnp.float32), theta_w, precision=lax.Precision.HIGHEST)
    partial_field = lax.map(field_block, blocks).reshape(CELLS, -1)
    logk = mean_logk[None] + partial_field.T
    chains_n = logk.shape[0]
    faces = NY * NZ
    offset = (jnp.arange(NNC_TOT) // NNC_DEV * C_DEV).astype(jnp.int32)
    near_cell = fault_pairs[:, 0].astype(jnp.int32) + offset
    far_cell = fault_pairs[:, 1].astype(jnp.int32) + offset
    perm = jnp.exp(logk).reshape(chains_n, NX, faces)
    perm_ext = extend_zero(perm)
    mult_ext = extend_zero(face_mult[0].reshape(1, NX, faces))
    trans = transmit(perm_ext, mult_ext, face_mult[1], face_mult[2], near_cell, far_cell, fault_mult, NY, NZ)
    diag = diagonal_of(trans, storage, near_cell, far_cell, NY, NZ)

    def apply_fn(field):
        return operate(extend_zero(field.reshape(chains_n, NX, faces)), trans, storage, near_cell, far_cell, NY, NZ)
    rhs = jnp.broadcast_to(sources[None], logk.shape)
    pressure = solve(rhs, apply_fn, diag)
    misfit = obs_weight[None] * (pressure - obs_data[None])
    adjoint = solve(misfit, apply_fn, diag)
    pres_ext = extend_zero(pressure.reshape(chains_n, NX, faces))
    adj_ext = extend_zero(adjoint.reshape(chains_n, NX, faces))
    glogk = gradient_of(pres_ext, adj_ext, perm_ext, trans, near_cell, far_cell, NY, NZ)
    glogk_b = glogk.astype(jnp.bfloat16)
    grad_blocks = jnp.transpose(glogk_b.reshape(chains_n, N_CELLS, C_DEV), (1, 0, 2))

    def grad_step(total, pair):
        gpiece, bpiece = pair
        return (total + jnp.dot(gpiece.astype(jnp.float32), bpiece.astype(jnp.float32), precision=lax.Precision.HIGHEST), None)
    grad_rows, unused = lax.scan(grad_step, jnp.zeros((chains_n, MODES), jnp.float32), (grad_blocks, blocks))
    grad = grad_rows.T
    theta_next = theta - STEP_SIZE * (grad + theta) + math.sqrt(2.0 * STEP_SIZE) * noise
    return (theta_next, grad, pressure)
```

```python
import functools
import math

import jax
import jax.numpy as jnp
from jax import lax
from jax.experimental import pallas as pl
from jax.experimental.pallas import tpu as pltpu
from jax.sharding import PartitionSpec as P

NY = 32
NZ = 64
SWEEPS = 6


LOW_EIG = 0.1
HIGH_EIG = 1.9
STEP_SIZE = 0.01


def extended(block, sides, width):
    for axis, dim in sides:
        count = lax.axis_size(axis)
        forward = [(i, i + 1) for i in range(count - 1)]
        backward = [(target, source) for source, target in forward]
        low = lax.ppermute(
            lax.slice_in_dim(block, block.shape[dim] - width, None, axis=dim), axis, forward
        )
        high = lax.ppermute(lax.slice_in_dim(block, 0, width, axis=dim), axis, backward)
        block = jnp.concatenate([low, block, high], axis=dim)
    return block


def harmonic(left, right):
    return 2.0 * left * right / (left + right)


def pad_axis(array, axis, before, after):
    widths = [(0, 0)] * array.ndim
    widths[axis] = (before, after)
    return jnp.pad(array, widths)


def transmit(perm_ext, mult_ext, mult_y, mult_z, near_cell, far_cell, fault_mult, depth_y, depth_z):
    chains_n = perm_ext.shape[0]
    layers = perm_ext.shape[1] - 2
    trans_x = harmonic(perm_ext[:, :-1], perm_ext[:, 1:]) * mult_ext[:, :-1]
    perm = perm_ext[:, 1:-1].reshape(chains_n, layers, depth_y, depth_z)
    trans_y = (
        harmonic(perm[:, :, :-1], perm[:, :, 1:])
        * mult_y.reshape(1, layers, depth_y, depth_z)[:, :, :-1]
    )
    trans_z = (
        harmonic(perm[..., :-1], perm[..., 1:])
        * mult_z.reshape(1, layers, depth_y, depth_z)[..., :-1]
    )
    flat = perm.reshape(chains_n, -1)
    live = fault_mult * (near_cell != far_cell).astype(jnp.float32)
    trans_n = harmonic(flat[:, near_cell], flat[:, far_cell]) * live[None]
    return (trans_x, trans_y, trans_z, trans_n)


def diagonal_of(trans, storage, near_cell, far_cell, depth_y, depth_z):
    trans_x, trans_y, trans_z, trans_n = trans
    chains_n = trans_x.shape[0]
    layers = trans_x.shape[1] - 1
    total = (trans_x[:, 1:] + trans_x[:, :-1]).reshape(chains_n, layers, depth_y, depth_z)
    total = total + pad_axis(trans_y, 2, 0, 1) + pad_axis(trans_y, 2, 1, 0)
    total = total + pad_axis(trans_z, 3, 0, 1) + pad_axis(trans_z, 3, 1, 0)
    total = total.reshape(chains_n, -1)
    total = total.at[:, near_cell].add(trans_n).at[:, far_cell].add(trans_n)
    return total + storage[None]


def operate(field_ext, trans, storage, near_cell, far_cell, depth_y, depth_z):
    trans_x, trans_y, trans_z, trans_n = trans
    chains_n = field_ext.shape[0]
    layers = field_ext.shape[1] - 2
    flux_x = trans_x * (field_ext[:, :-1] - field_ext[:, 1:])
    result = (flux_x[:, 1:] - flux_x[:, :-1]).reshape(chains_n, layers, depth_y, depth_z)
    field = field_ext[:, 1:-1].reshape(chains_n, layers, depth_y, depth_z)
    flux_y = trans_y * (field[:, :, :-1] - field[:, :, 1:])
    result = result + pad_axis(flux_y, 2, 0, 1) - pad_axis(flux_y, 2, 1, 0)
    flux_z = trans_z * (field[..., :-1] - field[..., 1:])
    result = result + pad_axis(flux_z, 3, 0, 1) - pad_axis(flux_z, 3, 1, 0)
    result = result.reshape(chains_n, -1)
    flat = field.reshape(chains_n, -1)
    flux_n = trans_n * (flat[:, near_cell] - flat[:, far_cell])
    result = result.at[:, near_cell].add(flux_n).at[:, far_cell].add(-flux_n)
    return result + storage[None] * flat


def solve(rhs, apply_fn, diag):
    center = 0.5 * (HIGH_EIG + LOW_EIG)
    half = 0.5 * (HIGH_EIG - LOW_EIG)
    sigma = center / half
    resid = rhs / diag
    direction = resid / center
    iterate = jnp.zeros_like(rhs)
    rho = jnp.asarray(1.0 / sigma, dtype=rhs.dtype)

    def sweep_step(sweep, carry):
        iterate, resid, direction, rho = carry
        iterate = iterate + direction
        resid = resid - apply_fn(direction) / diag
        rho_next = 1.0 / (2.0 * sigma - rho)
        direction = rho_next * rho * direction + 2.0 * rho_next / half * resid
        return (iterate, resid, direction, rho_next)

    iterate, resid, direction, rho = lax.fori_loop(
        0, SWEEPS, sweep_step, (iterate, resid, direction, rho)
    )
    return iterate + direction


def gradient_of(pres_ext, adj_ext, perm_ext, trans, near_cell, far_cell, depth_y, depth_z):
    trans_x, trans_y, trans_z, trans_n = trans
    chains_n = perm_ext.shape[0]
    layers = perm_ext.shape[1] - 2
    coef_x = (
        -(adj_ext[:, :-1] - adj_ext[:, 1:])
        * (pres_ext[:, :-1] - pres_ext[:, 1:])
        * trans_x
        / (perm_ext[:, :-1] + perm_ext[:, 1:])
    )
    result = coef_x[:, 1:] * perm_ext[:, 2:] + coef_x[:, :-1] * perm_ext[:, :-2]
    result = result.reshape(chains_n, layers, depth_y, depth_z)
    shape4 = (chains_n, layers, depth_y, depth_z)
    perm = perm_ext[:, 1:-1].reshape(shape4)
    pres = pres_ext[:, 1:-1].reshape(shape4)
    adj = adj_ext[:, 1:-1].reshape(shape4)
    coef_y = (
        -(adj[:, :, :-1] - adj[:, :, 1:])
        * (pres[:, :, :-1] - pres[:, :, 1:])
        * trans_y
        / (perm[:, :, :-1] + perm[:, :, 1:])
    )
    result = (
        result
        + pad_axis(coef_y * perm[:, :, 1:], 2, 0, 1)
        + pad_axis(coef_y * perm[:, :, :-1], 2, 1, 0)
    )
    coef_z = (
        -(adj[..., :-1] - adj[..., 1:])
        * (pres[..., :-1] - pres[..., 1:])
        * trans_z
        / (perm[..., :-1] + perm[..., 1:])
    )
    result = (
        result
        + pad_axis(coef_z * perm[..., 1:], 3, 0, 1)
        + pad_axis(coef_z * perm[..., :-1], 3, 1, 0)
    )
    result = result.reshape(chains_n, -1)
    perm_f = perm.reshape(chains_n, -1)
    pres_f = pres.reshape(chains_n, -1)
    adj_f = adj.reshape(chains_n, -1)
    perm_a = perm_f[:, near_cell]
    perm_b = perm_f[:, far_cell]
    coef_n = (
        -(adj_f[:, near_cell] - adj_f[:, far_cell])
        * (pres_f[:, near_cell] - pres_f[:, far_cell])
        * trans_n
        / (perm_a + perm_b)
    )
    return result.at[:, near_cell].add(coef_n * perm_b).at[:, far_cell].add(coef_n * perm_a)


def physics(logk, face_mult, storage, sources, obs_data, obs_weight, fault_pairs, fault_mult):
    chains_n, cells_n = logk.shape
    faces = NY * NZ
    layers = cells_n // faces
    near_cell = fault_pairs[:, 0]
    far_cell = fault_pairs[:, 1]
    perm = jnp.exp(logk).reshape(chains_n, layers, faces)
    stacked = jnp.concatenate([perm, face_mult[0].reshape(1, layers, faces)], 0)
    stacked_ext = extended(stacked, (("cells", 1),), 1)
    perm_ext = stacked_ext[:chains_n]
    mult_ext = stacked_ext[chains_n:]
    trans = transmit(
        perm_ext, mult_ext, face_mult[1], face_mult[2], near_cell, far_cell, fault_mult, NY, NZ
    )
    diag = diagonal_of(trans, storage, near_cell, far_cell, NY, NZ)

    def apply_fn(field):
        field_ext = extended(field.reshape(chains_n, layers, faces), (("cells", 1),), 1)
        return operate(field_ext, trans, storage, near_cell, far_cell, NY, NZ)

    rhs = jnp.broadcast_to(sources[None], (chains_n, cells_n))
    pressure = solve(rhs, apply_fn, diag)
    misfit = obs_weight[None] * (pressure - obs_data[None])
    adjoint = solve(misfit, apply_fn, diag)
    both = jnp.concatenate([pressure, adjoint], 0).reshape(2 * chains_n, layers, faces)
    both_ext = extended(both, (("cells", 1),), 1)
    glogk = gradient_of(
        both_ext[:chains_n], both_ext[chains_n:], perm_ext, trans, near_cell, far_cell, NY, NZ
    )
    return (pressure, glogk)


def body(
    theta,
    basis,
    mean_logk,
    face_mult,
    storage,
    sources,
    obs_data,
    obs_weight,
    fault_pairs,
    fault_mult,
    noise,
):
    chains = theta.shape[1]
    share = chains // lax.axis_size("modes")
    theta_b = theta.astype(jnp.bfloat16)
    local_field = lax.dot_general(
        theta_b, basis, (((0,), (1,)), ((), ())), preferred_element_type=jnp.float32
    )
    partial_field = lax.psum(local_field, "modes")
    logk = mean_logk[None] + partial_field
    pressure, glogk = physics(
        logk, face_mult, storage, sources, obs_data, obs_weight, fault_pairs, fault_mult
    )
    glogk_b = glogk.astype(jnp.bfloat16)
    grad_rows = jnp.dot(glogk_b, basis, preferred_element_type=jnp.float32)
    pressure_out = lax.dynamic_slice_in_dim(pressure, lax.axis_index("modes") * share, share, 0)
    mode_grad = lax.psum(grad_rows, "cells")
    grad = mode_grad.T
    theta_next = theta - STEP_SIZE * (grad + theta) + math.sqrt(2.0 * STEP_SIZE) * noise
    return (theta_next, grad, pressure_out)


LANES = 128
STAT = 4


def chebyshev(rhs, inv, sweep):
    center = 0.5 * (HIGH_EIG + LOW_EIG)
    half = 0.5 * (HIGH_EIG - LOW_EIG)
    sigma = center / half
    resid = [b * v for b, v in zip(rhs, inv)]
    direction = [v * (1.0 / center) for v in resid]
    iterate = None
    rho = 1.0 / sigma
    for _ in range(SWEEPS):
        iterate = direction if iterate is None else [a + b for a, b in zip(iterate, direction)]
        resid = [v - d + s for v, d, s in zip(resid, direction, sweep(direction))]
        rho_next = 1.0 / (2.0 * sigma - rho)
        direction = [
            (rho_next * rho) * d + (2.0 * rho_next / half) * v for d, v in zip(direction, resid)
        ]
        rho = rho_next
    return [a + b for a, b in zip(iterate, direction)]


def chain_physics(nx, rows, logk_of, static_of, fault_row, parts, fault_s, coef, pres_s, before_fields, after_pressure, glogk_s):
    hi_iota = lax.broadcasted_iota(jnp.int32, (rows, LANES), 0)
    lo_iota = lax.broadcasted_iota(jnp.int32, (LANES, LANES), 0)
    for x in range(nx):
        got = None
        for part in range(parts):
            near = fault_row(x, part).astype(jnp.int32)
            shift = fault_row(x, parts + part).astype(jnp.int32) - near - NZ
            lo = (lo_iota == (near & (LANES - 1))).astype(jnp.float32)
            hot = jnp.where(hi_iota == (near >> 7), fault_row(x, 2 * parts + part), 0.0)
            left = jnp.concatenate([jnp.where(shift == s, hot, 0.0) for s in (1, 2, 3)], 0)
            term = lax.dot_general(
                left, lo, (((1,), (1,)), ((), ())),
                precision=lax.Precision.HIGHEST, preferred_element_type=jnp.float32,
            )
            got = term if got is None else got + term
        for s in range(3):
            fault_s[s, pl.ds(x * rows, rows), :] = got[s * rows : (s + 1) * rows]

    before_fields()
    lane = lax.broadcasted_iota(jnp.int32, (nx, LANES), 1)
    xpos = lax.broadcasted_iota(jnp.int32, (nx, LANES), 0)
    low = lane < NZ
    zpos = jnp.where(low, lane, lane - NZ)

    def fwd_lane(v, s):
        return pltpu.roll(v, LANES - s, 1)

    def bwd_lane(v, s):
        return pltpu.roll(v, s, 1)

    def halves(vs):
        return [pltpu.roll(v, NZ, 1) for v in vs]

    def up_y(vs, hs):
        n = len(vs)
        return [jnp.where(low, hs[r], hs[(r + 1) % n]) for r in range(n)]

    def down_y(vs, hs):
        n = len(vs)
        return [jnp.where(low, hs[r - 1], hs[r]) for r in range(n)]

    def ahead(vs, hs=None):
        hs = halves(vs) if hs is None else hs
        wy = up_y(vs, hs)
        return (
            [pltpu.roll(v, nx - 1, 0) for v in vs],
            wy,
            [fwd_lane(v, 1) for v in vs],
            [fwd_lane(w, 1) for w in wy],
            [fwd_lane(w, 2) for w in wy],
            [fwd_lane(w, 3) for w in wy],
        )

    def behind_one(kind, vs):
        if kind == 0:
            return [pltpu.roll(v, 1, 0) for v in vs]
        if kind == 2:
            return [bwd_lane(v, 1) for v in vs]
        wy = down_y(vs, halves(vs))
        return wy if kind == 1 else [bwd_lane(w, kind - 2) for w in wy]

    every = range(rows)
    perm = [jnp.exp(logk_of(r)) for r in every]
    perm_a = ahead(perm)
    zero = jnp.zeros((nx, LANES), jnp.float32)
    diag = [static_of(3, r) for r in every]
    for k in range(6):
        trans = []
        for r in every:
            if k < 3:
                m = static_of(k, r)
            else:
                m = fault_s[k - 3, pl.ds(r, nx, stride=rows), :]
            if k == 0:
                live = xpos < nx - 1
            elif k == 1:
                live = None if r < rows - 1 else low
            elif k == 2:
                live = zpos < NZ - 1
            else:
                live = m > 0.0
            a, b = perm[r], perm_a[k][r]
            total = a + b
            t = 2.0 * a * b / total * m
            if live is not None:
                t = jnp.where(live, t, zero)
            g = t / total
            coef[12 + k, r] = g
            trans.append(t)
        back = behind_one(k, trans)
        for r in every:
            coef[2 * k, r] = trans[r]
            coef[2 * k + 1, r] = back[r]
            diag[r] = diag[r] + trans[r] + back[r]
    inv = [1.0 / v for v in diag]
    for k in range(12):
        for r in every:
            coef[k, r] = coef[k, r] * inv[r]

    def sweep(d):
        hs = halves(d)
        up = up_y(d, hs)
        dn = down_y(d, hs)
        out = []
        for r in every:
            v = d[r]
            acc = coef[0, r] * pltpu.roll(v, nx - 1, 0) + coef[1, r] * pltpu.roll(v, 1, 0)
            acc2 = coef[2, r] * up[r] + coef[3, r] * dn[r]
            acc = acc + coef[4, r] * fwd_lane(v, 1) + coef[5, r] * bwd_lane(v, 1)
            for s in (1, 2, 3):
                acc2 = acc2 + coef[4 + 2 * s, r] * fwd_lane(up[r], s)
                acc = acc + coef[5 + 2 * s, r] * bwd_lane(dn[r], s)
            out.append(acc + acc2)
        return out

    pres = chebyshev([static_of(4, r) for r in every], inv, sweep)
    for r in every:
        pres_s[pl.ds(r, nx, stride=rows), :] = pres[r]
    after_pressure()
    misfit = [static_of(6, r) * (pres[r] - static_of(5, r)) for r in every]
    adj = chebyshev(misfit, inv, sweep)
    pres_a = ahead(pres)
    adj_a = ahead(adj)
    perm_a = ahead(perm)
    total = [zero for r in every]
    for k in range(6):
        q = [
            -(adj[r] - adj_a[k][r]) * (pres[r] - pres_a[k][r]) * coef[12 + k, r] for r in every
        ]
        back = behind_one(k, [q[r] * perm[r] for r in every])
        for r in every:
            total[r] = total[r] + q[r] * perm_a[k][r] + back[r]
    for r in every:
        glogk_s[pl.ds(r, nx, stride=rows), :] = total[r]


def fused_kernel(
    nd, nm, rows, parts, axes,
    theta_hbm, basis_hbm, mean_hbm, face_hbm, storage_hbm, sources_hbm, data_hbm, weight_hbm,
    pairs_hbm, mult_hbm,
    grad_out, pres_out,
    basis, theta_v, mean_v, face_v, pairs_v, mult_v, own_stat, stat, part, part_in, mine, field,
    fault_s, coef, pres_s, pres_in, glogk_s, gl_b, gl_all, gl_f, gsend, gin, gfin, gall,
    load_sem, copy_sem, send_sem, recv_sem,
):
    cells_ax, modes_ax = axes
    me, mo = lax.axis_index(cells_ax), lax.axis_index(modes_ax)
    chains, modes_n = theta_v.shape
    cells = rows * LANES
    blk = cells // nd
    pairs_n = nm // 2
    core, group = lax.rem(mo, 2), lax.div(mo, 2)
    high, low = lax.div(me, 2), lax.rem(me, 2)
    srows = STAT * rows
    small = [
        (theta_hbm, theta_v),
        (face_hbm, face_v),
        (storage_hbm, own_stat.at[0, pl.ds(3 * rows, rows)]),
        (sources_hbm, own_stat.at[1, pl.ds(0, rows)]),
        (data_hbm, own_stat.at[1, pl.ds(rows, rows)]),
        (weight_hbm, own_stat.at[1, pl.ds(2 * rows, rows)]),
        (pairs_hbm, pairs_v),
        (mult_hbm, mult_v),
        (mean_hbm, mean_v),
    ]
    small = [pltpu.make_async_copy(a, b, load_sem.at[i]) for i, (a, b) in enumerate(small)]
    loads = [
        pltpu.make_async_copy(
            basis_hbm.at[pl.ds(k * blk, blk)], basis.at[pl.ds(k * blk, blk)], copy_sem.at[k]
        )
        for k in range(nd)
    ]
    for load in small + loads:
        load.start()

    def block(i, size):
        return pl.ds(pl.multiple_of(i * size, size), size)

    steps = sorted(
        ((dz, dy) for dz in range(nd // 2) for dy in range(2)),
        key=lambda t: -(min(t[0], nd // 2 - t[0]) + t[1]),
    )

    def cell_of(step):
        return lax.rem(high + step[0], nd // 2) * 2 + lax.rem(low + step[1], 2)

    near = [t for t in steps if t != (0, 0)]
    wide = sorted(
        ((t, dx) for t in steps for dx in range(pairs_n) if (t, dx) != ((0, 0), 0)),
        key=lambda w: -(min(w[0][0], nd // 2 - w[0][0]) + w[0][1] + (w[1] > 0)),
    )
    mate = {modes_ax: group * 2 + 1 - core}

    def group_of(dx):
        return lax.rem(group + dx, pairs_n)

    def wide_peer(t, dx):
        return {cells_ax: cell_of(t), modes_ax: group_of(dx) * 2 + core}

    barrier = pltpu.get_barrier_semaphore()
    for peer in [wide_peer(t, dx) for t, dx in wide] + [mate]:
        pl.semaphore_signal(barrier, inc=1, device_id=peer, device_id_type=pl.DeviceIdType.MESH)
    greeted = len(wide) + 1
    sent = []
    count = [0]

    def send(src, dst, peer):
        slot = count[0]
        count[0] += 1
        copy = pltpu.make_async_remote_copy(
            src_ref=src, dst_ref=dst, send_sem=send_sem.at[slot], recv_sem=recv_sem.at[slot],
            device_id=peer, device_id_type=pl.DeviceIdType.MESH,
        )
        copy.start()
        sent.append(copy)
        return copy

    def cell_peer(t):
        return {cells_ax: cell_of(t)}

    for load in small:
        load.wait()
    for f in range(3):
        own_stat[0, f * rows : (f + 1) * rows, :] = jnp.concatenate(
            [face_v[f : f + 1, r * LANES : (r + 1) * LANES] for r in range(rows)], 0
        )
    pairs = pairs_v[...].astype(jnp.float32)
    spare = rows - 3 * parts
    own_stat[1, 3 * rows :, :] = jnp.concatenate(
        [pairs[e : e + 1, p * LANES : (p + 1) * LANES] for e in range(2) for p in range(parts)]
        + [mult_v[...]]
        + ([jnp.zeros((spare, LANES), jnp.float32)] if spare else []),
        0,
    )
    stat[core, block(me, srows), :] = own_stat[core]
    share = chains // nm
    theta_t = jnp.concatenate(
        [
            theta_v[(2 * x + c) * share : (2 * x + c + 1) * share, :]
            for c in range(2)
            for x in range(pairs_n)
        ],
        0,
    ).T.astype(jnp.bfloat16)
    half = rows // 2
    lead = 1
    stat_got, part_got = [], []
    for k in range(nd):
        loads[k].wait()
        got = jnp.dot(
            basis[pl.ds(k * blk, blk), :], theta_t, preferred_element_type=jnp.float32
        ).T
        for t in range(blk // LANES):
            r = k * (blk // LANES) + t
            part[r // half, pl.ds(r % half, chains, stride=half), :] = (
                got[:, t * LANES : (t + 1) * LANES]
            )
        if k == lead - 1:
            pl.semaphore_wait(barrier, greeted)
            stat_got = [
                send(own_stat.at[core], stat.at[core, block(me, srows)], cell_peer(t))
                for t in near
            ]
        if (k + 1) % (nd // 2) == 0:
            h = k // (nd // 2)
            part_got.append(
                send(part.at[h, block(1 - core, chains // 2 * half)], part_in.at[h], mate)
            )
    mean = 1.0 / pairs_n * mean_v[...]
    for h in range(2):
        total = part[h, block(core, chains // 2 * half), :].reshape(chains // 2, half, LANES)
        total = total + mean[h * half : (h + 1) * half][None]
        part_got[h].wait_recv()
        total = total + part_in[h].reshape(chains // 2, half, LANES)
        mine[:, h * half : (h + 1) * half, :] = total
    field_got = [
        send(
            mine.at[group_of(dx) * nd + cell_of(t)], field.at[group, block(me, rows)],
            wide_peer(t, dx),
        )
        for t, dx in wide
    ]
    field[group, block(me, rows), :] = mine[group * nd + me]
    for copy in stat_got:
        copy.wait_recv()
    send(stat.at[core], stat.at[core], mate).wait_recv()

    def before_fields():
        for copy in field_got:
            copy.wait_recv()

    def static_of(f, r):
        h, f = (0, f) if f < STAT else (1, f - STAT)
        return stat[h, pl.ds(f * rows + r, nd, stride=srows), :]

    def logk_of(r):
        value = field[0, pl.ds(r, nd, stride=rows), :]
        for g in range(1, pairs_n):
            value = value + field[g, pl.ds(r, nd, stride=rows), :]
        return value

    def fault_row(x, k):
        return stat[1, pl.ds(x * srows + 3 * rows + k, 1), :]

    pres_got = []

    def after_pressure():
        for t in near:
            pres_got.append(
                send(
                    pres_s.at[block(cell_of(t), rows)], pres_in.at[block(me, rows)], cell_peer(t)
                )
            )
        pres_in[block(me, rows), :] = pres_s[block(me, rows), :]

    chain_physics(
        nd, rows, logk_of, static_of, fault_row, parts, fault_s, coef, pres_s, before_fields,
        after_pressure, glogk_s,
    )

    gl_b[...] = glogk_s[...].astype(jnp.bfloat16)
    spot = block(group * nd + me, rows)
    gl_got = [
        send(gl_b.at[block(cell_of(t), rows)], gl_all.at[core, spot], wide_peer(t, dx))
        for t, dx in wide
    ]
    gl_all[core, spot, :] = gl_b[block(me, rows), :]
    for copy in gl_got:
        copy.wait_recv()
    mate_got = send(gl_all.at[core], gl_all.at[core], mate)
    for copy in pres_got:
        copy.wait_recv()
    pres_out[...] = pres_in[...]
    mate_got.wait_recv()
    held = chains // 2 * rows
    for c in range(2):
        gl_f[c * held : (c + 1) * held, :] = gl_all[c].astype(jnp.float32)
    glogk = jnp.concatenate(
        [gl_f[pl.ds(r, chains, stride=rows), :] for r in range(rows)], 1
    ).astype(jnp.bfloat16)

    width = modes_n // nd

    def piece(i):
        return jnp.dot(
            glogk, basis[:, block(i, width)], preferred_element_type=jnp.float32
        )

    g_got = []
    for k, t in enumerate(near):
        gsend[k] = piece(cell_of(t)).astype(jnp.bfloat16)
        g_got.append(send(gsend.at[k], gin.at[k], cell_peer(t)))
    grad = piece(me)
    for k, copy in enumerate(g_got):
        copy.wait_recv()
        grad = grad + gin[k].astype(jnp.float32)
    gfin[...] = grad.astype(jnp.bfloat16)
    g_got = [send(gfin, gall.at[me], cell_peer(t)) for t in near]
    gall[me] = gfin[...]
    for copy in g_got:
        copy.wait_recv()
    grad_out[...] = gall[...]
    for copy in sent:
        copy.wait_send()


def finish_kernel(nm, grad_ref, pres_ref, theta_ref, noise_ref, theta_out, grad_out, pres_out):
    pieces, chains, width = grad_ref.shape
    share = chains // nm
    order = [x * 2 + c for c in range(2) for x in range(nm // 2)]
    for p in range(pieces):
        cols = slice(p * width, (p + 1) * width)
        piece = grad_ref[p].astype(jnp.float32)
        g = jnp.concatenate(
            [piece[order.index(n) * share : (order.index(n) + 1) * share] for n in range(nm)], 0
        )
        t = theta_ref[:, cols]
        grad_out[:, cols] = g
        theta_out[:, cols] = (
            t - STEP_SIZE * (g + t) + math.sqrt(2.0 * STEP_SIZE) * noise_ref[:, cols]
        )
    count = pres_out.shape[0]
    rows = pres_out.shape[1] // LANES
    for r in range(rows):
        pres_out[:, r * LANES : (r + 1) * LANES] = pres_ref[pl.ds(r, count, stride=rows), :]


def fast_body(
    theta, basis, mean_logk, face_mult, storage, sources, obs_data, obs_weight,
    fault_pairs, fault_mult, noise,
):
    nd, nm = lax.axis_size("cells"), lax.axis_size("modes")
    cells, modes_n = basis.shape
    chains = theta.shape[1]
    rows = cells // LANES
    parts = fault_mult.shape[0] // LANES
    f32, bf16 = jnp.float32, jnp.bfloat16
    width = modes_n // nd
    pairs_n = nm // 2
    copies = 4 * (nd - 1) + 2 * (pairs_n * nd - 1) + 4
    vmem = pl.BlockSpec(memory_space=pltpu.VMEM)
    grad, pressure = pl.pallas_call(
        functools.partial(fused_kernel, nd, nm, rows, parts, ("cells", "modes")),
        out_shape=(
            jax.ShapeDtypeStruct((nd, chains, width), bf16),
            jax.ShapeDtypeStruct((nd * rows, LANES), f32),
        ),
        in_specs=[pl.BlockSpec(memory_space=pl.ANY)] * 10,
        out_specs=(vmem,) * 2,
        scratch_shapes=[
            pltpu.VMEM((cells, modes_n), bf16),
            pltpu.VMEM((chains, modes_n), f32),
            pltpu.VMEM((rows, LANES), f32),
            pltpu.VMEM((3, cells), f32),
            pltpu.VMEM((2, parts * LANES), jnp.int32),
            pltpu.VMEM((parts, LANES), f32),
            pltpu.VMEM((2, STAT * rows, LANES), f32),
            pltpu.VMEM((2, nd * STAT * rows, LANES), f32),
            pltpu.VMEM((2, chains * rows // 2, LANES), f32),
            pltpu.VMEM((2, chains // 2 * rows // 2, LANES), f32),
            pltpu.VMEM((pairs_n * nd, rows, LANES), f32),
            pltpu.VMEM((pairs_n, nd * rows, LANES), f32),
            pltpu.VMEM((3, nd * rows, LANES), f32),
            pltpu.VMEM((18, rows, nd, LANES), f32),
            pltpu.VMEM((nd * rows, LANES), f32),
            pltpu.VMEM((nd * rows, LANES), f32),
            pltpu.VMEM((nd * rows, LANES), f32),
            pltpu.VMEM((nd * rows, LANES), bf16),
            pltpu.VMEM((2, chains // 2 * rows, LANES), bf16),
            pltpu.VMEM((chains * rows, LANES), f32),
            pltpu.VMEM((nd - 1, chains, width), bf16),
            pltpu.VMEM((nd - 1, chains, width), bf16),
            pltpu.VMEM((chains, width), bf16),
            pltpu.VMEM((nd, chains, width), bf16),
            pltpu.SemaphoreType.DMA((9,)),
            pltpu.SemaphoreType.DMA((nd,)),
            pltpu.SemaphoreType.DMA((copies,)),
            pltpu.SemaphoreType.DMA((copies,)),
        ],
        compiler_params=pltpu.CompilerParams(collective_id=0, has_side_effects=True),
    )(
        theta.T, basis, mean_logk.reshape(-1, LANES), face_mult, storage.reshape(-1, LANES),
        sources.reshape(-1, LANES), obs_data.reshape(-1, LANES), obs_weight.reshape(-1, LANES),
        fault_pairs.T, fault_mult.reshape(-1, LANES),
    )
    theta_next, grad, pressure = pl.pallas_call(
        functools.partial(finish_kernel, nm),
        out_shape=(
            jax.ShapeDtypeStruct((chains, modes_n), f32),
            jax.ShapeDtypeStruct((chains, modes_n), f32),
            jax.ShapeDtypeStruct((chains // nm, cells), f32),
        ),
        in_specs=[vmem] * 4,
        out_specs=(vmem,) * 3,
    )(grad, pressure, theta.T, noise.T)
    return (theta_next.T, grad.T, pressure)


def choose_body(theta, basis, *rest):
    share = theta.shape[1] // lax.axis_size("modes")
    nx = lax.axis_size("cells")
    whole = basis.shape[0] == NY * NZ and rest[-2].shape[0] % LANES == 0 and 2 * NZ == LANES
    paired = lax.axis_size("modes") % 2 == 0 and 3 * rest[-2].shape[0] // LANES <= basis.shape[0] // LANES
    if paired and share == nx and nx == 8 and whole and basis.shape[1] % (nx * LANES) == 0:
        return fast_body(theta, basis, *rest)
    return body(theta, basis, *rest)


def solution(mesh):
    return jax.shard_map(
        choose_body,
        mesh=mesh,
        in_specs=(
            P("modes", None),
            P("cells", "modes"),
            P("cells"),
            P(None, "cells"),
            P("cells"),
            P("cells"),
            P("cells"),
            P("cells"),
            P("cells", None),
            P("cells"),
            P("modes", None),
        ),
        out_specs=(P("modes", None), P("modes", None), P("modes", "cells")),
        check_vma=False,
    )
```

```python
import functools
import math

import jax
import jax.numpy as jnp
from jax import lax
from jax.experimental import pallas as pl
from jax.experimental.pallas import tpu as pltpu
from jax.sharding import PartitionSpec as P

NY = 32
NZ = 64
SWEEPS = 6


LOW_EIG = 0.1
HIGH_EIG = 1.9
STEP_SIZE = 0.01


def extended(block, sides, width):
    for axis, dim in sides:
        count = lax.axis_size(axis)
        forward = [(i, i + 1) for i in range(count - 1)]
        backward = [(target, source) for source, target in forward]
        low = lax.ppermute(
            lax.slice_in_dim(block, block.shape[dim] - width, None, axis=dim), axis, forward
        )
        high = lax.ppermute(lax.slice_in_dim(block, 0, width, axis=dim), axis, backward)
        block = jnp.concatenate([low, block, high], axis=dim)
    return block


def harmonic(left, right):
    return 2.0 * left * right / (left + right)


def pad_axis(array, axis, before, after):
    widths = [(0, 0)] * array.ndim
    widths[axis] = (before, after)
    return jnp.pad(array, widths)


def transmit(perm_ext, mult_ext, mult_y, mult_z, near_cell, far_cell, fault_mult, depth_y, depth_z):
    chains_n = perm_ext.shape[0]
    layers = perm_ext.shape[1] - 2
    trans_x = harmonic(perm_ext[:, :-1], perm_ext[:, 1:]) * mult_ext[:, :-1]
    perm = perm_ext[:, 1:-1].reshape(chains_n, layers, depth_y, depth_z)
    trans_y = (
        harmonic(perm[:, :, :-1], perm[:, :, 1:])
        * mult_y.reshape(1, layers, depth_y, depth_z)[:, :, :-1]
    )
    trans_z = (
        harmonic(perm[..., :-1], perm[..., 1:])
        * mult_z.reshape(1, layers, depth_y, depth_z)[..., :-1]
    )
    flat = perm.reshape(chains_n, -1)
    live = fault_mult * (near_cell != far_cell).astype(jnp.float32)
    trans_n = harmonic(flat[:, near_cell], flat[:, far_cell]) * live[None]
    return (trans_x, trans_y, trans_z, trans_n)


def diagonal_of(trans, storage, near_cell, far_cell, depth_y, depth_z):
    trans_x, trans_y, trans_z, trans_n = trans
    chains_n = trans_x.shape[0]
    layers = trans_x.shape[1] - 1
    total = (trans_x[:, 1:] + trans_x[:, :-1]).reshape(chains_n, layers, depth_y, depth_z)
    total = total + pad_axis(trans_y, 2, 0, 1) + pad_axis(trans_y, 2, 1, 0)
    total = total + pad_axis(trans_z, 3, 0, 1) + pad_axis(trans_z, 3, 1, 0)
    total = total.reshape(chains_n, -1)
    total = total.at[:, near_cell].add(trans_n).at[:, far_cell].add(trans_n)
    return total + storage[None]


def operate(field_ext, trans, storage, near_cell, far_cell, depth_y, depth_z):
    trans_x, trans_y, trans_z, trans_n = trans
    chains_n = field_ext.shape[0]
    layers = field_ext.shape[1] - 2
    flux_x = trans_x * (field_ext[:, :-1] - field_ext[:, 1:])
    result = (flux_x[:, 1:] - flux_x[:, :-1]).reshape(chains_n, layers, depth_y, depth_z)
    field = field_ext[:, 1:-1].reshape(chains_n, layers, depth_y, depth_z)
    flux_y = trans_y * (field[:, :, :-1] - field[:, :, 1:])
    result = result + pad_axis(flux_y, 2, 0, 1) - pad_axis(flux_y, 2, 1, 0)
    flux_z = trans_z * (field[..., :-1] - field[..., 1:])
    result = result + pad_axis(flux_z, 3, 0, 1) - pad_axis(flux_z, 3, 1, 0)
    result = result.reshape(chains_n, -1)
    flat = field.reshape(chains_n, -1)
    flux_n = trans_n * (flat[:, near_cell] - flat[:, far_cell])
    result = result.at[:, near_cell].add(flux_n).at[:, far_cell].add(-flux_n)
    return result + storage[None] * flat


def solve(rhs, apply_fn, diag):
    center = 0.5 * (HIGH_EIG + LOW_EIG)
    half = 0.5 * (HIGH_EIG - LOW_EIG)
    sigma = center / half
    resid = rhs / diag
    direction = resid / center
    iterate = jnp.zeros_like(rhs)
    rho = jnp.asarray(1.0 / sigma, dtype=rhs.dtype)

    def sweep_step(sweep, carry):
        iterate, resid, direction, rho = carry
        iterate = iterate + direction
        resid = resid - apply_fn(direction) / diag
        rho_next = 1.0 / (2.0 * sigma - rho)
        direction = rho_next * rho * direction + 2.0 * rho_next / half * resid
        return (iterate, resid, direction, rho_next)

    iterate, resid, direction, rho = lax.fori_loop(
        0, SWEEPS, sweep_step, (iterate, resid, direction, rho)
    )
    return iterate + direction


def gradient_of(pres_ext, adj_ext, perm_ext, trans, near_cell, far_cell, depth_y, depth_z):
    trans_x, trans_y, trans_z, trans_n = trans
    chains_n = perm_ext.shape[0]
    layers = perm_ext.shape[1] - 2
    coef_x = (
        -(adj_ext[:, :-1] - adj_ext[:, 1:])
        * (pres_ext[:, :-1] - pres_ext[:, 1:])
        * trans_x
        / (perm_ext[:, :-1] + perm_ext[:, 1:])
    )
    result = coef_x[:, 1:] * perm_ext[:, 2:] + coef_x[:, :-1] * perm_ext[:, :-2]
    result = result.reshape(chains_n, layers, depth_y, depth_z)
    shape4 = (chains_n, layers, depth_y, depth_z)
    perm = perm_ext[:, 1:-1].reshape(shape4)
    pres = pres_ext[:, 1:-1].reshape(shape4)
    adj = adj_ext[:, 1:-1].reshape(shape4)
    coef_y = (
        -(adj[:, :, :-1] - adj[:, :, 1:])
        * (pres[:, :, :-1] - pres[:, :, 1:])
        * trans_y
        / (perm[:, :, :-1] + perm[:, :, 1:])
    )
    result = (
        result
        + pad_axis(coef_y * perm[:, :, 1:], 2, 0, 1)
        + pad_axis(coef_y * perm[:, :, :-1], 2, 1, 0)
    )
    coef_z = (
        -(adj[..., :-1] - adj[..., 1:])
        * (pres[..., :-1] - pres[..., 1:])
        * trans_z
        / (perm[..., :-1] + perm[..., 1:])
    )
    result = (
        result
        + pad_axis(coef_z * perm[..., 1:], 3, 0, 1)
        + pad_axis(coef_z * perm[..., :-1], 3, 1, 0)
    )
    result = result.reshape(chains_n, -1)
    perm_f = perm.reshape(chains_n, -1)
    pres_f = pres.reshape(chains_n, -1)
    adj_f = adj.reshape(chains_n, -1)
    perm_a = perm_f[:, near_cell]
    perm_b = perm_f[:, far_cell]
    coef_n = (
        -(adj_f[:, near_cell] - adj_f[:, far_cell])
        * (pres_f[:, near_cell] - pres_f[:, far_cell])
        * trans_n
        / (perm_a + perm_b)
    )
    return result.at[:, near_cell].add(coef_n * perm_b).at[:, far_cell].add(coef_n * perm_a)


def physics(logk, face_mult, storage, sources, obs_data, obs_weight, fault_pairs, fault_mult):
    chains_n, cells_n = logk.shape
    faces = NY * NZ
    layers = cells_n // faces
    near_cell = fault_pairs[:, 0]
    far_cell = fault_pairs[:, 1]
    perm = jnp.exp(logk).reshape(chains_n, layers, faces)
    stacked = jnp.concatenate([perm, face_mult[0].reshape(1, layers, faces)], 0)
    stacked_ext = extended(stacked, (("cells", 1),), 1)
    perm_ext = stacked_ext[:chains_n]
    mult_ext = stacked_ext[chains_n:]
    trans = transmit(
        perm_ext, mult_ext, face_mult[1], face_mult[2], near_cell, far_cell, fault_mult, NY, NZ
    )
    diag = diagonal_of(trans, storage, near_cell, far_cell, NY, NZ)

    def apply_fn(field):
        field_ext = extended(field.reshape(chains_n, layers, faces), (("cells", 1),), 1)
        return operate(field_ext, trans, storage, near_cell, far_cell, NY, NZ)

    rhs = jnp.broadcast_to(sources[None], (chains_n, cells_n))
    pressure = solve(rhs, apply_fn, diag)
    misfit = obs_weight[None] * (pressure - obs_data[None])
    adjoint = solve(misfit, apply_fn, diag)
    both = jnp.concatenate([pressure, adjoint], 0).reshape(2 * chains_n, layers, faces)
    both_ext = extended(both, (("cells", 1),), 1)
    glogk = gradient_of(
        both_ext[:chains_n], both_ext[chains_n:], perm_ext, trans, near_cell, far_cell, NY, NZ
    )
    return (pressure, glogk)


def body(
    theta,
    basis,
    mean_logk,
    face_mult,
    storage,
    sources,
    obs_data,
    obs_weight,
    fault_pairs,
    fault_mult,
    noise,
):
    chains = theta.shape[1]
    share = chains // lax.axis_size("modes")
    theta_b = theta.astype(jnp.bfloat16)
    local_field = lax.dot_general(
        theta_b, basis, (((0,), (1,)), ((), ())), preferred_element_type=jnp.float32
    )
    partial_field = lax.psum(local_field, "modes")
    logk = mean_logk[None] + partial_field
    pressure, glogk = physics(
        logk, face_mult, storage, sources, obs_data, obs_weight, fault_pairs, fault_mult
    )
    glogk_b = glogk.astype(jnp.bfloat16)
    grad_rows = jnp.dot(glogk_b, basis, preferred_element_type=jnp.float32)
    pressure_out = lax.dynamic_slice_in_dim(pressure, lax.axis_index("modes") * share, share, 0)
    mode_grad = lax.psum(grad_rows, "cells")
    grad = mode_grad.T
    theta_next = theta - STEP_SIZE * (grad + theta) + math.sqrt(2.0 * STEP_SIZE) * noise
    return (theta_next, grad, pressure_out)


LANES = 128
STAT = 4


def chebyshev(rhs, inv, sweep):
    center = 0.5 * (HIGH_EIG + LOW_EIG)
    half = 0.5 * (HIGH_EIG - LOW_EIG)
    sigma = center / half
    resid = [b * v for b, v in zip(rhs, inv)]
    direction = [v * (1.0 / center) for v in resid]
    iterate = None
    rho = 1.0 / sigma
    for _ in range(SWEEPS):
        iterate = direction if iterate is None else [a + b for a, b in zip(iterate, direction)]
        resid = [v - d + s for v, d, s in zip(resid, direction, sweep(direction))]
        rho_next = 1.0 / (2.0 * sigma - rho)
        direction = [
            (rho_next * rho) * d + (2.0 * rho_next / half) * v for d, v in zip(direction, resid)
        ]
        rho = rho_next
    return [a + b for a, b in zip(iterate, direction)]


def chain_physics(nx, rows, logk_of, static_of, fault_row, parts, fault_s, coef, pres_s, before_fields, after_pressure, glogk_s):
    hi_iota = lax.broadcasted_iota(jnp.int32, (rows, LANES), 0)
    lo_iota = lax.broadcasted_iota(jnp.int32, (LANES, LANES), 0)
    for x in range(nx):
        got = None
        for part in range(parts):
            near = fault_row(x, part).astype(jnp.int32)
            shift = fault_row(x, parts + part).astype(jnp.int32) - near - NZ
            lo = (lo_iota == (near & (LANES - 1))).astype(jnp.float32)
            hot = jnp.where(hi_iota == (near >> 7), fault_row(x, 2 * parts + part), 0.0)
            left = jnp.concatenate([jnp.where(shift == s, hot, 0.0) for s in (1, 2, 3)], 0)
            term = lax.dot_general(
                left, lo, (((1,), (1,)), ((), ())),
                precision=lax.Precision.HIGHEST, preferred_element_type=jnp.float32,
            )
            got = term if got is None else got + term
        for s in range(3):
            fault_s[s, pl.ds(x * rows, rows), :] = got[s * rows : (s + 1) * rows]

    before_fields()
    lane = lax.broadcasted_iota(jnp.int32, (nx, LANES), 1)
    xpos = lax.broadcasted_iota(jnp.int32, (nx, LANES), 0)
    low = lane < NZ
    zpos = jnp.where(low, lane, lane - NZ)

    def fwd_lane(v, s):
        return pltpu.roll(v, LANES - s, 1)

    def bwd_lane(v, s):
        return pltpu.roll(v, s, 1)

    fwd_low = [((lane + s) & (LANES - 1)) < NZ for s in range(4)]
    bwd_low = [((lane - s) & (LANES - 1)) < NZ for s in range(4)]

    def up_y(vs, s, hs=None):
        n = len(vs)
        hs = [pltpu.roll(v, NZ - s, 1) for v in vs] if hs is None else hs
        return [jnp.where(fwd_low[s], hs[r], hs[(r + 1) % n]) for r in range(n)]

    def down_y(vs, s, hs=None):
        n = len(vs)
        hs = [pltpu.roll(v, NZ + s, 1) for v in vs] if hs is None else hs
        return [jnp.where(bwd_low[s], hs[r - 1], hs[r]) for r in range(n)]

    def ahead(vs):
        return (
            [pltpu.roll(v, nx - 1, 0) for v in vs],
            up_y(vs, 0),
            [fwd_lane(v, 1) for v in vs],
            up_y(vs, 1),
            up_y(vs, 2),
            up_y(vs, 3),
        )

    def behind_one(kind, vs):
        if kind == 0:
            return [pltpu.roll(v, 1, 0) for v in vs]
        if kind == 2:
            return [bwd_lane(v, 1) for v in vs]
        return down_y(vs, max(kind - 2, 0))

    every = range(rows)
    perm = [jnp.exp(logk_of(r)) for r in every]
    perm_a = ahead(perm)
    zero = jnp.zeros((nx, LANES), jnp.float32)
    diag = [static_of(3, r) for r in every]
    for k in range(6):
        trans = []
        for r in every:
            if k < 3:
                m = static_of(k, r)
            else:
                m = fault_s[k - 3, pl.ds(r, nx, stride=rows), :]
            if k == 0:
                live = xpos < nx - 1
            elif k == 1:
                live = None if r < rows - 1 else low
            elif k == 2:
                live = zpos < NZ - 1
            else:
                live = m > 0.0
            a, b = perm[r], perm_a[k][r]
            total = a + b
            t = 2.0 * a * b / total * m
            if live is not None:
                t = jnp.where(live, t, zero)
            g = t / total
            coef[12 + k, r] = g
            trans.append(t)
        back = behind_one(k, trans)
        for r in every:
            coef[2 * k, r] = trans[r]
            coef[2 * k + 1, r] = back[r]
            diag[r] = diag[r] + trans[r] + back[r]
    inv = [1.0 / v for v in diag]
    for k in range(12):
        for r in every:
            coef[k, r] = coef[k, r] * inv[r]

    def sweep(d):
        hs = [pltpu.roll(v, NZ, 1) for v in d]
        ups = [up_y(d, 0, hs)] + [up_y(d, s) for s in (1, 2, 3)]
        dns = [down_y(d, 0, hs)] + [down_y(d, s) for s in (1, 2, 3)]
        out = []
        for r in every:
            v = d[r]
            acc = coef[0, r] * pltpu.roll(v, nx - 1, 0) + coef[1, r] * pltpu.roll(v, 1, 0)
            acc2 = coef[2, r] * ups[0][r] + coef[3, r] * dns[0][r]
            acc = acc + (coef[4, r] * fwd_lane(v, 1) + coef[5, r] * bwd_lane(v, 1))
            for s in (1, 2, 3):
                acc2 = acc2 + coef[4 + 2 * s, r] * ups[s][r]
                acc = acc + coef[5 + 2 * s, r] * dns[s][r]
            out.append(acc + acc2)
        return out

    pres = chebyshev([static_of(4, r) for r in every], inv, sweep)
    for r in every:
        pres_s[pl.ds(r, nx, stride=rows), :] = pres[r]
    after_pressure()
    misfit = [static_of(6, r) * (pres[r] - static_of(5, r)) for r in every]
    adj = chebyshev(misfit, inv, sweep)
    pres_a = ahead(pres)
    adj_a = ahead(adj)
    perm_a = ahead(perm)
    total = [zero for r in every]
    for k in range(6):
        q = [
            -(adj[r] - adj_a[k][r]) * (pres[r] - pres_a[k][r]) * coef[12 + k, r] for r in every
        ]
        back = behind_one(k, [q[r] * perm[r] for r in every])
        for r in every:
            total[r] = total[r] + q[r] * perm_a[k][r] + back[r]
    for r in every:
        glogk_s[pl.ds(r, nx, stride=rows), :] = total[r]


def fused_kernel(
    nd, nm, rows, parts, axes,
    theta_hbm, basis_hbm, mean_hbm, face_hbm, storage_hbm, sources_hbm, data_hbm, weight_hbm,
    pairs_hbm, mult_hbm,
    grad_out, pres_out,
    basis, theta_v, mean_v, face_v, pairs_v, mult_v, own_stat, stat, part, part_in, mine, field,
    fault_s, coef, pres_s, pres_in, glogk_s, gl_b, gl_all, gl_f, gsend, gin, gfin, gall,
    load_sem, copy_sem, send_sem, recv_sem,
):
    cells_ax, modes_ax = axes
    me, mo = lax.axis_index(cells_ax), lax.axis_index(modes_ax)
    chains, modes_n = theta_v.shape
    cells = rows * LANES
    blk = cells // nd
    pairs_n = nm // 2
    core, group = lax.rem(mo, 2), lax.div(mo, 2)
    high, low = lax.div(me, 2), lax.rem(me, 2)
    srows = STAT * rows
    small = [
        (theta_hbm, theta_v),
        (face_hbm, face_v),
        (storage_hbm, own_stat.at[0, pl.ds(3 * rows, rows)]),
        (sources_hbm, own_stat.at[1, pl.ds(0, rows)]),
        (data_hbm, own_stat.at[1, pl.ds(rows, rows)]),
        (weight_hbm, own_stat.at[1, pl.ds(2 * rows, rows)]),
        (pairs_hbm, pairs_v),
        (mult_hbm, mult_v),
        (mean_hbm, mean_v),
    ]
    small = [pltpu.make_async_copy(a, b, load_sem.at[i]) for i, (a, b) in enumerate(small)]
    loads = [
        pltpu.make_async_copy(
            basis_hbm.at[pl.ds(k * blk, blk)], basis.at[pl.ds(k * blk, blk)], copy_sem.at[k]
        )
        for k in range(nd)
    ]
    flight = nd // 2
    for load in small + loads[:flight]:
        load.start()

    def block(i, size):
        return pl.ds(pl.multiple_of(i * size, size), size)

    steps = sorted(
        ((dz, dy) for dz in range(nd // 2) for dy in range(2)),
        key=lambda t: -(min(t[0], nd // 2 - t[0]) + t[1]),
    )

    def cell_of(step):
        return lax.rem(high + step[0], nd // 2) * 2 + lax.rem(low + step[1], 2)

    near = [t for t in steps if t != (0, 0)]
    wide = sorted(
        ((t, dx) for t in steps for dx in range(pairs_n) if (t, dx) != ((0, 0), 0)),
        key=lambda w: -(min(w[0][0], nd // 2 - w[0][0]) + w[0][1] + (w[1] > 0)),
    )
    mate = {modes_ax: group * 2 + 1 - core}

    def group_of(dx):
        return lax.rem(group + dx, pairs_n)

    def wide_peer(t, dx):
        return {cells_ax: cell_of(t), modes_ax: group_of(dx) * 2 + core}

    barrier = pltpu.get_barrier_semaphore()
    for peer in [wide_peer(t, dx) for t, dx in wide] + [mate]:
        pl.semaphore_signal(barrier, inc=1, device_id=peer, device_id_type=pl.DeviceIdType.MESH)
    greeted = len(wide) + 1
    sent = []
    count = [0]

    def send(src, dst, peer):
        slot = count[0]
        count[0] += 1
        copy = pltpu.make_async_remote_copy(
            src_ref=src, dst_ref=dst, send_sem=send_sem.at[slot], recv_sem=recv_sem.at[slot],
            device_id=peer, device_id_type=pl.DeviceIdType.MESH,
        )
        copy.start()
        sent.append(copy)
        return copy

    def cell_peer(t):
        return {cells_ax: cell_of(t)}

    for load in small:
        load.wait()
    for f in range(3):
        own_stat[0, f * rows : (f + 1) * rows, :] = jnp.concatenate(
            [face_v[f : f + 1, r * LANES : (r + 1) * LANES] for r in range(rows)], 0
        )
    pairs = pairs_v[...].astype(jnp.float32)
    spare = rows - 3 * parts
    own_stat[1, 3 * rows :, :] = jnp.concatenate(
        [pairs[e : e + 1, p * LANES : (p + 1) * LANES] for e in range(2) for p in range(parts)]
        + [mult_v[...]]
        + ([jnp.zeros((spare, LANES), jnp.float32)] if spare else []),
        0,
    )
    stat[core, block(me, srows), :] = own_stat[core]
    share = chains // nm
    theta_b = jnp.concatenate(
        [
            theta_v[(2 * x + c) * share : (2 * x + c + 1) * share, :]
            for c in range(2)
            for x in range(pairs_n)
        ],
        0,
    ).astype(jnp.bfloat16)
    half = rows // 2
    stat_got, part_got = [], []
    for k in range(0, nd, 2):
        for load in (k, k + 1):
            loads[load].wait()
            if load + flight < nd:
                loads[load + flight].start()
        got = lax.dot_general(
            theta_b, basis[k * blk : (k + 2) * blk, :], (((1,), (1,)), ((), ())),
            preferred_element_type=jnp.float32,
        )
        for t in range(2 * blk // LANES):
            r = k * (blk // LANES) + t
            part[r // half, pl.ds(r % half, chains, stride=half), :] = (
                got[:, t * LANES : (t + 1) * LANES]
            )
        if k == 0:
            pl.semaphore_wait(barrier, greeted)
            stat_got = [
                send(own_stat.at[core], stat.at[core, block(me, srows)], cell_peer(t))
                for t in near
            ]
        if (k + 2) % (nd // 2) == 0:
            h = k // (nd // 2)
            part_got.append(
                send(part.at[h, block(1 - core, chains // 2 * half)], part_in.at[h], mate)
            )
    mean = 1.0 / pairs_n * mean_v[...]
    for h in range(2):
        total = part[h, block(core, chains // 2 * half), :].reshape(chains // 2, half, LANES)
        total = total + mean[h * half : (h + 1) * half][None]
        part_got[h].wait_recv()
        total = total + part_in[h].reshape(chains // 2, half, LANES)
        mine[:, h * half : (h + 1) * half, :] = total
    field_got = [
        send(
            mine.at[group_of(dx) * nd + cell_of(t)], field.at[group, block(me, rows)],
            wide_peer(t, dx),
        )
        for t, dx in wide
    ]
    field[group, block(me, rows), :] = mine[group * nd + me]
    for copy in stat_got:
        copy.wait_recv()
    send(stat.at[core], stat.at[core], mate).wait_recv()

    def before_fields():
        for copy in field_got:
            copy.wait_recv()

    def static_of(f, r):
        h, f = (0, f) if f < STAT else (1, f - STAT)
        return stat[h, pl.ds(f * rows + r, nd, stride=srows), :]

    def logk_of(r):
        value = field[0, pl.ds(r, nd, stride=rows), :]
        for g in range(1, pairs_n):
            value = value + field[g, pl.ds(r, nd, stride=rows), :]
        return value

    def fault_row(x, k):
        return stat[1, pl.ds(x * srows + 3 * rows + k, 1), :]

    pres_got = []

    def after_pressure():
        for t in near:
            pres_got.append(
                send(
                    pres_s.at[block(cell_of(t), rows)], pres_in.at[block(me, rows)], cell_peer(t)
                )
            )
        pres_in[block(me, rows), :] = pres_s[block(me, rows), :]

    chain_physics(
        nd, rows, logk_of, static_of, fault_row, parts, fault_s, coef, pres_s, before_fields,
        after_pressure, glogk_s,
    )

    gl_b[...] = glogk_s[...].astype(jnp.bfloat16)
    spot = block(group * nd + me, rows)
    gl_got = [
        send(gl_b.at[block(cell_of(t), rows)], gl_all.at[core, spot], wide_peer(t, dx))
        for t, dx in wide
    ]
    gl_all[core, spot, :] = gl_b[block(me, rows), :]
    for copy in gl_got:
        copy.wait_recv()
    mate_got = send(gl_all.at[core], gl_all.at[core], mate)
    for copy in pres_got:
        copy.wait_recv()
    pres_out[...] = pres_in[...]
    mate_got.wait_recv()
    held = chains // 2 * rows
    for c in range(2):
        gl_f[c * held : (c + 1) * held, :] = gl_all[c].astype(jnp.float32)
    glogk = jnp.concatenate(
        [gl_f[pl.ds(r, chains, stride=rows), :] for r in range(rows)], 1
    ).astype(jnp.bfloat16)

    width = modes_n // nd

    def piece(i):
        return jnp.dot(
            glogk, basis[:, block(i, width)], preferred_element_type=jnp.float32
        )

    g_got = []
    for first, last in ((0, nd // 2), (nd // 2, nd - 1)):
        for k in range(first, last):
            gsend[k] = piece(cell_of(near[k])).astype(jnp.bfloat16)
        for k in range(first, last):
            g_got.append(send(gsend.at[k], gin.at[k], cell_peer(near[k])))
    grad = piece(me)
    for k, copy in enumerate(g_got):
        copy.wait_recv()
        grad = grad + gin[k].astype(jnp.float32)
    gfin[...] = grad.astype(jnp.bfloat16)
    g_got = [send(gfin, gall.at[me], cell_peer(t)) for t in near]
    gall[me] = gfin[...]
    for copy in g_got:
        copy.wait_recv()
    grad_out[...] = gall[...]
    for copy in sent:
        copy.wait_send()


def finish_kernel(nm, grad_ref, pres_ref, theta_ref, noise_ref, theta_out, grad_out, pres_out):
    pieces, chains, width = grad_ref.shape
    share = chains // nm
    order = [x * 2 + c for c in range(2) for x in range(nm // 2)]
    for p in range(pieces):
        cols = slice(p * width, (p + 1) * width)
        piece = grad_ref[p].astype(jnp.float32)
        g = jnp.concatenate(
            [piece[order.index(n) * share : (order.index(n) + 1) * share] for n in range(nm)], 0
        )
        t = theta_ref[:, cols]
        grad_out[:, cols] = g
        theta_out[:, cols] = (
            t - STEP_SIZE * (g + t) + math.sqrt(2.0 * STEP_SIZE) * noise_ref[:, cols]
        )
    count = pres_out.shape[0]
    rows = pres_out.shape[1] // LANES
    for r in range(rows):
        pres_out[:, r * LANES : (r + 1) * LANES] = pres_ref[pl.ds(r, count, stride=rows), :]


def fast_body(
    theta, basis, mean_logk, face_mult, storage, sources, obs_data, obs_weight,
    fault_pairs, fault_mult, noise,
):
    nd, nm = lax.axis_size("cells"), lax.axis_size("modes")
    cells, modes_n = basis.shape
    chains = theta.shape[1]
    rows = cells // LANES
    parts = fault_mult.shape[0] // LANES
    f32, bf16 = jnp.float32, jnp.bfloat16
    width = modes_n // nd
    pairs_n = nm // 2
    copies = 4 * (nd - 1) + 2 * (pairs_n * nd - 1) + 4
    vmem = pl.BlockSpec(memory_space=pltpu.VMEM)
    grad, pressure = pl.pallas_call(
        functools.partial(fused_kernel, nd, nm, rows, parts, ("cells", "modes")),
        out_shape=(
            jax.ShapeDtypeStruct((nd, chains, width), bf16),
            jax.ShapeDtypeStruct((nd * rows, LANES), f32),
        ),
        in_specs=[pl.BlockSpec(memory_space=pl.ANY)] * 10,
        out_specs=(vmem,) * 2,
        scratch_shapes=[
            pltpu.VMEM((cells, modes_n), bf16),
            pltpu.VMEM((chains, modes_n), f32),
            pltpu.VMEM((rows, LANES), f32),
            pltpu.VMEM((3, cells), f32),
            pltpu.VMEM((2, parts * LANES), jnp.int32),
            pltpu.VMEM((parts, LANES), f32),
            pltpu.VMEM((2, STAT * rows, LANES), f32),
            pltpu.VMEM((2, nd * STAT * rows, LANES), f32),
            pltpu.VMEM((2, chains * rows // 2, LANES), f32),
            pltpu.VMEM((2, chains // 2 * rows // 2, LANES), f32),
            pltpu.VMEM((pairs_n * nd, rows, LANES), f32),
            pltpu.VMEM((pairs_n, nd * rows, LANES), f32),
            pltpu.VMEM((3, nd * rows, LANES), f32),
            pltpu.VMEM((18, rows, nd, LANES), f32),
            pltpu.VMEM((nd * rows, LANES), f32),
            pltpu.VMEM((nd * rows, LANES), f32),
            pltpu.VMEM((nd * rows, LANES), f32),
            pltpu.VMEM((nd * rows, LANES), bf16),
            pltpu.VMEM((2, chains // 2 * rows, LANES), bf16),
            pltpu.VMEM((chains * rows, LANES), f32),
            pltpu.VMEM((nd - 1, chains, width), bf16),
            pltpu.VMEM((nd - 1, chains, width), bf16),
            pltpu.VMEM((chains, width), bf16),
            pltpu.VMEM((nd, chains, width), bf16),
            pltpu.SemaphoreType.DMA((9,)),
            pltpu.SemaphoreType.DMA((nd,)),
            pltpu.SemaphoreType.DMA((copies,)),
            pltpu.SemaphoreType.DMA((copies,)),
        ],
        compiler_params=pltpu.CompilerParams(collective_id=0, has_side_effects=True),
    )(
        theta.T, basis, mean_logk.reshape(-1, LANES), face_mult, storage.reshape(-1, LANES),
        sources.reshape(-1, LANES), obs_data.reshape(-1, LANES), obs_weight.reshape(-1, LANES),
        fault_pairs.T, fault_mult.reshape(-1, LANES),
    )
    theta_next, grad, pressure = pl.pallas_call(
        functools.partial(finish_kernel, nm),
        out_shape=(
            jax.ShapeDtypeStruct((chains, modes_n), f32),
            jax.ShapeDtypeStruct((chains, modes_n), f32),
            jax.ShapeDtypeStruct((chains // nm, cells), f32),
        ),
        in_specs=[vmem] * 4,
        out_specs=(vmem,) * 3,
    )(grad, pressure, theta.T, noise.T)
    return (theta_next.T, grad.T, pressure)


def choose_body(theta, basis, *rest):
    share = theta.shape[1] // lax.axis_size("modes")
    nx = lax.axis_size("cells")
    whole = basis.shape[0] == NY * NZ and rest[-2].shape[0] % LANES == 0 and 2 * NZ == LANES
    paired = lax.axis_size("modes") % 2 == 0 and 3 * rest[-2].shape[0] // LANES <= basis.shape[0] // LANES
    if paired and share == nx and nx == 8 and whole and basis.shape[1] % (nx * LANES) == 0:
        return fast_body(theta, basis, *rest)
    return body(theta, basis, *rest)


def solution(mesh):
    return jax.shard_map(
        choose_body,
        mesh=mesh,
        in_specs=(
            P("modes", None),
            P("cells", "modes"),
            P("cells"),
            P(None, "cells"),
            P("cells"),
            P("cells"),
            P("cells"),
            P("cells"),
            P("cells", None),
            P("cells"),
            P("modes", None),
        ),
        out_specs=(P("modes", None), P("modes", None), P("modes", "cells")),
        check_vma=False,
    )
```

```python
import functools
import math

import jax
import jax.numpy as jnp
from jax import lax
from jax.experimental import pallas as pl
from jax.experimental.pallas import tpu as pltpu
from jax.sharding import PartitionSpec as P

NY = 32
NZ = 64
SWEEPS = 6


LOW_EIG = 0.1
HIGH_EIG = 1.9
STEP_SIZE = 0.01


def extended(block, sides, width):
    for axis, dim in sides:
        count = lax.axis_size(axis)
        forward = [(i, i + 1) for i in range(count - 1)]
        backward = [(target, source) for source, target in forward]
        low = lax.ppermute(
            lax.slice_in_dim(block, block.shape[dim] - width, None, axis=dim), axis, forward
        )
        high = lax.ppermute(lax.slice_in_dim(block, 0, width, axis=dim), axis, backward)
        block = jnp.concatenate([low, block, high], axis=dim)
    return block


def harmonic(left, right):
    return 2.0 * left * right / (left + right)


def pad_axis(array, axis, before, after):
    widths = [(0, 0)] * array.ndim
    widths[axis] = (before, after)
    return jnp.pad(array, widths)


def transmit(perm_ext, mult_ext, mult_y, mult_z, near_cell, far_cell, fault_mult, depth_y, depth_z):
    chains_n = perm_ext.shape[0]
    layers = perm_ext.shape[1] - 2
    trans_x = harmonic(perm_ext[:, :-1], perm_ext[:, 1:]) * mult_ext[:, :-1]
    perm = perm_ext[:, 1:-1].reshape(chains_n, layers, depth_y, depth_z)
    trans_y = (
        harmonic(perm[:, :, :-1], perm[:, :, 1:])
        * mult_y.reshape(1, layers, depth_y, depth_z)[:, :, :-1]
    )
    trans_z = (
        harmonic(perm[..., :-1], perm[..., 1:])
        * mult_z.reshape(1, layers, depth_y, depth_z)[..., :-1]
    )
    flat = perm.reshape(chains_n, -1)
    live = fault_mult * (near_cell != far_cell).astype(jnp.float32)
    trans_n = harmonic(flat[:, near_cell], flat[:, far_cell]) * live[None]
    return (trans_x, trans_y, trans_z, trans_n)


def diagonal_of(trans, storage, near_cell, far_cell, depth_y, depth_z):
    trans_x, trans_y, trans_z, trans_n = trans
    chains_n = trans_x.shape[0]
    layers = trans_x.shape[1] - 1
    total = (trans_x[:, 1:] + trans_x[:, :-1]).reshape(chains_n, layers, depth_y, depth_z)
    total = total + pad_axis(trans_y, 2, 0, 1) + pad_axis(trans_y, 2, 1, 0)
    total = total + pad_axis(trans_z, 3, 0, 1) + pad_axis(trans_z, 3, 1, 0)
    total = total.reshape(chains_n, -1)
    total = total.at[:, near_cell].add(trans_n).at[:, far_cell].add(trans_n)
    return total + storage[None]


def operate(field_ext, trans, storage, near_cell, far_cell, depth_y, depth_z):
    trans_x, trans_y, trans_z, trans_n = trans
    chains_n = field_ext.shape[0]
    layers = field_ext.shape[1] - 2
    flux_x = trans_x * (field_ext[:, :-1] - field_ext[:, 1:])
    result = (flux_x[:, 1:] - flux_x[:, :-1]).reshape(chains_n, layers, depth_y, depth_z)
    field = field_ext[:, 1:-1].reshape(chains_n, layers, depth_y, depth_z)
    flux_y = trans_y * (field[:, :, :-1] - field[:, :, 1:])
    result = result + pad_axis(flux_y, 2, 0, 1) - pad_axis(flux_y, 2, 1, 0)
    flux_z = trans_z * (field[..., :-1] - field[..., 1:])
    result = result + pad_axis(flux_z, 3, 0, 1) - pad_axis(flux_z, 3, 1, 0)
    result = result.reshape(chains_n, -1)
    flat = field.reshape(chains_n, -1)
    flux_n = trans_n * (flat[:, near_cell] - flat[:, far_cell])
    result = result.at[:, near_cell].add(flux_n).at[:, far_cell].add(-flux_n)
    return result + storage[None] * flat


def solve(rhs, apply_fn, diag):
    center = 0.5 * (HIGH_EIG + LOW_EIG)
    half = 0.5 * (HIGH_EIG - LOW_EIG)
    sigma = center / half
    resid = rhs / diag
    direction = resid / center
    iterate = jnp.zeros_like(rhs)
    rho = jnp.asarray(1.0 / sigma, dtype=rhs.dtype)

    def sweep_step(sweep, carry):
        iterate, resid, direction, rho = carry
        iterate = iterate + direction
        resid = resid - apply_fn(direction) / diag
        rho_next = 1.0 / (2.0 * sigma - rho)
        direction = rho_next * rho * direction + 2.0 * rho_next / half * resid
        return (iterate, resid, direction, rho_next)

    iterate, resid, direction, rho = lax.fori_loop(
        0, SWEEPS, sweep_step, (iterate, resid, direction, rho)
    )
    return iterate + direction


def gradient_of(pres_ext, adj_ext, perm_ext, trans, near_cell, far_cell, depth_y, depth_z):
    trans_x, trans_y, trans_z, trans_n = trans
    chains_n = perm_ext.shape[0]
    layers = perm_ext.shape[1] - 2
    coef_x = (
        -(adj_ext[:, :-1] - adj_ext[:, 1:])
        * (pres_ext[:, :-1] - pres_ext[:, 1:])
        * trans_x
        / (perm_ext[:, :-1] + perm_ext[:, 1:])
    )
    result = coef_x[:, 1:] * perm_ext[:, 2:] + coef_x[:, :-1] * perm_ext[:, :-2]
    result = result.reshape(chains_n, layers, depth_y, depth_z)
    shape4 = (chains_n, layers, depth_y, depth_z)
    perm = perm_ext[:, 1:-1].reshape(shape4)
    pres = pres_ext[:, 1:-1].reshape(shape4)
    adj = adj_ext[:, 1:-1].reshape(shape4)
    coef_y = (
        -(adj[:, :, :-1] - adj[:, :, 1:])
        * (pres[:, :, :-1] - pres[:, :, 1:])
        * trans_y
        / (perm[:, :, :-1] + perm[:, :, 1:])
    )
    result = (
        result
        + pad_axis(coef_y * perm[:, :, 1:], 2, 0, 1)
        + pad_axis(coef_y * perm[:, :, :-1], 2, 1, 0)
    )
    coef_z = (
        -(adj[..., :-1] - adj[..., 1:])
        * (pres[..., :-1] - pres[..., 1:])
        * trans_z
        / (perm[..., :-1] + perm[..., 1:])
    )
    result = (
        result
        + pad_axis(coef_z * perm[..., 1:], 3, 0, 1)
        + pad_axis(coef_z * perm[..., :-1], 3, 1, 0)
    )
    result = result.reshape(chains_n, -1)
    perm_f = perm.reshape(chains_n, -1)
    pres_f = pres.reshape(chains_n, -1)
    adj_f = adj.reshape(chains_n, -1)
    perm_a = perm_f[:, near_cell]
    perm_b = perm_f[:, far_cell]
    coef_n = (
        -(adj_f[:, near_cell] - adj_f[:, far_cell])
        * (pres_f[:, near_cell] - pres_f[:, far_cell])
        * trans_n
        / (perm_a + perm_b)
    )
    return result.at[:, near_cell].add(coef_n * perm_b).at[:, far_cell].add(coef_n * perm_a)


def physics(logk, face_mult, storage, sources, obs_data, obs_weight, fault_pairs, fault_mult):
    chains_n, cells_n = logk.shape
    faces = NY * NZ
    layers = cells_n // faces
    near_cell = fault_pairs[:, 0]
    far_cell = fault_pairs[:, 1]
    perm = jnp.exp(logk).reshape(chains_n, layers, faces)
    stacked = jnp.concatenate([perm, face_mult[0].reshape(1, layers, faces)], 0)
    stacked_ext = extended(stacked, (("cells", 1),), 1)
    perm_ext = stacked_ext[:chains_n]
    mult_ext = stacked_ext[chains_n:]
    trans = transmit(
        perm_ext, mult_ext, face_mult[1], face_mult[2], near_cell, far_cell, fault_mult, NY, NZ
    )
    diag = diagonal_of(trans, storage, near_cell, far_cell, NY, NZ)

    def apply_fn(field):
        field_ext = extended(field.reshape(chains_n, layers, faces), (("cells", 1),), 1)
        return operate(field_ext, trans, storage, near_cell, far_cell, NY, NZ)

    rhs = jnp.broadcast_to(sources[None], (chains_n, cells_n))
    pressure = solve(rhs, apply_fn, diag)
    misfit = obs_weight[None] * (pressure - obs_data[None])
    adjoint = solve(misfit, apply_fn, diag)
    both = jnp.concatenate([pressure, adjoint], 0).reshape(2 * chains_n, layers, faces)
    both_ext = extended(both, (("cells", 1),), 1)
    glogk = gradient_of(
        both_ext[:chains_n], both_ext[chains_n:], perm_ext, trans, near_cell, far_cell, NY, NZ
    )
    return (pressure, glogk)


def body(
    theta,
    basis,
    mean_logk,
    face_mult,
    storage,
    sources,
    obs_data,
    obs_weight,
    fault_pairs,
    fault_mult,
    noise,
):
    chains = theta.shape[1]
    share = chains // lax.axis_size("modes")
    theta_b = theta.astype(jnp.bfloat16)
    local_field = lax.dot_general(
        theta_b, basis, (((0,), (1,)), ((), ())), preferred_element_type=jnp.float32
    )
    partial_field = lax.psum(local_field, "modes")
    logk = mean_logk[None] + partial_field
    pressure, glogk = physics(
        logk, face_mult, storage, sources, obs_data, obs_weight, fault_pairs, fault_mult
    )
    glogk_b = glogk.astype(jnp.bfloat16)
    grad_rows = jnp.dot(glogk_b, basis, preferred_element_type=jnp.float32)
    pressure_out = lax.dynamic_slice_in_dim(pressure, lax.axis_index("modes") * share, share, 0)
    mode_grad = lax.psum(grad_rows, "cells")
    grad = mode_grad.T
    theta_next = theta - STEP_SIZE * (grad + theta) + math.sqrt(2.0 * STEP_SIZE) * noise
    return (theta_next, grad, pressure_out)


LANES = 128
STAT = 3


def chebyshev(rhs, inv, sweep):
    center = 0.5 * (HIGH_EIG + LOW_EIG)
    half = 0.5 * (HIGH_EIG - LOW_EIG)
    sigma = center / half
    resid = [b * v for b, v in zip(rhs, inv)]
    direction = [v * (1.0 / center) for v in resid]
    iterate = None
    rho = 1.0 / sigma
    for _ in range(SWEEPS):
        iterate = direction if iterate is None else [a + b for a, b in zip(iterate, direction)]
        resid = [v - d + s for v, d, s in zip(resid, direction, sweep(direction))]
        rho_next = 1.0 / (2.0 * sigma - rho)
        direction = [
            (rho_next * rho) * d + (2.0 * rho_next / half) * v for d, v in zip(direction, resid)
        ]
        rho = rho_next
    return [a + b for a, b in zip(iterate, direction)]


def chain_physics(nx, rows, logk_of, static_of, fault_row, parts, fault_s, coef, pres_s, before_fields, before_solve, after_pressure, glogk_s):
    hi_iota = lax.broadcasted_iota(jnp.int32, (rows, LANES), 0)
    lo_iota = lax.broadcasted_iota(jnp.int32, (LANES, LANES), 0)
    for x in range(nx):
        lefts, los = [], []
        for part in range(parts):
            near = fault_row(x, part).astype(jnp.int32)
            shift = fault_row(x, parts + part).astype(jnp.int32) - near - NZ
            los.append((lo_iota == (near & (LANES - 1))).astype(jnp.bfloat16))
            hot = jnp.where(hi_iota == (near >> 7), fault_row(x, 2 * parts + part), 0.0)
            rest = [jnp.where(shift == s, hot, 0.0) for s in (1, 2, 3)]
            pieces = []
            for _ in range(3):
                top = [v.astype(jnp.bfloat16) for v in rest]
                rest = [v - t.astype(jnp.float32) for v, t in zip(rest, top)]
                pieces += top
            lefts.append(jnp.concatenate(pieces, 0))
        got = lax.dot_general(
            jnp.concatenate(lefts, 1), jnp.concatenate(los, 1), (((1,), (1,)), ((), ())),
            preferred_element_type=jnp.float32,
        )
        got = (got[: 3 * rows] + got[3 * rows : 6 * rows]) + got[6 * rows :]
        for s in range(3):
            fault_s[s, pl.ds(x * rows, rows), :] = got[s * rows : (s + 1) * rows]

    before_fields()
    lane = lax.broadcasted_iota(jnp.int32, (nx, LANES), 1)
    xpos = lax.broadcasted_iota(jnp.int32, (nx, LANES), 0)
    low = lane < NZ
    zpos = jnp.where(low, lane, lane - NZ)

    def fwd_lane(v, s):
        return pltpu.roll(v, LANES - s, 1)

    def bwd_lane(v, s):
        return pltpu.roll(v, s, 1)

    fwd_low = [((lane + s) & (LANES - 1)) < NZ for s in range(4)]
    bwd_low = [((lane - s) & (LANES - 1)) < NZ for s in range(4)]

    def up_y(vs, s, hs=None):
        n = len(vs)
        hs = [pltpu.roll(v, NZ - s, 1) for v in vs] if hs is None else hs
        return [jnp.where(fwd_low[s], hs[r], hs[(r + 1) % n]) for r in range(n)]

    def down_y(vs, s, hs=None):
        n = len(vs)
        hs = [pltpu.roll(v, NZ + s, 1) for v in vs] if hs is None else hs
        return [jnp.where(bwd_low[s], hs[r - 1], hs[r]) for r in range(n)]

    def ahead(vs):
        return (
            [pltpu.roll(v, nx - 1, 0) for v in vs],
            up_y(vs, 0),
            [fwd_lane(v, 1) for v in vs],
            up_y(vs, 1),
            up_y(vs, 2),
            up_y(vs, 3),
        )

    def behind_one(kind, vs):
        if kind == 0:
            return [pltpu.roll(v, 1, 0) for v in vs]
        if kind == 2:
            return [bwd_lane(v, 1) for v in vs]
        return down_y(vs, max(kind - 2, 0))

    every = range(rows)
    perm = [jnp.exp(logk_of(r)) for r in every]
    perm_a = ahead(perm)
    zero = jnp.zeros((nx, LANES), jnp.float32)
    diag = [static_of(3, r) for r in every]
    for k in range(6):
        trans = []
        for r in every:
            if k < 3:
                m = static_of(k, r)
            else:
                m = fault_s[k - 3, pl.ds(r, nx, stride=rows), :]
            if k == 0:
                live = xpos < nx - 1
            elif k == 1:
                live = None if r < rows - 1 else low
            elif k == 2:
                live = zpos < NZ - 1
            else:
                live = m > 0.0
            a, b = perm[r], perm_a[k][r]
            total = a + b
            t = 2.0 * a * b / total * m
            if live is not None:
                t = jnp.where(live, t, zero)
            g = t / total
            coef[12 + k, r] = g
            trans.append(t)
        back = behind_one(k, trans)
        for r in every:
            coef[2 * k, r] = trans[r]
            coef[2 * k + 1, r] = back[r]
            diag[r] = diag[r] + trans[r] + back[r]
    inv = [1.0 / v for v in diag]
    for k in range(12):
        for r in every:
            coef[k, r] = coef[k, r] * inv[r]

    def sweep(d):
        hs = [pltpu.roll(v, NZ, 1) for v in d]
        ups = [up_y(d, 0, hs)] + [up_y(d, s) for s in (1, 2, 3)]
        dns = [down_y(d, 0, hs)] + [down_y(d, s) for s in (1, 2, 3)]
        out = []
        for r in every:
            v = d[r]
            acc = coef[0, r] * pltpu.roll(v, nx - 1, 0) + coef[1, r] * pltpu.roll(v, 1, 0)
            acc2 = coef[2, r] * ups[0][r] + coef[3, r] * dns[0][r]
            acc = acc + (coef[4, r] * fwd_lane(v, 1) + coef[5, r] * bwd_lane(v, 1))
            for s in (1, 2, 3):
                acc2 = acc2 + coef[4 + 2 * s, r] * ups[s][r]
                acc = acc + coef[5 + 2 * s, r] * dns[s][r]
            out.append(acc + acc2)
        return out

    before_solve()
    pres = chebyshev([static_of(4, r) for r in every], inv, sweep)
    for r in every:
        pres_s[pl.ds(r, nx, stride=rows), :] = pres[r]
    after_pressure()
    misfit = [static_of(6, r) * (pres[r] - static_of(5, r)) for r in every]
    adj = chebyshev(misfit, inv, sweep)
    pres_a = ahead(pres)
    adj_a = ahead(adj)
    perm_a = ahead(perm)
    total = [zero for r in every]
    for k in range(6):
        q = [
            -(adj[r] - adj_a[k][r]) * (pres[r] - pres_a[k][r]) * coef[12 + k, r] for r in every
        ]
        back = behind_one(k, [q[r] * perm[r] for r in every])
        for r in every:
            total[r] = total[r] + q[r] * perm_a[k][r] + back[r]
    for r in every:
        glogk_s[pl.ds(r, nx, stride=rows), :] = total[r]


def fused_kernel(
    nd, nm, rows, parts, axes,
    theta_hbm, basis_hbm, mean_hbm, face_hbm, storage_hbm, sources_hbm, data_hbm, weight_hbm,
    pairs_hbm, mult_hbm,
    grad_out, pres_out,
    basis, theta_v, mean_v, face_v, pairs_v, mult_v, own_stat, own_late, stat, late, part, part_in, mine, field,
    fault_s, coef, pres_s, pres_in, glogk_s, gl_b, gl_all, gl_f, gsend, gin, gfin, gall,
    load_sem, copy_sem, send_sem, recv_sem,
):
    cells_ax, modes_ax = axes
    me, mo = lax.axis_index(cells_ax), lax.axis_index(modes_ax)
    chains, modes_n = theta_v.shape
    cells = rows * LANES
    blk = cells // nd
    pairs_n = nm // 2
    core, group = lax.rem(mo, 2), lax.div(mo, 2)
    high, low = lax.div(me, 2), lax.rem(me, 2)
    srows = STAT * rows
    small = [
        (theta_hbm, theta_v),
        (face_hbm, face_v),
        (storage_hbm, own_stat.at[1, pl.ds(0, rows)]),
        (sources_hbm, own_stat.at[1, pl.ds(rows, rows)]),
        (data_hbm, own_late.at[0]),
        (weight_hbm, own_late.at[1]),
        (pairs_hbm, pairs_v),
        (mult_hbm, mult_v),
        (mean_hbm, mean_v),
    ]
    small = [pltpu.make_async_copy(a, b, load_sem.at[i]) for i, (a, b) in enumerate(small)]
    loads = [
        pltpu.make_async_copy(
            basis_hbm.at[pl.ds(k * blk, blk)], basis.at[pl.ds(k * blk, blk)], copy_sem.at[k]
        )
        for k in range(nd)
    ]
    flight = nd // 2
    for load in small + loads[:flight]:
        load.start()

    def block(i, size):
        return pl.ds(pl.multiple_of(i * size, size), size)

    steps = sorted(
        ((dz, dy) for dz in range(nd // 2) for dy in range(2)),
        key=lambda t: -(min(t[0], nd // 2 - t[0]) + t[1]),
    )

    def cell_of(step):
        return lax.rem(high + step[0], nd // 2) * 2 + lax.rem(low + step[1], 2)

    near = [t for t in steps if t != (0, 0)]
    wide = sorted(
        ((t, dx) for t in steps for dx in range(pairs_n) if (t, dx) != ((0, 0), 0)),
        key=lambda w: -(min(w[0][0], nd // 2 - w[0][0]) + w[0][1] + (w[1] > 0)),
    )
    mate = {modes_ax: group * 2 + 1 - core}

    def group_of(dx):
        return lax.rem(group + dx, pairs_n)

    def wide_peer(t, dx):
        return {cells_ax: cell_of(t), modes_ax: group_of(dx) * 2 + core}

    barrier = pltpu.get_barrier_semaphore()
    for peer in [wide_peer(t, dx) for t, dx in wide] + [mate]:
        pl.semaphore_signal(barrier, inc=1, device_id=peer, device_id_type=pl.DeviceIdType.MESH)
    greeted = len(wide) + 1
    sent = []
    count = [0]

    def send(src, dst, peer):
        slot = count[0]
        count[0] += 1
        copy = pltpu.make_async_remote_copy(
            src_ref=src, dst_ref=dst, send_sem=send_sem.at[slot], recv_sem=recv_sem.at[slot],
            device_id=peer, device_id_type=pl.DeviceIdType.MESH,
        )
        copy.start()
        sent.append(copy)
        return copy

    def cell_peer(t):
        return {cells_ax: cell_of(t)}

    for load in small:
        load.wait()
    for f in range(3):
        own_stat[0, f * rows : (f + 1) * rows, :] = jnp.concatenate(
            [face_v[f : f + 1, r * LANES : (r + 1) * LANES] for r in range(rows)], 0
        )
    pairs = pairs_v[...].astype(jnp.float32)
    spare = rows - 3 * parts
    own_stat[1, 2 * rows :, :] = jnp.concatenate(
        [pairs[e : e + 1, p * LANES : (p + 1) * LANES] for e in range(2) for p in range(parts)]
        + [mult_v[...]]
        + ([jnp.zeros((spare, LANES), jnp.float32)] if spare else []),
        0,
    )
    stat[core, block(me, srows), :] = own_stat[core]
    late[core, block(me, rows), :] = own_late[core]
    share = chains // nm
    theta_b = jnp.concatenate(
        [
            theta_v[(2 * x + c) * share : (2 * x + c + 1) * share, :]
            for c in range(2)
            for x in range(pairs_n)
        ],
        0,
    ).astype(jnp.bfloat16)
    half = rows // 2
    stat_got, part_got = [], []
    for k in range(0, nd, 2):
        for load in (k, k + 1):
            loads[load].wait()
            if load + flight < nd:
                loads[load + flight].start()
        got = lax.dot_general(
            theta_b, basis[k * blk : (k + 2) * blk, :], (((1,), (1,)), ((), ())),
            preferred_element_type=jnp.float32,
        )
        for t in range(2 * blk // LANES):
            r = k * (blk // LANES) + t
            part[r // half, pl.ds(r % half, chains, stride=half), :] = (
                got[:, t * LANES : (t + 1) * LANES]
            )
        if k == 0:
            pl.semaphore_wait(barrier, greeted)
            stat_got = [
                send(own_stat.at[core], stat.at[core, block(me, srows)], cell_peer(t))
                for t in near
            ]
        if (k + 2) % (nd // 2) == 0:
            h = k // (nd // 2)
            part_got.append(
                send(part.at[h, block(1 - core, chains // 2 * half)], part_in.at[h], mate)
            )
    mean = 1.0 / pairs_n * mean_v[...]
    for h in range(2):
        total = part[h, block(core, chains // 2 * half), :].reshape(chains // 2, half, LANES)
        total = total + mean[h * half : (h + 1) * half][None]
        part_got[h].wait_recv()
        total = total + part_in[h].reshape(chains // 2, half, LANES)
        mine[:, h * half : (h + 1) * half, :] = total
    field_got = [
        send(
            mine.at[group_of(dx) * nd + cell_of(t)], field.at[group, block(me, rows)],
            wide_peer(t, dx),
        )
        for t, dx in wide
    ]
    field[group, block(me, rows), :] = mine[group * nd + me]
    late_got = [
        send(own_late.at[core], late.at[core, block(me, rows)], cell_peer(t)) for t in near
    ]
    for copy in stat_got:
        copy.wait_recv()
    send(stat.at[core], stat.at[core], mate).wait_recv()

    def before_fields():
        for copy in field_got:
            copy.wait_recv()

    def static_of(f, r):
        if f > STAT + 1:
            return late[f - STAT - 2, pl.ds(r, nd, stride=rows), :]
        h, f = (0, f) if f < STAT else (1, f - STAT)
        return stat[h, pl.ds(f * rows + r, nd, stride=srows), :]

    def logk_of(r):
        value = field[0, pl.ds(r, nd, stride=rows), :]
        for g in range(1, pairs_n):
            value = value + field[g, pl.ds(r, nd, stride=rows), :]
        return value

    def fault_row(x, k):
        return stat[1, pl.ds(x * srows + 2 * rows + k, 1), :]

    pres_got, swapped = [], []

    def before_solve():
        for copy in late_got:
            copy.wait_recv()
        swapped.append(send(late.at[core], late.at[core], mate))

    def after_pressure():
        for t in near:
            pres_got.append(
                send(
                    pres_s.at[block(cell_of(t), rows)], pres_in.at[block(me, rows)], cell_peer(t)
                )
            )
        pres_in[block(me, rows), :] = pres_s[block(me, rows), :]
        swapped[0].wait_recv()

    chain_physics(
        nd, rows, logk_of, static_of, fault_row, parts, fault_s, coef, pres_s, before_fields,
        before_solve, after_pressure, glogk_s,
    )

    gl_b[...] = glogk_s[...].astype(jnp.bfloat16)
    spot = block(group * nd + me, rows)
    gl_got = [
        send(gl_b.at[block(cell_of(t), rows)], gl_all.at[core, spot], wide_peer(t, dx))
        for t, dx in wide
    ]
    gl_all[core, spot, :] = gl_b[block(me, rows), :]
    for copy in gl_got:
        copy.wait_recv()
    mate_got = send(gl_all.at[core], gl_all.at[core], mate)
    for copy in pres_got:
        copy.wait_recv()
    pres_out[...] = pres_in[...]
    mate_got.wait_recv()
    held = chains // 2 * rows
    for c in range(2):
        gl_f[c * held : (c + 1) * held, :] = gl_all[c].astype(jnp.float32)
    glogk = jnp.concatenate(
        [gl_f[pl.ds(r, chains, stride=rows), :] for r in range(rows)], 1
    ).astype(jnp.bfloat16)

    width = modes_n // nd

    def piece(i):
        return jnp.dot(
            glogk, basis[:, block(i, width)], preferred_element_type=jnp.float32
        )

    g_got = []
    for first, last in ((0, nd // 2), (nd // 2, nd - 1)):
        for k in range(first, last):
            gsend[k] = piece(cell_of(near[k])).astype(jnp.bfloat16)
        for k in range(first, last):
            g_got.append(send(gsend.at[k], gin.at[k], cell_peer(near[k])))
    grad = piece(me)
    for k, copy in enumerate(g_got):
        copy.wait_recv()
        grad = grad + gin[k].astype(jnp.float32)
    gfin[...] = grad.astype(jnp.bfloat16)
    g_got = [send(gfin, gall.at[me], cell_peer(t)) for t in near]
    gall[me] = gfin[...]
    for copy in g_got:
        copy.wait_recv()
    grad_out[...] = gall[...]
    for copy in sent:
        copy.wait_send()


def finish_kernel(nm, grad_ref, pres_ref, theta_ref, noise_ref, theta_out, grad_out, pres_out):
    pieces, chains, width = grad_ref.shape
    share = chains // nm
    order = [x * 2 + c for c in range(2) for x in range(nm // 2)]
    for p in range(pieces):
        cols = slice(p * width, (p + 1) * width)
        piece = grad_ref[p].astype(jnp.float32)
        g = jnp.concatenate(
            [piece[order.index(n) * share : (order.index(n) + 1) * share] for n in range(nm)], 0
        )
        t = theta_ref[:, cols]
        grad_out[:, cols] = g
        theta_out[:, cols] = (
            t - STEP_SIZE * (g + t) + math.sqrt(2.0 * STEP_SIZE) * noise_ref[:, cols]
        )
    count = pres_out.shape[0]
    rows = pres_out.shape[1] // LANES
    for r in range(rows):
        pres_out[:, r * LANES : (r + 1) * LANES] = pres_ref[pl.ds(r, count, stride=rows), :]


def fast_body(
    theta, basis, mean_logk, face_mult, storage, sources, obs_data, obs_weight,
    fault_pairs, fault_mult, noise,
):
    nd, nm = lax.axis_size("cells"), lax.axis_size("modes")
    cells, modes_n = basis.shape
    chains = theta.shape[1]
    rows = cells // LANES
    parts = fault_mult.shape[0] // LANES
    f32, bf16 = jnp.float32, jnp.bfloat16
    width = modes_n // nd
    pairs_n = nm // 2
    copies = 5 * (nd - 1) + 2 * (pairs_n * nd - 1) + 5
    vmem = pl.BlockSpec(memory_space=pltpu.VMEM)
    grad, pressure = pl.pallas_call(
        functools.partial(fused_kernel, nd, nm, rows, parts, ("cells", "modes")),
        out_shape=(
            jax.ShapeDtypeStruct((nd, chains, width), bf16),
            jax.ShapeDtypeStruct((nd * rows, LANES), f32),
        ),
        in_specs=[pl.BlockSpec(memory_space=pl.ANY)] * 10,
        out_specs=(vmem,) * 2,
        scratch_shapes=[
            pltpu.VMEM((cells, modes_n), bf16),
            pltpu.VMEM((chains, modes_n), f32),
            pltpu.VMEM((rows, LANES), f32),
            pltpu.VMEM((3, cells), f32),
            pltpu.VMEM((2, parts * LANES), jnp.int32),
            pltpu.VMEM((parts, LANES), f32),
            pltpu.VMEM((2, STAT * rows, LANES), f32),
            pltpu.VMEM((2, rows, LANES), f32),
            pltpu.VMEM((2, nd * STAT * rows, LANES), f32),
            pltpu.VMEM((2, nd * rows, LANES), f32),
            pltpu.VMEM((2, chains * rows // 2, LANES), f32),
            pltpu.VMEM((2, chains // 2 * rows // 2, LANES), f32),
            pltpu.VMEM((pairs_n * nd, rows, LANES), f32),
            pltpu.VMEM((pairs_n, nd * rows, LANES), f32),
            pltpu.VMEM((3, nd * rows, LANES), f32),
            pltpu.VMEM((18, rows, nd, LANES), f32),
            pltpu.VMEM((nd * rows, LANES), f32),
            pltpu.VMEM((nd * rows, LANES), f32),
            pltpu.VMEM((nd * rows, LANES), f32),
            pltpu.VMEM((nd * rows, LANES), bf16),
            pltpu.VMEM((2, chains // 2 * rows, LANES), bf16),
            pltpu.VMEM((chains * rows, LANES), f32),
            pltpu.VMEM((nd - 1, chains, width), bf16),
            pltpu.VMEM((nd - 1, chains, width), bf16),
            pltpu.VMEM((chains, width), bf16),
            pltpu.VMEM((nd, chains, width), bf16),
            pltpu.SemaphoreType.DMA((9,)),
            pltpu.SemaphoreType.DMA((nd,)),
            pltpu.SemaphoreType.DMA((copies,)),
            pltpu.SemaphoreType.DMA((copies,)),
        ],
        compiler_params=pltpu.CompilerParams(collective_id=0, has_side_effects=True, vmem_limit_bytes=24 << 20),
    )(
        *[pltpu.with_memory_space_constraint(a, pltpu.HBM) for a in (theta.T, basis, mean_logk.reshape(-1, LANES), face_mult, storage.reshape(-1, LANES),
        sources.reshape(-1, LANES), obs_data.reshape(-1, LANES), obs_weight.reshape(-1, LANES),
        fault_pairs.T, fault_mult.reshape(-1, LANES))],
    )
    theta_next, grad, pressure = pl.pallas_call(
        functools.partial(finish_kernel, nm),
        out_shape=(
            jax.ShapeDtypeStruct((chains, modes_n), f32),
            jax.ShapeDtypeStruct((chains, modes_n), f32),
            jax.ShapeDtypeStruct((chains // nm, cells), f32),
        ),
        in_specs=[vmem] * 4,
        out_specs=(vmem,) * 3,
        compiler_params=pltpu.CompilerParams(vmem_limit_bytes=16 << 20),
    )(grad, pressure, theta.T, noise.T)
    return (theta_next.T, grad.T, pressure)


def choose_body(theta, basis, *rest):
    share = theta.shape[1] // lax.axis_size("modes")
    nx = lax.axis_size("cells")
    whole = basis.shape[0] == NY * NZ and rest[-2].shape[0] % LANES == 0 and 2 * NZ == LANES
    paired = lax.axis_size("modes") % 2 == 0 and 3 * rest[-2].shape[0] // LANES <= basis.shape[0] // LANES
    if paired and share == nx and nx == 8 and whole and basis.shape[1] % (nx * LANES) == 0:
        return fast_body(theta, basis, *rest)
    return body(theta, basis, *rest)


def solution(mesh):
    return jax.shard_map(
        choose_body,
        mesh=mesh,
        in_specs=(
            P("modes", None),
            P("cells", "modes"),
            P("cells"),
            P(None, "cells"),
            P("cells"),
            P("cells"),
            P("cells"),
            P("cells"),
            P("cells", None),
            P("cells"),
            P("modes", None),
        ),
        out_specs=(P("modes", None), P("modes", None), P("modes", "cells")),
        check_vma=False,
    )
```

```python
import functools
import math

import jax
import jax.numpy as jnp
from jax import lax
from jax.experimental import pallas as pl
from jax.experimental.pallas import tpu as pltpu
from jax.sharding import PartitionSpec as P

NY = 32
NZ = 64
SWEEPS = 6


LOW_EIG = 0.1
HIGH_EIG = 1.9
STEP_SIZE = 0.01


def extended(block, sides, width):
    for axis, dim in sides:
        count = lax.axis_size(axis)
        forward = [(i, i + 1) for i in range(count - 1)]
        backward = [(target, source) for source, target in forward]
        low = lax.ppermute(
            lax.slice_in_dim(block, block.shape[dim] - width, None, axis=dim), axis, forward
        )
        high = lax.ppermute(lax.slice_in_dim(block, 0, width, axis=dim), axis, backward)
        block = jnp.concatenate([low, block, high], axis=dim)
    return block


def harmonic(left, right):
    return 2.0 * left * right / (left + right)


def pad_axis(array, axis, before, after):
    widths = [(0, 0)] * array.ndim
    widths[axis] = (before, after)
    return jnp.pad(array, widths)


def transmit(perm_ext, mult_ext, mult_y, mult_z, near_cell, far_cell, fault_mult, depth_y, depth_z):
    chains_n = perm_ext.shape[0]
    layers = perm_ext.shape[1] - 2
    trans_x = harmonic(perm_ext[:, :-1], perm_ext[:, 1:]) * mult_ext[:, :-1]
    perm = perm_ext[:, 1:-1].reshape(chains_n, layers, depth_y, depth_z)
    trans_y = (
        harmonic(perm[:, :, :-1], perm[:, :, 1:])
        * mult_y.reshape(1, layers, depth_y, depth_z)[:, :, :-1]
    )
    trans_z = (
        harmonic(perm[..., :-1], perm[..., 1:])
        * mult_z.reshape(1, layers, depth_y, depth_z)[..., :-1]
    )
    flat = perm.reshape(chains_n, -1)
    live = fault_mult * (near_cell != far_cell).astype(jnp.float32)
    trans_n = harmonic(flat[:, near_cell], flat[:, far_cell]) * live[None]
    return (trans_x, trans_y, trans_z, trans_n)


def diagonal_of(trans, storage, near_cell, far_cell, depth_y, depth_z):
    trans_x, trans_y, trans_z, trans_n = trans
    chains_n = trans_x.shape[0]
    layers = trans_x.shape[1] - 1
    total = (trans_x[:, 1:] + trans_x[:, :-1]).reshape(chains_n, layers, depth_y, depth_z)
    total = total + pad_axis(trans_y, 2, 0, 1) + pad_axis(trans_y, 2, 1, 0)
    total = total + pad_axis(trans_z, 3, 0, 1) + pad_axis(trans_z, 3, 1, 0)
    total = total.reshape(chains_n, -1)
    total = total.at[:, near_cell].add(trans_n).at[:, far_cell].add(trans_n)
    return total + storage[None]


def operate(field_ext, trans, storage, near_cell, far_cell, depth_y, depth_z):
    trans_x, trans_y, trans_z, trans_n = trans
    chains_n = field_ext.shape[0]
    layers = field_ext.shape[1] - 2
    flux_x = trans_x * (field_ext[:, :-1] - field_ext[:, 1:])
    result = (flux_x[:, 1:] - flux_x[:, :-1]).reshape(chains_n, layers, depth_y, depth_z)
    field = field_ext[:, 1:-1].reshape(chains_n, layers, depth_y, depth_z)
    flux_y = trans_y * (field[:, :, :-1] - field[:, :, 1:])
    result = result + pad_axis(flux_y, 2, 0, 1) - pad_axis(flux_y, 2, 1, 0)
    flux_z = trans_z * (field[..., :-1] - field[..., 1:])
    result = result + pad_axis(flux_z, 3, 0, 1) - pad_axis(flux_z, 3, 1, 0)
    result = result.reshape(chains_n, -1)
    flat = field.reshape(chains_n, -1)
    flux_n = trans_n * (flat[:, near_cell] - flat[:, far_cell])
    result = result.at[:, near_cell].add(flux_n).at[:, far_cell].add(-flux_n)
    return result + storage[None] * flat


def solve(rhs, apply_fn, diag):
    center = 0.5 * (HIGH_EIG + LOW_EIG)
    half = 0.5 * (HIGH_EIG - LOW_EIG)
    sigma = center / half
    resid = rhs / diag
    direction = resid / center
    iterate = jnp.zeros_like(rhs)
    rho = jnp.asarray(1.0 / sigma, dtype=rhs.dtype)

    def sweep_step(sweep, carry):
        iterate, resid, direction, rho = carry
        iterate = iterate + direction
        resid = resid - apply_fn(direction) / diag
        rho_next = 1.0 / (2.0 * sigma - rho)
        direction = rho_next * rho * direction + 2.0 * rho_next / half * resid
        return (iterate, resid, direction, rho_next)

    iterate, resid, direction, rho = lax.fori_loop(
        0, SWEEPS, sweep_step, (iterate, resid, direction, rho)
    )
    return iterate + direction


def gradient_of(pres_ext, adj_ext, perm_ext, trans, near_cell, far_cell, depth_y, depth_z):
    trans_x, trans_y, trans_z, trans_n = trans
    chains_n = perm_ext.shape[0]
    layers = perm_ext.shape[1] - 2
    coef_x = (
        -(adj_ext[:, :-1] - adj_ext[:, 1:])
        * (pres_ext[:, :-1] - pres_ext[:, 1:])
        * trans_x
        / (perm_ext[:, :-1] + perm_ext[:, 1:])
    )
    result = coef_x[:, 1:] * perm_ext[:, 2:] + coef_x[:, :-1] * perm_ext[:, :-2]
    result = result.reshape(chains_n, layers, depth_y, depth_z)
    shape4 = (chains_n, layers, depth_y, depth_z)
    perm = perm_ext[:, 1:-1].reshape(shape4)
    pres = pres_ext[:, 1:-1].reshape(shape4)
    adj = adj_ext[:, 1:-1].reshape(shape4)
    coef_y = (
        -(adj[:, :, :-1] - adj[:, :, 1:])
        * (pres[:, :, :-1] - pres[:, :, 1:])
        * trans_y
        / (perm[:, :, :-1] + perm[:, :, 1:])
    )
    result = (
        result
        + pad_axis(coef_y * perm[:, :, 1:], 2, 0, 1)
        + pad_axis(coef_y * perm[:, :, :-1], 2, 1, 0)
    )
    coef_z = (
        -(adj[..., :-1] - adj[..., 1:])
        * (pres[..., :-1] - pres[..., 1:])
        * trans_z
        / (perm[..., :-1] + perm[..., 1:])
    )
    result = (
        result
        + pad_axis(coef_z * perm[..., 1:], 3, 0, 1)
        + pad_axis(coef_z * perm[..., :-1], 3, 1, 0)
    )
    result = result.reshape(chains_n, -1)
    perm_f = perm.reshape(chains_n, -1)
    pres_f = pres.reshape(chains_n, -1)
    adj_f = adj.reshape(chains_n, -1)
    perm_a = perm_f[:, near_cell]
    perm_b = perm_f[:, far_cell]
    coef_n = (
        -(adj_f[:, near_cell] - adj_f[:, far_cell])
        * (pres_f[:, near_cell] - pres_f[:, far_cell])
        * trans_n
        / (perm_a + perm_b)
    )
    return result.at[:, near_cell].add(coef_n * perm_b).at[:, far_cell].add(coef_n * perm_a)


def physics(logk, face_mult, storage, sources, obs_data, obs_weight, fault_pairs, fault_mult):
    chains_n, cells_n = logk.shape
    faces = NY * NZ
    layers = cells_n // faces
    near_cell = fault_pairs[:, 0]
    far_cell = fault_pairs[:, 1]
    perm = jnp.exp(logk).reshape(chains_n, layers, faces)
    stacked = jnp.concatenate([perm, face_mult[0].reshape(1, layers, faces)], 0)
    stacked_ext = extended(stacked, (("cells", 1),), 1)
    perm_ext = stacked_ext[:chains_n]
    mult_ext = stacked_ext[chains_n:]
    trans = transmit(
        perm_ext, mult_ext, face_mult[1], face_mult[2], near_cell, far_cell, fault_mult, NY, NZ
    )
    diag = diagonal_of(trans, storage, near_cell, far_cell, NY, NZ)

    def apply_fn(field):
        field_ext = extended(field.reshape(chains_n, layers, faces), (("cells", 1),), 1)
        return operate(field_ext, trans, storage, near_cell, far_cell, NY, NZ)

    rhs = jnp.broadcast_to(sources[None], (chains_n, cells_n))
    pressure = solve(rhs, apply_fn, diag)
    misfit = obs_weight[None] * (pressure - obs_data[None])
    adjoint = solve(misfit, apply_fn, diag)
    both = jnp.concatenate([pressure, adjoint], 0).reshape(2 * chains_n, layers, faces)
    both_ext = extended(both, (("cells", 1),), 1)
    glogk = gradient_of(
        both_ext[:chains_n], both_ext[chains_n:], perm_ext, trans, near_cell, far_cell, NY, NZ
    )
    return (pressure, glogk)


def body(
    theta,
    basis,
    mean_logk,
    face_mult,
    storage,
    sources,
    obs_data,
    obs_weight,
    fault_pairs,
    fault_mult,
    noise,
):
    chains = theta.shape[1]
    share = chains // lax.axis_size("modes")
    theta_b = theta.astype(jnp.bfloat16)
    local_field = lax.dot_general(
        theta_b, basis, (((0,), (1,)), ((), ())), preferred_element_type=jnp.float32
    )
    partial_field = lax.psum(local_field, "modes")
    logk = mean_logk[None] + partial_field
    pressure, glogk = physics(
        logk, face_mult, storage, sources, obs_data, obs_weight, fault_pairs, fault_mult
    )
    glogk_b = glogk.astype(jnp.bfloat16)
    grad_rows = jnp.dot(glogk_b, basis, preferred_element_type=jnp.float32)
    pressure_out = lax.dynamic_slice_in_dim(pressure, lax.axis_index("modes") * share, share, 0)
    mode_grad = lax.psum(grad_rows, "cells")
    grad = mode_grad.T
    theta_next = theta - STEP_SIZE * (grad + theta) + math.sqrt(2.0 * STEP_SIZE) * noise
    return (theta_next, grad, pressure_out)


LANES = 128
STAT = 3


def chebyshev(rhs, inv, sweep):
    center = 0.5 * (HIGH_EIG + LOW_EIG)
    half = 0.5 * (HIGH_EIG - LOW_EIG)
    sigma = center / half
    resid = [b * v for b, v in zip(rhs, inv)]
    direction = [v * (1.0 / center) for v in resid]
    iterate = None
    rho = 1.0 / sigma
    for _ in range(SWEEPS):
        iterate = direction if iterate is None else [a + b for a, b in zip(iterate, direction)]
        resid = [v - d + s for v, d, s in zip(resid, direction, sweep(direction))]
        rho_next = 1.0 / (2.0 * sigma - rho)
        direction = [
            (rho_next * rho) * d + (2.0 * rho_next / half) * v for d, v in zip(direction, resid)
        ]
        rho = rho_next
    return [a + b for a, b in zip(iterate, direction)]


def chain_physics(nx, rows, logk_of, static_of, fault_row, parts, fault_s, coef, pres_s, before_fields, before_misfit, glogk_s):
    hi_iota = lax.broadcasted_iota(jnp.int32, (rows, LANES), 0)
    lo_iota = lax.broadcasted_iota(jnp.int32, (LANES, LANES), 0)
    for x in range(nx):
        lefts, los = [], []
        for part in range(parts):
            near = fault_row(x, part).astype(jnp.int32)
            shift = fault_row(x, parts + part).astype(jnp.int32) - near - NZ
            los.append((lo_iota == (near & (LANES - 1))).astype(jnp.bfloat16))
            hot = jnp.where(hi_iota == (near >> 7), fault_row(x, 2 * parts + part), 0.0)
            rest = [jnp.where(shift == s, hot, 0.0) for s in (1, 2, 3)]
            pieces = []
            for _ in range(3):
                top = [v.astype(jnp.bfloat16) for v in rest]
                rest = [v - t.astype(jnp.float32) for v, t in zip(rest, top)]
                pieces += top
            lefts.append(jnp.concatenate(pieces, 0))
        got = lax.dot_general(
            jnp.concatenate(lefts, 1), jnp.concatenate(los, 1), (((1,), (1,)), ((), ())),
            preferred_element_type=jnp.float32,
        )
        got = (got[: 3 * rows] + got[3 * rows : 6 * rows]) + got[6 * rows :]
        for s in range(3):
            fault_s[s, pl.ds(x * rows, rows), :] = got[s * rows : (s + 1) * rows]

    before_fields()
    lane = lax.broadcasted_iota(jnp.int32, (nx, LANES), 1)
    xpos = lax.broadcasted_iota(jnp.int32, (nx, LANES), 0)
    low = lane < NZ
    zpos = jnp.where(low, lane, lane - NZ)

    def fwd_lane(v, s):
        return pltpu.roll(v, LANES - s, 1)

    def bwd_lane(v, s):
        return pltpu.roll(v, s, 1)

    fwd_low = [((lane + s) & (LANES - 1)) < NZ for s in range(4)]
    bwd_low = [((lane - s) & (LANES - 1)) < NZ for s in range(4)]

    def up_y(vs, s, hs=None):
        n = len(vs)
        hs = [pltpu.roll(v, NZ - s, 1) for v in vs] if hs is None else hs
        return [jnp.where(fwd_low[s], hs[r], hs[(r + 1) % n]) for r in range(n)]

    def down_y(vs, s, hs=None):
        n = len(vs)
        hs = [pltpu.roll(v, NZ + s, 1) for v in vs] if hs is None else hs
        return [jnp.where(bwd_low[s], hs[r - 1], hs[r]) for r in range(n)]

    def ahead(vs):
        return (
            [pltpu.roll(v, nx - 1, 0) for v in vs],
            up_y(vs, 0),
            [fwd_lane(v, 1) for v in vs],
            up_y(vs, 1),
            up_y(vs, 2),
            up_y(vs, 3),
        )

    def behind_one(kind, vs):
        if kind == 0:
            return [pltpu.roll(v, 1, 0) for v in vs]
        if kind == 2:
            return [bwd_lane(v, 1) for v in vs]
        return down_y(vs, max(kind - 2, 0))

    every = range(rows)
    perm = [jnp.exp(logk_of(r)) for r in every]
    perm_a = ahead(perm)
    zero = jnp.zeros((nx, LANES), jnp.float32)
    diag = [static_of(3, r) for r in every]
    for k in range(6):
        trans = []
        for r in every:
            if k < 3:
                m = static_of(k, r)
            else:
                m = fault_s[k - 3, pl.ds(r, nx, stride=rows), :]
            if k == 0:
                live = xpos < nx - 1
            elif k == 1:
                live = None if r < rows - 1 else low
            elif k == 2:
                live = zpos < NZ - 1
            else:
                live = m > 0.0
            a, b = perm[r], perm_a[k][r]
            total = a + b
            t = 2.0 * a * b / total * m
            if live is not None:
                t = jnp.where(live, t, zero)
            g = t / total
            coef[12 + k, r] = g
            trans.append(t)
        back = behind_one(k, trans)
        for r in every:
            coef[2 * k, r] = trans[r]
            coef[2 * k + 1, r] = back[r]
            diag[r] = diag[r] + trans[r] + back[r]
    inv = [1.0 / v for v in diag]
    for k in range(12):
        for r in every:
            coef[k, r] = coef[k, r] * inv[r]

    def sweep(d):
        hs = [pltpu.roll(v, NZ, 1) for v in d]
        ups = [up_y(d, 0, hs)] + [up_y(d, s) for s in (1, 2, 3)]
        dns = [down_y(d, 0, hs)] + [down_y(d, s) for s in (1, 2, 3)]
        out = []
        for r in every:
            v = d[r]
            acc = coef[0, r] * pltpu.roll(v, nx - 1, 0) + coef[1, r] * pltpu.roll(v, 1, 0)
            acc2 = coef[2, r] * ups[0][r] + coef[3, r] * dns[0][r]
            acc = acc + (coef[4, r] * fwd_lane(v, 1) + coef[5, r] * bwd_lane(v, 1))
            for s in (1, 2, 3):
                acc2 = acc2 + coef[4 + 2 * s, r] * ups[s][r]
                acc = acc + coef[5 + 2 * s, r] * dns[s][r]
            out.append(acc + acc2)
        return out

    pres = chebyshev([static_of(4, r) for r in every], inv, sweep)
    for r in every:
        pres_s[pl.ds(r, nx, stride=rows), :] = pres[r]
    before_misfit()
    misfit = [static_of(6, r) * (pres[r] - static_of(5, r)) for r in every]
    adj = chebyshev(misfit, inv, sweep)
    pres_a = ahead(pres)
    adj_a = ahead(adj)
    perm_a = ahead(perm)
    total = [zero for r in every]
    for k in range(6):
        q = [
            -(adj[r] - adj_a[k][r]) * (pres[r] - pres_a[k][r]) * coef[12 + k, r] for r in every
        ]
        back = behind_one(k, [q[r] * perm[r] for r in every])
        for r in every:
            total[r] = total[r] + q[r] * perm_a[k][r] + back[r]
    for r in every:
        glogk_s[pl.ds(r, nx, stride=rows), :] = total[r]


def fused_kernel(
    nd, nm, rows, parts, axes,
    theta_hbm, basis_hbm, mean_hbm, face_hbm, storage_hbm, sources_hbm, data_hbm, weight_hbm,
    pairs_hbm, mult_hbm,
    grad_out, pres_out,
    basis, theta_v, mean_v, face_v, pairs_v, mult_v, own_stat, own_late, stat, late, part, part_in, mine, field,
    fault_s, coef, pres_s, pres_in, glogk_s, gl_b, gl_all, gl_f, gsend, gin, gfin, gall,
    load_sem, copy_sem, send_sem, recv_sem,
):
    cells_ax, modes_ax = axes
    me, mo = lax.axis_index(cells_ax), lax.axis_index(modes_ax)
    chains, modes_n = theta_v.shape
    cells = rows * LANES
    blk = cells // nd
    pairs_n = nm // 2
    core, group = lax.rem(mo, 2), lax.div(mo, 2)
    high, low = lax.div(me, 2), lax.rem(me, 2)
    srows = STAT * rows
    small = [
        (theta_hbm, theta_v),
        (face_hbm, face_v),
        (storage_hbm, own_stat.at[1, pl.ds(0, rows)]),
        (sources_hbm, own_stat.at[1, pl.ds(rows, rows)]),
        (data_hbm, own_late.at[0]),
        (weight_hbm, own_late.at[1]),
        (pairs_hbm, pairs_v),
        (mult_hbm, mult_v),
        (mean_hbm, mean_v),
    ]
    small = [pltpu.make_async_copy(a, b, load_sem.at[i]) for i, (a, b) in enumerate(small)]
    loads = [
        pltpu.make_async_copy(
            basis_hbm.at[pl.ds(k * blk, blk)], basis.at[pl.ds(k * blk, blk)], copy_sem.at[k]
        )
        for k in range(nd)
    ]
    flight = nd // 2
    for load in small + loads[:flight]:
        load.start()

    def block(i, size):
        return pl.ds(pl.multiple_of(i * size, size), size)

    steps = sorted(
        ((dz, dy) for dz in range(nd // 2) for dy in range(2)),
        key=lambda t: -(min(t[0], nd // 2 - t[0]) + t[1]),
    )

    def cell_of(step):
        return lax.rem(high + step[0], nd // 2) * 2 + lax.rem(low + step[1], 2)

    near = [t for t in steps if t != (0, 0)]
    wide = sorted(
        ((t, dx) for t in steps for dx in range(pairs_n) if (t, dx) != ((0, 0), 0)),
        key=lambda w: -(min(w[0][0], nd // 2 - w[0][0]) + w[0][1] + (w[1] > 0)),
    )
    mate = {modes_ax: group * 2 + 1 - core}

    def group_of(dx):
        return lax.rem(group + dx, pairs_n)

    def wide_peer(t, dx):
        return {cells_ax: cell_of(t), modes_ax: group_of(dx) * 2 + core}

    barrier = pltpu.get_barrier_semaphore()
    for peer in [wide_peer(t, dx) for t, dx in wide] + [mate]:
        pl.semaphore_signal(barrier, inc=1, device_id=peer, device_id_type=pl.DeviceIdType.MESH)
    greeted = len(wide) + 1
    sent = []
    count = [0]

    def send(src, dst, peer):
        slot = count[0]
        count[0] += 1
        copy = pltpu.make_async_remote_copy(
            src_ref=src, dst_ref=dst, send_sem=send_sem.at[slot], recv_sem=recv_sem.at[slot],
            device_id=peer, device_id_type=pl.DeviceIdType.MESH,
        )
        copy.start()
        sent.append(copy)
        return copy

    def cell_peer(t):
        return {cells_ax: cell_of(t)}

    for load in small:
        load.wait()
    for f in range(3):
        own_stat[0, f * rows : (f + 1) * rows, :] = jnp.concatenate(
            [face_v[f : f + 1, r * LANES : (r + 1) * LANES] for r in range(rows)], 0
        )
    pairs = pairs_v[...].astype(jnp.float32)
    spare = rows - 3 * parts
    own_stat[1, 2 * rows :, :] = jnp.concatenate(
        [pairs[e : e + 1, p * LANES : (p + 1) * LANES] for e in range(2) for p in range(parts)]
        + [mult_v[...]]
        + ([jnp.zeros((spare, LANES), jnp.float32)] if spare else []),
        0,
    )
    stat[core, block(me, srows), :] = own_stat[core]
    late[:, block(me, rows), :] = own_late[...]
    share = chains // nm
    theta_b = jnp.concatenate(
        [
            theta_v[(2 * x + c) * share : (2 * x + c + 1) * share, :]
            for c in range(2)
            for x in range(pairs_n)
        ],
        0,
    ).astype(jnp.bfloat16)
    half = rows // 2
    stat_got, part_got = [], []
    for k in range(0, nd, 2):
        for load in (k, k + 1):
            loads[load].wait()
            if load + flight < nd:
                loads[load + flight].start()
        got = lax.dot_general(
            theta_b, basis[k * blk : (k + 2) * blk, :], (((1,), (1,)), ((), ())),
            preferred_element_type=jnp.float32,
        )
        for t in range(2 * blk // LANES):
            r = k * (blk // LANES) + t
            part[r // half, pl.ds(r % half, chains, stride=half), :] = (
                got[:, t * LANES : (t + 1) * LANES]
            )
        if k == 0:
            pl.semaphore_wait(barrier, greeted)
            stat_got = [
                send(own_stat.at[core], stat.at[core, block(me, srows)], cell_peer(t))
                for t in near
            ]
        if (k + 2) % (nd // 2) == 0:
            h = k // (nd // 2)
            part_got.append(
                send(part.at[h, block(1 - core, chains // 2 * half)], part_in.at[h], mate)
            )
    mean = 1.0 / pairs_n * mean_v[...]
    for h in range(2):
        total = part[h, block(core, chains // 2 * half), :].reshape(chains // 2, half, LANES)
        total = total + mean[h * half : (h + 1) * half][None]
        part_got[h].wait_recv()
        total = total + part_in[h].reshape(chains // 2, half, LANES)
        mine[:, h * half : (h + 1) * half, :] = total
    field_got = [
        send(
            mine.at[group_of(dx) * nd + cell_of(t)], field.at[group, block(me, rows)],
            wide_peer(t, dx),
        )
        for t, dx in wide
    ]
    field[group, block(me, rows), :] = mine[group * nd + me]
    late_got = [
        send(own_late, late.at[:, block(me, rows)], cell_peer(t)) for t in near
    ]
    for copy in stat_got:
        copy.wait_recv()
    send(stat.at[core], stat.at[core], mate).wait_recv()

    def before_fields():
        for copy in field_got:
            copy.wait_recv()

    def static_of(f, r):
        if f > STAT + 1:
            return late[f - STAT - 2, pl.ds(r, nd, stride=rows), :]
        h, f = (0, f) if f < STAT else (1, f - STAT)
        return stat[h, pl.ds(f * rows + r, nd, stride=srows), :]

    def logk_of(r):
        value = field[0, pl.ds(r, nd, stride=rows), :]
        for g in range(1, pairs_n):
            value = value + field[g, pl.ds(r, nd, stride=rows), :]
        return value

    def fault_row(x, k):
        return stat[1, pl.ds(x * srows + 2 * rows + k, 1), :]

    def before_misfit():
        for copy in late_got:
            copy.wait_recv()

    chain_physics(
        nd, rows, logk_of, static_of, fault_row, parts, fault_s, coef, pres_s, before_fields,
        before_misfit, glogk_s,
    )

    gl_b[...] = glogk_s[...].astype(jnp.bfloat16)
    spot = block(group * nd + me, rows)
    gl_got = [
        send(gl_b.at[block(cell_of(t), rows)], gl_all.at[core, spot], wide_peer(t, dx))
        for t, dx in wide
    ]
    gl_all[core, spot, :] = gl_b[block(me, rows), :]
    pres_got = [
        send(pres_s.at[block(cell_of(t), rows)], pres_in.at[block(me, rows)], cell_peer(t))
        for t in near
    ]
    pres_in[block(me, rows), :] = pres_s[block(me, rows), :]
    for copy in gl_got:
        copy.wait_recv()
    mate_got = send(gl_all.at[core], gl_all.at[core], mate)
    mate_got.wait_recv()
    held = chains // 2 * rows
    for c in range(2):
        gl_f[c * held : (c + 1) * held, :] = gl_all[c].astype(jnp.float32)
    glogk = jnp.concatenate(
        [gl_f[pl.ds(r, chains, stride=rows), :] for r in range(rows)], 1
    ).astype(jnp.bfloat16)

    width = modes_n // nd

    def piece(i):
        return jnp.dot(
            glogk, basis[:, block(i, width)], preferred_element_type=jnp.float32
        )

    g_got = []
    for first, last in ((0, 2), (2, 4), (4, nd - 1)):
        for k in range(first, last):
            gsend[k] = piece(cell_of(near[k])).astype(jnp.bfloat16)
        for k in range(first, last):
            g_got.append(send(gsend.at[k], gin.at[k], cell_peer(near[k])))
    grad = piece(me)
    for k, copy in enumerate(g_got):
        copy.wait_recv()
        grad = grad + gin[k].astype(jnp.float32)
    gfin[...] = grad.astype(jnp.bfloat16)
    g_got = [send(gfin, gall.at[me], cell_peer(t)) for t in near]
    gall[me] = gfin[...]
    for copy in pres_got:
        copy.wait_recv()
    pres_out[...] = pres_in[...]
    for copy in sent[: -len(near)]:
        copy.wait_send()
    for copy in g_got:
        copy.wait_recv()
    grad_out[...] = gall[...]
    for copy in sent[-len(near) :]:
        copy.wait_send()


def finish_kernel(nm, grad_ref, pres_ref, theta_ref, noise_ref, theta_out, grad_out, pres_out):
    pieces, chains, width = grad_ref.shape
    share = chains // nm
    order = [x * 2 + c for c in range(2) for x in range(nm // 2)]
    for p in range(pieces):
        cols = slice(p * width, (p + 1) * width)
        piece = grad_ref[p].astype(jnp.float32)
        g = jnp.concatenate(
            [piece[order.index(n) * share : (order.index(n) + 1) * share] for n in range(nm)], 0
        )
        t = theta_ref[:, cols]
        grad_out[:, cols] = g
        theta_out[:, cols] = (
            t - STEP_SIZE * (g + t) + math.sqrt(2.0 * STEP_SIZE) * noise_ref[:, cols]
        )
    count = pres_out.shape[0]
    rows = pres_out.shape[1] // LANES
    for r in range(rows):
        pres_out[:, r * LANES : (r + 1) * LANES] = pres_ref[pl.ds(r, count, stride=rows), :]


def fast_body(
    theta, basis, mean_logk, face_mult, storage, sources, obs_data, obs_weight,
    fault_pairs, fault_mult, noise,
):
    nd, nm = lax.axis_size("cells"), lax.axis_size("modes")
    cells, modes_n = basis.shape
    chains = theta.shape[1]
    rows = cells // LANES
    parts = fault_mult.shape[0] // LANES
    f32, bf16 = jnp.float32, jnp.bfloat16
    width = modes_n // nd
    pairs_n = nm // 2
    copies = 5 * (nd - 1) + 2 * (pairs_n * nd - 1) + 4
    vmem = pl.BlockSpec(memory_space=pltpu.VMEM)
    grad, pressure = pl.pallas_call(
        functools.partial(fused_kernel, nd, nm, rows, parts, ("cells", "modes")),
        out_shape=(
            jax.ShapeDtypeStruct((nd, chains, width), bf16),
            jax.ShapeDtypeStruct((nd * rows, LANES), f32),
        ),
        in_specs=[pl.BlockSpec(memory_space=pl.ANY)] * 10,
        out_specs=(vmem,) * 2,
        scratch_shapes=[
            pltpu.VMEM((cells, modes_n), bf16),
            pltpu.VMEM((chains, modes_n), f32),
            pltpu.VMEM((rows, LANES), f32),
            pltpu.VMEM((3, cells), f32),
            pltpu.VMEM((2, parts * LANES), jnp.int32),
            pltpu.VMEM((parts, LANES), f32),
            pltpu.VMEM((2, STAT * rows, LANES), f32),
            pltpu.VMEM((2, rows, LANES), f32),
            pltpu.VMEM((2, nd * STAT * rows, LANES), f32),
            pltpu.VMEM((2, nd * rows, LANES), f32),
            pltpu.VMEM((2, chains * rows // 2, LANES), f32),
            pltpu.VMEM((2, chains // 2 * rows // 2, LANES), f32),
            pltpu.VMEM((pairs_n * nd, rows, LANES), f32),
            pltpu.VMEM((pairs_n, nd * rows, LANES), f32),
            pltpu.VMEM((3, nd * rows, LANES), f32),
            pltpu.VMEM((18, rows, nd, LANES), f32),
            pltpu.VMEM((nd * rows, LANES), f32),
            pltpu.VMEM((nd * rows, LANES), f32),
            pltpu.VMEM((nd * rows, LANES), f32),
            pltpu.VMEM((nd * rows, LANES), bf16),
            pltpu.VMEM((2, chains // 2 * rows, LANES), bf16),
            pltpu.VMEM((chains * rows, LANES), f32),
            pltpu.VMEM((nd - 1, chains, width), bf16),
            pltpu.VMEM((nd - 1, chains, width), bf16),
            pltpu.VMEM((chains, width), bf16),
            pltpu.VMEM((nd, chains, width), bf16),
            pltpu.SemaphoreType.DMA((9,)),
            pltpu.SemaphoreType.DMA((nd,)),
            pltpu.SemaphoreType.DMA((copies,)),
            pltpu.SemaphoreType.DMA((copies,)),
        ],
        compiler_params=pltpu.CompilerParams(collective_id=0, has_side_effects=True, vmem_limit_bytes=24 << 20),
    )(
        *[pltpu.with_memory_space_constraint(a, pltpu.HBM) for a in (theta.T, basis, mean_logk.reshape(-1, LANES), face_mult, storage.reshape(-1, LANES),
        sources.reshape(-1, LANES), obs_data.reshape(-1, LANES), obs_weight.reshape(-1, LANES),
        fault_pairs.T, fault_mult.reshape(-1, LANES))],
    )
    theta_next, grad, pressure = pl.pallas_call(
        functools.partial(finish_kernel, nm),
        out_shape=(
            jax.ShapeDtypeStruct((chains, modes_n), f32),
            jax.ShapeDtypeStruct((chains, modes_n), f32),
            jax.ShapeDtypeStruct((chains // nm, cells), f32),
        ),
        in_specs=[vmem] * 4,
        out_specs=(vmem,) * 3,
        compiler_params=pltpu.CompilerParams(vmem_limit_bytes=16 << 20),
    )(grad, pressure, theta.T, noise.T)
    return (theta_next.T, grad.T, pressure)


def choose_body(theta, basis, *rest):
    share = theta.shape[1] // lax.axis_size("modes")
    nx = lax.axis_size("cells")
    whole = basis.shape[0] == NY * NZ and rest[-2].shape[0] % LANES == 0 and 2 * NZ == LANES
    paired = lax.axis_size("modes") % 2 == 0 and 3 * rest[-2].shape[0] // LANES <= basis.shape[0] // LANES
    if paired and share == nx and nx == 8 and whole and basis.shape[1] % (nx * LANES) == 0:
        return fast_body(theta, basis, *rest)
    return body(theta, basis, *rest)


def solution(mesh):
    return jax.shard_map(
        choose_body,
        mesh=mesh,
        in_specs=(
            P("modes", None),
            P("cells", "modes"),
            P("cells"),
            P(None, "cells"),
            P("cells"),
            P("cells"),
            P("cells"),
            P("cells"),
            P("cells", None),
            P("cells"),
            P("modes", None),
        ),
        out_specs=(P("modes", None), P("modes", None), P("modes", "cells")),
        check_vma=False,
    )
```

```python
import functools
import math

import jax
import jax.numpy as jnp
from jax import lax
from jax.experimental import pallas as pl
from jax.experimental.pallas import tpu as pltpu
from jax.sharding import PartitionSpec as P

NY = 32
NZ = 64
SWEEPS = 6


LOW_EIG = 0.1
HIGH_EIG = 1.9
STEP_SIZE = 0.01


def extended(block, sides, width):
    for axis, dim in sides:
        count = lax.axis_size(axis)
        forward = [(i, i + 1) for i in range(count - 1)]
        backward = [(target, source) for source, target in forward]
        low = lax.ppermute(
            lax.slice_in_dim(block, block.shape[dim] - width, None, axis=dim), axis, forward
        )
        high = lax.ppermute(lax.slice_in_dim(block, 0, width, axis=dim), axis, backward)
        block = jnp.concatenate([low, block, high], axis=dim)
    return block


def harmonic(left, right):
    return 2.0 * left * right / (left + right)


def pad_axis(array, axis, before, after):
    widths = [(0, 0)] * array.ndim
    widths[axis] = (before, after)
    return jnp.pad(array, widths)


def transmit(perm_ext, mult_ext, mult_y, mult_z, near_cell, far_cell, fault_mult, depth_y, depth_z):
    chains_n = perm_ext.shape[0]
    layers = perm_ext.shape[1] - 2
    trans_x = harmonic(perm_ext[:, :-1], perm_ext[:, 1:]) * mult_ext[:, :-1]
    perm = perm_ext[:, 1:-1].reshape(chains_n, layers, depth_y, depth_z)
    trans_y = (
        harmonic(perm[:, :, :-1], perm[:, :, 1:])
        * mult_y.reshape(1, layers, depth_y, depth_z)[:, :, :-1]
    )
    trans_z = (
        harmonic(perm[..., :-1], perm[..., 1:])
        * mult_z.reshape(1, layers, depth_y, depth_z)[..., :-1]
    )
    flat = perm.reshape(chains_n, -1)
    live = fault_mult * (near_cell != far_cell).astype(jnp.float32)
    trans_n = harmonic(flat[:, near_cell], flat[:, far_cell]) * live[None]
    return (trans_x, trans_y, trans_z, trans_n)


def diagonal_of(trans, storage, near_cell, far_cell, depth_y, depth_z):
    trans_x, trans_y, trans_z, trans_n = trans
    chains_n = trans_x.shape[0]
    layers = trans_x.shape[1] - 1
    total = (trans_x[:, 1:] + trans_x[:, :-1]).reshape(chains_n, layers, depth_y, depth_z)
    total = total + pad_axis(trans_y, 2, 0, 1) + pad_axis(trans_y, 2, 1, 0)
    total = total + pad_axis(trans_z, 3, 0, 1) + pad_axis(trans_z, 3, 1, 0)
    total = total.reshape(chains_n, -1)
    total = total.at[:, near_cell].add(trans_n).at[:, far_cell].add(trans_n)
    return total + storage[None]


def operate(field_ext, trans, storage, near_cell, far_cell, depth_y, depth_z):
    trans_x, trans_y, trans_z, trans_n = trans
    chains_n = field_ext.shape[0]
    layers = field_ext.shape[1] - 2
    flux_x = trans_x * (field_ext[:, :-1] - field_ext[:, 1:])
    result = (flux_x[:, 1:] - flux_x[:, :-1]).reshape(chains_n, layers, depth_y, depth_z)
    field = field_ext[:, 1:-1].reshape(chains_n, layers, depth_y, depth_z)
    flux_y = trans_y * (field[:, :, :-1] - field[:, :, 1:])
    result = result + pad_axis(flux_y, 2, 0, 1) - pad_axis(flux_y, 2, 1, 0)
    flux_z = trans_z * (field[..., :-1] - field[..., 1:])
    result = result + pad_axis(flux_z, 3, 0, 1) - pad_axis(flux_z, 3, 1, 0)
    result = result.reshape(chains_n, -1)
    flat = field.reshape(chains_n, -1)
    flux_n = trans_n * (flat[:, near_cell] - flat[:, far_cell])
    result = result.at[:, near_cell].add(flux_n).at[:, far_cell].add(-flux_n)
    return result + storage[None] * flat


def solve(rhs, apply_fn, diag):
    center = 0.5 * (HIGH_EIG + LOW_EIG)
    half = 0.5 * (HIGH_EIG - LOW_EIG)
    sigma = center / half
    resid = rhs / diag
    direction = resid / center
    iterate = jnp.zeros_like(rhs)
    rho = jnp.asarray(1.0 / sigma, dtype=rhs.dtype)

    def sweep_step(sweep, carry):
        iterate, resid, direction, rho = carry
        iterate = iterate + direction
        resid = resid - apply_fn(direction) / diag
        rho_next = 1.0 / (2.0 * sigma - rho)
        direction = rho_next * rho * direction + 2.0 * rho_next / half * resid
        return (iterate, resid, direction, rho_next)

    iterate, resid, direction, rho = lax.fori_loop(
        0, SWEEPS, sweep_step, (iterate, resid, direction, rho)
    )
    return iterate + direction


def gradient_of(pres_ext, adj_ext, perm_ext, trans, near_cell, far_cell, depth_y, depth_z):
    trans_x, trans_y, trans_z, trans_n = trans
    chains_n = perm_ext.shape[0]
    layers = perm_ext.shape[1] - 2
    coef_x = (
        -(adj_ext[:, :-1] - adj_ext[:, 1:])
        * (pres_ext[:, :-1] - pres_ext[:, 1:])
        * trans_x
        / (perm_ext[:, :-1] + perm_ext[:, 1:])
    )
    result = coef_x[:, 1:] * perm_ext[:, 2:] + coef_x[:, :-1] * perm_ext[:, :-2]
    result = result.reshape(chains_n, layers, depth_y, depth_z)
    shape4 = (chains_n, layers, depth_y, depth_z)
    perm = perm_ext[:, 1:-1].reshape(shape4)
    pres = pres_ext[:, 1:-1].reshape(shape4)
    adj = adj_ext[:, 1:-1].reshape(shape4)
    coef_y = (
        -(adj[:, :, :-1] - adj[:, :, 1:])
        * (pres[:, :, :-1] - pres[:, :, 1:])
        * trans_y
        / (perm[:, :, :-1] + perm[:, :, 1:])
    )
    result = (
        result
        + pad_axis(coef_y * perm[:, :, 1:], 2, 0, 1)
        + pad_axis(coef_y * perm[:, :, :-1], 2, 1, 0)
    )
    coef_z = (
        -(adj[..., :-1] - adj[..., 1:])
        * (pres[..., :-1] - pres[..., 1:])
        * trans_z
        / (perm[..., :-1] + perm[..., 1:])
    )
    result = (
        result
        + pad_axis(coef_z * perm[..., 1:], 3, 0, 1)
        + pad_axis(coef_z * perm[..., :-1], 3, 1, 0)
    )
    result = result.reshape(chains_n, -1)
    perm_f = perm.reshape(chains_n, -1)
    pres_f = pres.reshape(chains_n, -1)
    adj_f = adj.reshape(chains_n, -1)
    perm_a = perm_f[:, near_cell]
    perm_b = perm_f[:, far_cell]
    coef_n = (
        -(adj_f[:, near_cell] - adj_f[:, far_cell])
        * (pres_f[:, near_cell] - pres_f[:, far_cell])
        * trans_n
        / (perm_a + perm_b)
    )
    return result.at[:, near_cell].add(coef_n * perm_b).at[:, far_cell].add(coef_n * perm_a)


def physics(logk, face_mult, storage, sources, obs_data, obs_weight, fault_pairs, fault_mult):
    chains_n, cells_n = logk.shape
    faces = NY * NZ
    layers = cells_n // faces
    near_cell = fault_pairs[:, 0]
    far_cell = fault_pairs[:, 1]
    perm = jnp.exp(logk).reshape(chains_n, layers, faces)
    stacked = jnp.concatenate([perm, face_mult[0].reshape(1, layers, faces)], 0)
    stacked_ext = extended(stacked, (("cells", 1),), 1)
    perm_ext = stacked_ext[:chains_n]
    mult_ext = stacked_ext[chains_n:]
    trans = transmit(
        perm_ext, mult_ext, face_mult[1], face_mult[2], near_cell, far_cell, fault_mult, NY, NZ
    )
    diag = diagonal_of(trans, storage, near_cell, far_cell, NY, NZ)

    def apply_fn(field):
        field_ext = extended(field.reshape(chains_n, layers, faces), (("cells", 1),), 1)
        return operate(field_ext, trans, storage, near_cell, far_cell, NY, NZ)

    rhs = jnp.broadcast_to(sources[None], (chains_n, cells_n))
    pressure = solve(rhs, apply_fn, diag)
    misfit = obs_weight[None] * (pressure - obs_data[None])
    adjoint = solve(misfit, apply_fn, diag)
    both = jnp.concatenate([pressure, adjoint], 0).reshape(2 * chains_n, layers, faces)
    both_ext = extended(both, (("cells", 1),), 1)
    glogk = gradient_of(
        both_ext[:chains_n], both_ext[chains_n:], perm_ext, trans, near_cell, far_cell, NY, NZ
    )
    return (pressure, glogk)


def body(
    theta,
    basis,
    mean_logk,
    face_mult,
    storage,
    sources,
    obs_data,
    obs_weight,
    fault_pairs,
    fault_mult,
    noise,
):
    chains = theta.shape[1]
    share = chains // lax.axis_size("modes")
    theta_b = theta.astype(jnp.bfloat16)
    local_field = lax.dot_general(
        theta_b, basis, (((0,), (1,)), ((), ())), preferred_element_type=jnp.float32
    )
    partial_field = lax.psum(local_field, "modes")
    logk = mean_logk[None] + partial_field
    pressure, glogk = physics(
        logk, face_mult, storage, sources, obs_data, obs_weight, fault_pairs, fault_mult
    )
    glogk_b = glogk.astype(jnp.bfloat16)
    grad_rows = jnp.dot(glogk_b, basis, preferred_element_type=jnp.float32)
    pressure_out = lax.dynamic_slice_in_dim(pressure, lax.axis_index("modes") * share, share, 0)
    mode_grad = lax.psum(grad_rows, "cells")
    grad = mode_grad.T
    theta_next = theta - STEP_SIZE * (grad + theta) + math.sqrt(2.0 * STEP_SIZE) * noise
    return (theta_next, grad, pressure_out)


LANES = 128
STAT = 3


def chebyshev(rhs, inv, sweep):
    center = 0.5 * (HIGH_EIG + LOW_EIG)
    half = 0.5 * (HIGH_EIG - LOW_EIG)
    sigma = center / half
    resid = [b * v for b, v in zip(rhs, inv)]
    direction = [v * (1.0 / center) for v in resid]
    iterate = None
    rho = 1.0 / sigma
    for _ in range(SWEEPS):
        iterate = direction if iterate is None else [a + b for a, b in zip(iterate, direction)]
        resid = [v - d + s for v, d, s in zip(resid, direction, sweep(direction))]
        rho_next = 1.0 / (2.0 * sigma - rho)
        direction = [
            (rho_next * rho) * d + (2.0 * rho_next / half) * v for d, v in zip(direction, resid)
        ]
        rho = rho_next
    return [a + b for a, b in zip(iterate, direction)]


def chain_physics(nx, rows, logk_of, static_of, fault_row, parts, fault_s, coef, pres_s, before_fields, before_misfit, glogk_s):
    hi_iota = lax.broadcasted_iota(jnp.int32, (rows, LANES), 0)
    lo_iota = lax.broadcasted_iota(jnp.int32, (LANES, LANES), 0)
    for x in range(nx):
        lefts, los = [], []
        for part in range(parts):
            near = fault_row(x, part).astype(jnp.int32)
            shift = fault_row(x, parts + part).astype(jnp.int32) - near - NZ
            los.append((lo_iota == (near & (LANES - 1))).astype(jnp.bfloat16))
            hot = jnp.where(hi_iota == (near >> 7), fault_row(x, 2 * parts + part), 0.0)
            rest = [jnp.where(shift == s, hot, 0.0) for s in (1, 2, 3)]
            pieces = []
            for _ in range(3):
                top = [v.astype(jnp.bfloat16) for v in rest]
                rest = [v - t.astype(jnp.float32) for v, t in zip(rest, top)]
                pieces += top
            lefts.append(jnp.concatenate(pieces, 0))
        got = lax.dot_general(
            jnp.concatenate(lefts, 1), jnp.concatenate(los, 1), (((1,), (1,)), ((), ())),
            preferred_element_type=jnp.float32,
        )
        got = (got[: 3 * rows] + got[3 * rows : 6 * rows]) + got[6 * rows :]
        for s in range(3):
            fault_s[s, pl.ds(x * rows, rows), :] = got[s * rows : (s + 1) * rows]

    before_fields()
    lane = lax.broadcasted_iota(jnp.int32, (nx, LANES), 1)
    xpos = lax.broadcasted_iota(jnp.int32, (nx, LANES), 0)
    low = lane < NZ
    zpos = jnp.where(low, lane, lane - NZ)

    def fwd_lane(v, s):
        return pltpu.roll(v, LANES - s, 1)

    def bwd_lane(v, s):
        return pltpu.roll(v, s, 1)

    fwd_low = [((lane + s) & (LANES - 1)) < NZ for s in range(4)]
    bwd_low = [((lane - s) & (LANES - 1)) < NZ for s in range(4)]

    def up_y(vs, s, hs=None):
        n = len(vs)
        hs = [pltpu.roll(v, NZ - s, 1) for v in vs] if hs is None else hs
        return [jnp.where(fwd_low[s], hs[r], hs[(r + 1) % n]) for r in range(n)]

    def down_y(vs, s, hs=None):
        n = len(vs)
        hs = [pltpu.roll(v, NZ + s, 1) for v in vs] if hs is None else hs
        return [jnp.where(bwd_low[s], hs[r - 1], hs[r]) for r in range(n)]

    def ahead(vs):
        return (
            [pltpu.roll(v, nx - 1, 0) for v in vs],
            up_y(vs, 0),
            [fwd_lane(v, 1) for v in vs],
            up_y(vs, 1),
            up_y(vs, 2),
            up_y(vs, 3),
        )

    def behind_one(kind, vs):
        if kind == 0:
            return [pltpu.roll(v, 1, 0) for v in vs]
        if kind == 2:
            return [bwd_lane(v, 1) for v in vs]
        return down_y(vs, max(kind - 2, 0))

    every = range(rows)
    perm = [jnp.exp(logk_of(r)) for r in every]
    perm_a = ahead(perm)
    zero = jnp.zeros((nx, LANES), jnp.float32)
    diag = [static_of(3, r) for r in every]
    for k in range(6):
        trans = []
        for r in every:
            if k < 3:
                m = static_of(k, r)
            else:
                m = fault_s[k - 3, pl.ds(r, nx, stride=rows), :]
            if k == 0:
                live = xpos < nx - 1
            elif k == 1:
                live = None if r < rows - 1 else low
            elif k == 2:
                live = zpos < NZ - 1
            else:
                live = m > 0.0
            a, b = perm[r], perm_a[k][r]
            total = a + b
            t = 2.0 * a * b / total * m
            if live is not None:
                t = jnp.where(live, t, zero)
            g = t / total
            coef[12 + k, r] = g
            trans.append(t)
        back = behind_one(k, trans)
        for r in every:
            coef[2 * k, r] = trans[r]
            coef[2 * k + 1, r] = back[r]
            diag[r] = diag[r] + trans[r] + back[r]
    inv = [1.0 / v for v in diag]
    for k in range(12):
        for r in every:
            coef[k, r] = coef[k, r] * inv[r]

    def sweep(d):
        hs = [pltpu.roll(v, NZ, 1) for v in d]
        ups = [up_y(d, 0, hs)] + [up_y(d, s) for s in (1, 2, 3)]
        dns = [down_y(d, 0, hs)] + [down_y(d, s) for s in (1, 2, 3)]
        out = []
        for r in every:
            v = d[r]
            acc = coef[0, r] * pltpu.roll(v, nx - 1, 0) + coef[1, r] * pltpu.roll(v, 1, 0)
            acc2 = coef[2, r] * ups[0][r] + coef[3, r] * dns[0][r]
            acc = acc + (coef[4, r] * fwd_lane(v, 1) + coef[5, r] * bwd_lane(v, 1))
            for s in (1, 2, 3):
                acc2 = acc2 + coef[4 + 2 * s, r] * ups[s][r]
                acc = acc + coef[5 + 2 * s, r] * dns[s][r]
            out.append(acc + acc2)
        return out

    pres = chebyshev([static_of(4, r) for r in every], inv, sweep)
    for r in every:
        pres_s[pl.ds(r, nx, stride=rows), :] = pres[r]
    pres_a = ahead(pres)
    perm_a = ahead(perm)
    for k in range(6):
        for r in every:
            drop = (pres[r] - pres_a[k][r]) * coef[12 + k, r]
            coef[12 + k, r] = drop * perm_a[k][r]
            coef[18 + k, r] = drop * perm[r]
    before_misfit()
    misfit = [static_of(6, r) * (pres[r] - static_of(5, r)) for r in every]
    adj = chebyshev(misfit, inv, sweep)
    adj_a = ahead(adj)
    total = [zero for r in every]
    for k in range(6):
        rise = [adj_a[k][r] - adj[r] for r in every]
        back = behind_one(k, [rise[r] * coef[18 + k, r] for r in every])
        for r in every:
            total[r] = total[r] + rise[r] * coef[12 + k, r] + back[r]
    for r in every:
        glogk_s[pl.ds(r, nx, stride=rows), :] = total[r]


def fused_kernel(
    nd, nm, rows, parts, axes,
    theta_hbm, basis_hbm, mean_hbm, face_hbm, storage_hbm, sources_hbm, data_hbm, weight_hbm,
    pairs_hbm, mult_hbm, noise_hbm,
    grad_out, pres_out, drift_out,
    basis, theta_v, noise_v, mean_v, face_v, pairs_v, mult_v, own_stat, own_late, stat, late, part, part_in, mine, field,
    fault_s, coef, pres_s, pres_in, glogk_s, gl_b, gl_all, gl_f, gsend, gin, gfin, gall,
    load_sem, copy_sem, noise_sem, send_sem, recv_sem,
):
    cells_ax, modes_ax = axes
    me, mo = lax.axis_index(cells_ax), lax.axis_index(modes_ax)
    chains, modes_n = theta_v.shape
    cells = rows * LANES
    blk = cells // nd
    pairs_n = nm // 2
    core, group = lax.rem(mo, 2), lax.div(mo, 2)
    high, low = lax.div(me, 2), lax.rem(me, 2)
    srows = STAT * rows
    small = [
        (theta_hbm, theta_v),
        (face_hbm, face_v),
        (storage_hbm, own_stat.at[1, pl.ds(0, rows)]),
        (sources_hbm, own_stat.at[1, pl.ds(rows, rows)]),
        (data_hbm, own_late.at[0]),
        (weight_hbm, own_late.at[1]),
        (pairs_hbm, pairs_v),
        (mult_hbm, mult_v),
        (mean_hbm, mean_v),
    ]
    small = [pltpu.make_async_copy(a, b, load_sem.at[i]) for i, (a, b) in enumerate(small)]
    loads = [
        pltpu.make_async_copy(
            basis_hbm.at[pl.ds(k * blk, blk)], basis.at[pl.ds(k * blk, blk)], copy_sem.at[k]
        )
        for k in range(nd)
    ]
    flight = nd // 2
    for load in small + loads[:flight]:
        load.start()

    def block(i, size):
        return pl.ds(pl.multiple_of(i * size, size), size)

    steps = sorted(
        ((dz, dy) for dz in range(nd // 2) for dy in range(2)),
        key=lambda t: -(min(t[0], nd // 2 - t[0]) + 2 * t[1]),
    )

    def cell_of(step):
        return lax.rem(high + step[0], nd // 2) * 2 + lax.rem(low + step[1], 2)

    near = [t for t in steps if t != (0, 0)]
    wide = sorted(
        ((t, dx) for t in steps for dx in range(pairs_n) if (t, dx) != ((0, 0), 0)),
        key=lambda w: -(min(w[0][0], nd // 2 - w[0][0]) + 2 * w[0][1] + 2 * (w[1] > 0)),
    )
    mate = {modes_ax: group * 2 + 1 - core}

    def group_of(dx):
        return lax.rem(group + dx, pairs_n)

    def wide_peer(t, dx):
        return {cells_ax: cell_of(t), modes_ax: group_of(dx) * 2 + core}

    barrier = pltpu.get_barrier_semaphore()
    for peer in [wide_peer(t, dx) for t, dx in wide] + [mate]:
        pl.semaphore_signal(barrier, inc=1, device_id=peer, device_id_type=pl.DeviceIdType.MESH)
    greeted = len(wide) + 1
    sent = []
    count = [0]

    def send(src, dst, peer):
        slot = count[0]
        count[0] += 1
        copy = pltpu.make_async_remote_copy(
            src_ref=src, dst_ref=dst, send_sem=send_sem.at[slot], recv_sem=recv_sem.at[slot],
            device_id=peer, device_id_type=pl.DeviceIdType.MESH,
        )
        copy.start()
        sent.append(copy)
        return copy

    def cell_peer(t):
        return {cells_ax: cell_of(t)}

    for load in small:
        load.wait()
    for f in range(3):
        own_stat[0, f * rows : (f + 1) * rows, :] = jnp.concatenate(
            [face_v[f : f + 1, r * LANES : (r + 1) * LANES] for r in range(rows)], 0
        )
    pairs = pairs_v[...].astype(jnp.float32)
    spare = rows - 3 * parts
    own_stat[1, 2 * rows :, :] = jnp.concatenate(
        [pairs[e : e + 1, p * LANES : (p + 1) * LANES] for e in range(2) for p in range(parts)]
        + [mult_v[...]]
        + ([jnp.zeros((spare, LANES), jnp.float32)] if spare else []),
        0,
    )
    stat[core, block(me, srows), :] = own_stat[core]
    late[:, block(me, rows), :] = own_late[...]
    share = chains // nm
    theta_b = jnp.concatenate(
        [
            theta_v[(2 * x + c) * share : (2 * x + c + 1) * share, :]
            for c in range(2)
            for x in range(pairs_n)
        ],
        0,
    ).astype(jnp.bfloat16)
    half = rows // 2
    stat_got, part_got = [], []
    for k in range(0, nd, 2):
        for load in (k, k + 1):
            loads[load].wait()
            if load + flight < nd:
                loads[load + flight].start()
        got = lax.dot_general(
            theta_b, basis[k * blk : (k + 2) * blk, :], (((1,), (1,)), ((), ())),
            preferred_element_type=jnp.float32,
        )
        for t in range(2 * blk // LANES):
            r = k * (blk // LANES) + t
            part[r // half, pl.ds(r % half, chains, stride=half), :] = (
                got[:, t * LANES : (t + 1) * LANES]
            )
        if k == 0:
            pl.semaphore_wait(barrier, greeted)
            stat_got = [
                send(own_stat.at[core], stat.at[core, block(me, srows)], cell_peer(t))
                for t in near
            ]
        if (k + 2) % (nd // 2) == 0:
            h = k // (nd // 2)
            part_got.append(
                send(part.at[h, block(1 - core, chains // 2 * half)], part_in.at[h], mate)
            )
    noise_load = pltpu.make_async_copy(noise_hbm, noise_v, noise_sem)
    noise_load.start()
    mean = 1.0 / pairs_n * mean_v[...]
    for h in range(2):
        total = part[h, block(core, chains // 2 * half), :].reshape(chains // 2, half, LANES)
        total = total + mean[h * half : (h + 1) * half][None]
        part_got[h].wait_recv()
        total = total + part_in[h].reshape(chains // 2, half, LANES)
        mine[:, h * half : (h + 1) * half, :] = total
    field_got = [
        send(
            mine.at[group_of(dx) * nd + cell_of(t)], field.at[group, block(me, rows)],
            wide_peer(t, dx),
        )
        for t, dx in wide
    ]
    field[group, block(me, rows), :] = mine[group * nd + me]
    late_got = [
        send(own_late, late.at[:, block(me, rows)], cell_peer(t)) for t in near
    ]
    for copy in stat_got:
        copy.wait_recv()
    send(stat.at[core], stat.at[core], mate).wait_recv()

    def before_fields():
        for copy in field_got:
            copy.wait_recv()

    def static_of(f, r):
        if f > STAT + 1:
            return late[f - STAT - 2, pl.ds(r, nd, stride=rows), :]
        h, f = (0, f) if f < STAT else (1, f - STAT)
        return stat[h, pl.ds(f * rows + r, nd, stride=srows), :]

    def logk_of(r):
        value = field[0, pl.ds(r, nd, stride=rows), :]
        for g in range(1, pairs_n):
            value = value + field[g, pl.ds(r, nd, stride=rows), :]
        return value

    def fault_row(x, k):
        return stat[1, pl.ds(x * srows + 2 * rows + k, 1), :]

    def before_misfit():
        for copy in late_got:
            copy.wait_recv()

    chain_physics(
        nd, rows, logk_of, static_of, fault_row, parts, fault_s, coef, pres_s, before_fields,
        before_misfit, glogk_s,
    )

    gl_b[...] = glogk_s[...].astype(jnp.bfloat16)
    spot = block(group * nd + me, rows)
    gl_got = [
        send(gl_b.at[block(cell_of(t), rows)], gl_all.at[core, spot], wide_peer(t, dx))
        for t, dx in wide
    ]
    gl_all[core, spot, :] = gl_b[block(me, rows), :]
    pres_got = [
        send(pres_s.at[block(cell_of(t), rows)], pres_in.at[block(me, rows)], cell_peer(t))
        for t in near
    ]
    pres_in[block(me, rows), :] = pres_s[block(me, rows), :]
    noise_load.wait()
    drift_out[...] = (1.0 - STEP_SIZE) * theta_v[...] + math.sqrt(2.0 * STEP_SIZE) * noise_v[...]
    for copy in gl_got:
        copy.wait_recv()
    mate_got = send(gl_all.at[core], gl_all.at[core], mate)
    mate_got.wait_recv()
    held = chains // 2 * rows
    for c in range(2):
        gl_f[c * held : (c + 1) * held, :] = gl_all[c].astype(jnp.float32)
    glogk = jnp.concatenate(
        [gl_f[pl.ds(r, chains, stride=rows), :] for r in range(rows)], 1
    ).astype(jnp.bfloat16)

    width = modes_n // nd

    def piece(i):
        return jnp.dot(
            glogk, basis[:, block(i, width)], preferred_element_type=jnp.float32
        )

    g_got = []
    for first, last in ((0, 2), (2, 4), (4, nd - 1)):
        for k in range(first, last):
            gsend[k] = piece(cell_of(near[k])).astype(jnp.bfloat16)
        for k in range(first, last):
            g_got.append(send(gsend.at[k], gin.at[k], cell_peer(near[k])))
    grad = piece(me)
    for k, copy in enumerate(g_got):
        copy.wait_recv()
        grad = grad + gin[k].astype(jnp.float32)
    gfin[...] = grad.astype(jnp.bfloat16)
    g_got = [send(gfin, gall.at[me], cell_peer(t)) for t in near]
    gall[me] = gfin[...]
    for copy in pres_got:
        copy.wait_recv()
    pres_out[...] = pres_in[...]
    for copy in sent[: -len(near)]:
        copy.wait_send()
    for copy in g_got:
        copy.wait_recv()
    grad_out[...] = gall[...]
    for copy in sent[-len(near) :]:
        copy.wait_send()


def finish_kernel(
    nm, grad_ref, pres_ref, drift_ref, theta_hbm, grad_hbm, pres_hbm, theta_v, grad_v, pres_v, sems
):
    pieces, chains, width = grad_ref.shape
    share = chains // nm
    order = [x * 2 + c for c in range(2) for x in range(nm // 2)]
    count = pres_v.shape[0]
    rows = pres_v.shape[1] // LANES
    for r in range(rows):
        pres_v[:, r * LANES : (r + 1) * LANES] = pres_ref[pl.ds(r, count, stride=rows), :]
    copies = [pltpu.make_async_copy(pres_v, pres_hbm, sems.at[0])]
    copies[0].start()
    group = pieces // 4
    for q in range(4):
        for p in range(q * group, (q + 1) * group):
            cols = slice(p * width, (p + 1) * width)
            piece = grad_ref[p].astype(jnp.float32)
            g = jnp.concatenate(
                [piece[order.index(n) * share : (order.index(n) + 1) * share] for n in range(nm)],
                0,
            )
            grad_v[:, cols] = g
            theta_v[:, cols] = drift_ref[:, cols] - STEP_SIZE * g
        cols = pl.ds(q * group * width, group * width)
        for i, (src, dst) in enumerate(((grad_v, grad_hbm), (theta_v, theta_hbm))):
            copy = pltpu.make_async_copy(src.at[:, cols], dst.at[:, cols], sems.at[1 + 2 * q + i])
            copy.start()
            copies.append(copy)
    for copy in copies:
        copy.wait()


def fast_body(
    theta, basis, mean_logk, face_mult, storage, sources, obs_data, obs_weight,
    fault_pairs, fault_mult, noise,
):
    nd, nm = lax.axis_size("cells"), lax.axis_size("modes")
    cells, modes_n = basis.shape
    chains = theta.shape[1]
    rows = cells // LANES
    parts = fault_mult.shape[0] // LANES
    f32, bf16 = jnp.float32, jnp.bfloat16
    width = modes_n // nd
    pairs_n = nm // 2
    copies = 5 * (nd - 1) + 2 * (pairs_n * nd - 1) + 4
    vmem = pl.BlockSpec(memory_space=pltpu.VMEM)
    grad, pressure, drift = pl.pallas_call(
        functools.partial(fused_kernel, nd, nm, rows, parts, ("cells", "modes")),
        out_shape=(
            jax.ShapeDtypeStruct((nd, chains, width), bf16),
            jax.ShapeDtypeStruct((nd * rows, LANES), f32),
            jax.ShapeDtypeStruct((chains, modes_n), f32),
        ),
        in_specs=[pl.BlockSpec(memory_space=pl.ANY)] * 11,
        out_specs=(vmem,) * 3,
        scratch_shapes=[
            pltpu.VMEM((cells, modes_n), bf16),
            pltpu.VMEM((chains, modes_n), f32),
            pltpu.VMEM((chains, modes_n), f32),
            pltpu.VMEM((rows, LANES), f32),
            pltpu.VMEM((3, cells), f32),
            pltpu.VMEM((2, parts * LANES), jnp.int32),
            pltpu.VMEM((parts, LANES), f32),
            pltpu.VMEM((2, STAT * rows, LANES), f32),
            pltpu.VMEM((2, rows, LANES), f32),
            pltpu.VMEM((2, nd * STAT * rows, LANES), f32),
            pltpu.VMEM((2, nd * rows, LANES), f32),
            pltpu.VMEM((2, chains * rows // 2, LANES), f32),
            pltpu.VMEM((2, chains // 2 * rows // 2, LANES), f32),
            pltpu.VMEM((pairs_n * nd, rows, LANES), f32),
            pltpu.VMEM((pairs_n, nd * rows, LANES), f32),
            pltpu.VMEM((3, nd * rows, LANES), f32),
            pltpu.VMEM((24, rows, nd, LANES), f32),
            pltpu.VMEM((nd * rows, LANES), f32),
            pltpu.VMEM((nd * rows, LANES), f32),
            pltpu.VMEM((nd * rows, LANES), f32),
            pltpu.VMEM((nd * rows, LANES), bf16),
            pltpu.VMEM((2, chains // 2 * rows, LANES), bf16),
            pltpu.VMEM((chains * rows, LANES), f32),
            pltpu.VMEM((nd - 1, chains, width), bf16),
            pltpu.VMEM((nd - 1, chains, width), bf16),
            pltpu.VMEM((chains, width), bf16),
            pltpu.VMEM((nd, chains, width), bf16),
            pltpu.SemaphoreType.DMA((9,)),
            pltpu.SemaphoreType.DMA((nd,)),
            pltpu.SemaphoreType.DMA,
            pltpu.SemaphoreType.DMA((copies,)),
            pltpu.SemaphoreType.DMA((copies,)),
        ],
        compiler_params=pltpu.CompilerParams(collective_id=0, has_side_effects=True, vmem_limit_bytes=24 << 20),
    )(
        *[pltpu.with_memory_space_constraint(a, pltpu.HBM) for a in (theta.T, basis, mean_logk.reshape(-1, LANES), face_mult, storage.reshape(-1, LANES),
        sources.reshape(-1, LANES), obs_data.reshape(-1, LANES), obs_weight.reshape(-1, LANES),
        fault_pairs.T, fault_mult.reshape(-1, LANES), noise.T)],
    )
    theta_next, grad, pressure = pl.pallas_call(
        functools.partial(finish_kernel, nm),
        out_shape=(
            jax.ShapeDtypeStruct((chains, modes_n), f32),
            jax.ShapeDtypeStruct((chains, modes_n), f32),
            jax.ShapeDtypeStruct((chains // nm, cells), f32),
        ),
        in_specs=[vmem] * 3,
        out_specs=(pl.BlockSpec(memory_space=pl.ANY),) * 3,
        scratch_shapes=[
            pltpu.VMEM((chains, modes_n), f32),
            pltpu.VMEM((chains, modes_n), f32),
            pltpu.VMEM((chains // nm, cells), f32),
            pltpu.SemaphoreType.DMA((9,)),
        ],
        compiler_params=pltpu.CompilerParams(vmem_limit_bytes=16 << 20),
    )(grad, pressure, drift)
    return (theta_next.T, grad.T, pressure)


def choose_body(theta, basis, *rest):
    share = theta.shape[1] // lax.axis_size("modes")
    nx = lax.axis_size("cells")
    whole = basis.shape[0] == NY * NZ and rest[-2].shape[0] % LANES == 0 and 2 * NZ == LANES
    paired = lax.axis_size("modes") % 2 == 0 and 3 * rest[-2].shape[0] // LANES <= basis.shape[0] // LANES
    if paired and share == nx and nx == 8 and whole and basis.shape[1] % (nx * LANES) == 0:
        return fast_body(theta, basis, *rest)
    return body(theta, basis, *rest)


def solution(mesh):
    return jax.shard_map(
        choose_body,
        mesh=mesh,
        in_specs=(
            P("modes", None),
            P("cells", "modes"),
            P("cells"),
            P(None, "cells"),
            P("cells"),
            P("cells"),
            P("cells"),
            P("cells"),
            P("cells", None),
            P("cells"),
            P("modes", None),
        ),
        out_specs=(P("modes", None), P("modes", None), P("modes", "cells")),
        check_vma=False,
    )
```

```python
import functools
import math

import jax
import jax.numpy as jnp
from jax import lax
from jax.experimental import pallas as pl
from jax.experimental.pallas import tpu as pltpu
from jax.sharding import PartitionSpec as P

NY = 32
NZ = 64
SWEEPS = 6


LOW_EIG = 0.1
HIGH_EIG = 1.9
STEP_SIZE = 0.01


def extended(block, sides, width):
    for axis, dim in sides:
        count = lax.axis_size(axis)
        forward = [(i, i + 1) for i in range(count - 1)]
        backward = [(target, source) for source, target in forward]
        low = lax.ppermute(
            lax.slice_in_dim(block, block.shape[dim] - width, None, axis=dim), axis, forward
        )
        high = lax.ppermute(lax.slice_in_dim(block, 0, width, axis=dim), axis, backward)
        block = jnp.concatenate([low, block, high], axis=dim)
    return block


def harmonic(left, right):
    return 2.0 * left * right / (left + right)


def pad_axis(array, axis, before, after):
    widths = [(0, 0)] * array.ndim
    widths[axis] = (before, after)
    return jnp.pad(array, widths)


def transmit(perm_ext, mult_ext, mult_y, mult_z, near_cell, far_cell, fault_mult, depth_y, depth_z):
    chains_n = perm_ext.shape[0]
    layers = perm_ext.shape[1] - 2
    trans_x = harmonic(perm_ext[:, :-1], perm_ext[:, 1:]) * mult_ext[:, :-1]
    perm = perm_ext[:, 1:-1].reshape(chains_n, layers, depth_y, depth_z)
    trans_y = (
        harmonic(perm[:, :, :-1], perm[:, :, 1:])
        * mult_y.reshape(1, layers, depth_y, depth_z)[:, :, :-1]
    )
    trans_z = (
        harmonic(perm[..., :-1], perm[..., 1:])
        * mult_z.reshape(1, layers, depth_y, depth_z)[..., :-1]
    )
    flat = perm.reshape(chains_n, -1)
    live = fault_mult * (near_cell != far_cell).astype(jnp.float32)
    trans_n = harmonic(flat[:, near_cell], flat[:, far_cell]) * live[None]
    return (trans_x, trans_y, trans_z, trans_n)


def diagonal_of(trans, storage, near_cell, far_cell, depth_y, depth_z):
    trans_x, trans_y, trans_z, trans_n = trans
    chains_n = trans_x.shape[0]
    layers = trans_x.shape[1] - 1
    total = (trans_x[:, 1:] + trans_x[:, :-1]).reshape(chains_n, layers, depth_y, depth_z)
    total = total + pad_axis(trans_y, 2, 0, 1) + pad_axis(trans_y, 2, 1, 0)
    total = total + pad_axis(trans_z, 3, 0, 1) + pad_axis(trans_z, 3, 1, 0)
    total = total.reshape(chains_n, -1)
    total = total.at[:, near_cell].add(trans_n).at[:, far_cell].add(trans_n)
    return total + storage[None]


def operate(field_ext, trans, storage, near_cell, far_cell, depth_y, depth_z):
    trans_x, trans_y, trans_z, trans_n = trans
    chains_n = field_ext.shape[0]
    layers = field_ext.shape[1] - 2
    flux_x = trans_x * (field_ext[:, :-1] - field_ext[:, 1:])
    result = (flux_x[:, 1:] - flux_x[:, :-1]).reshape(chains_n, layers, depth_y, depth_z)
    field = field_ext[:, 1:-1].reshape(chains_n, layers, depth_y, depth_z)
    flux_y = trans_y * (field[:, :, :-1] - field[:, :, 1:])
    result = result + pad_axis(flux_y, 2, 0, 1) - pad_axis(flux_y, 2, 1, 0)
    flux_z = trans_z * (field[..., :-1] - field[..., 1:])
    result = result + pad_axis(flux_z, 3, 0, 1) - pad_axis(flux_z, 3, 1, 0)
    result = result.reshape(chains_n, -1)
    flat = field.reshape(chains_n, -1)
    flux_n = trans_n * (flat[:, near_cell] - flat[:, far_cell])
    result = result.at[:, near_cell].add(flux_n).at[:, far_cell].add(-flux_n)
    return result + storage[None] * flat


def solve(rhs, apply_fn, diag):
    center = 0.5 * (HIGH_EIG + LOW_EIG)
    half = 0.5 * (HIGH_EIG - LOW_EIG)
    sigma = center / half
    resid = rhs / diag
    direction = resid / center
    iterate = jnp.zeros_like(rhs)
    rho = jnp.asarray(1.0 / sigma, dtype=rhs.dtype)

    def sweep_step(sweep, carry):
        iterate, resid, direction, rho = carry
        iterate = iterate + direction
        resid = resid - apply_fn(direction) / diag
        rho_next = 1.0 / (2.0 * sigma - rho)
        direction = rho_next * rho * direction + 2.0 * rho_next / half * resid
        return (iterate, resid, direction, rho_next)

    iterate, resid, direction, rho = lax.fori_loop(
        0, SWEEPS, sweep_step, (iterate, resid, direction, rho)
    )
    return iterate + direction


def gradient_of(pres_ext, adj_ext, perm_ext, trans, near_cell, far_cell, depth_y, depth_z):
    trans_x, trans_y, trans_z, trans_n = trans
    chains_n = perm_ext.shape[0]
    layers = perm_ext.shape[1] - 2
    coef_x = (
        -(adj_ext[:, :-1] - adj_ext[:, 1:])
        * (pres_ext[:, :-1] - pres_ext[:, 1:])
        * trans_x
        / (perm_ext[:, :-1] + perm_ext[:, 1:])
    )
    result = coef_x[:, 1:] * perm_ext[:, 2:] + coef_x[:, :-1] * perm_ext[:, :-2]
    result = result.reshape(chains_n, layers, depth_y, depth_z)
    shape4 = (chains_n, layers, depth_y, depth_z)
    perm = perm_ext[:, 1:-1].reshape(shape4)
    pres = pres_ext[:, 1:-1].reshape(shape4)
    adj = adj_ext[:, 1:-1].reshape(shape4)
    coef_y = (
        -(adj[:, :, :-1] - adj[:, :, 1:])
        * (pres[:, :, :-1] - pres[:, :, 1:])
        * trans_y
        / (perm[:, :, :-1] + perm[:, :, 1:])
    )
    result = (
        result
        + pad_axis(coef_y * perm[:, :, 1:], 2, 0, 1)
        + pad_axis(coef_y * perm[:, :, :-1], 2, 1, 0)
    )
    coef_z = (
        -(adj[..., :-1] - adj[..., 1:])
        * (pres[..., :-1] - pres[..., 1:])
        * trans_z
        / (perm[..., :-1] + perm[..., 1:])
    )
    result = (
        result
        + pad_axis(coef_z * perm[..., 1:], 3, 0, 1)
        + pad_axis(coef_z * perm[..., :-1], 3, 1, 0)
    )
    result = result.reshape(chains_n, -1)
    perm_f = perm.reshape(chains_n, -1)
    pres_f = pres.reshape(chains_n, -1)
    adj_f = adj.reshape(chains_n, -1)
    perm_a = perm_f[:, near_cell]
    perm_b = perm_f[:, far_cell]
    coef_n = (
        -(adj_f[:, near_cell] - adj_f[:, far_cell])
        * (pres_f[:, near_cell] - pres_f[:, far_cell])
        * trans_n
        / (perm_a + perm_b)
    )
    return result.at[:, near_cell].add(coef_n * perm_b).at[:, far_cell].add(coef_n * perm_a)


def physics(logk, face_mult, storage, sources, obs_data, obs_weight, fault_pairs, fault_mult):
    chains_n, cells_n = logk.shape
    faces = NY * NZ
    layers = cells_n // faces
    near_cell = fault_pairs[:, 0]
    far_cell = fault_pairs[:, 1]
    perm = jnp.exp(logk).reshape(chains_n, layers, faces)
    stacked = jnp.concatenate([perm, face_mult[0].reshape(1, layers, faces)], 0)
    stacked_ext = extended(stacked, (("cells", 1),), 1)
    perm_ext = stacked_ext[:chains_n]
    mult_ext = stacked_ext[chains_n:]
    trans = transmit(
        perm_ext, mult_ext, face_mult[1], face_mult[2], near_cell, far_cell, fault_mult, NY, NZ
    )
    diag = diagonal_of(trans, storage, near_cell, far_cell, NY, NZ)

    def apply_fn(field):
        field_ext = extended(field.reshape(chains_n, layers, faces), (("cells", 1),), 1)
        return operate(field_ext, trans, storage, near_cell, far_cell, NY, NZ)

    rhs = jnp.broadcast_to(sources[None], (chains_n, cells_n))
    pressure = solve(rhs, apply_fn, diag)
    misfit = obs_weight[None] * (pressure - obs_data[None])
    adjoint = solve(misfit, apply_fn, diag)
    both = jnp.concatenate([pressure, adjoint], 0).reshape(2 * chains_n, layers, faces)
    both_ext = extended(both, (("cells", 1),), 1)
    glogk = gradient_of(
        both_ext[:chains_n], both_ext[chains_n:], perm_ext, trans, near_cell, far_cell, NY, NZ
    )
    return (pressure, glogk)


def body(
    theta,
    basis,
    mean_logk,
    face_mult,
    storage,
    sources,
    obs_data,
    obs_weight,
    fault_pairs,
    fault_mult,
    noise,
):
    chains = theta.shape[1]
    share = chains // lax.axis_size("modes")
    theta_b = theta.astype(jnp.bfloat16)
    local_field = lax.dot_general(
        theta_b, basis, (((0,), (1,)), ((), ())), preferred_element_type=jnp.float32
    )
    partial_field = lax.psum(local_field, "modes")
    logk = mean_logk[None] + partial_field
    pressure, glogk = physics(
        logk, face_mult, storage, sources, obs_data, obs_weight, fault_pairs, fault_mult
    )
    glogk_b = glogk.astype(jnp.bfloat16)
    grad_rows = jnp.dot(glogk_b, basis, preferred_element_type=jnp.float32)
    pressure_out = lax.dynamic_slice_in_dim(pressure, lax.axis_index("modes") * share, share, 0)
    mode_grad = lax.psum(grad_rows, "cells")
    grad = mode_grad.T
    theta_next = theta - STEP_SIZE * (grad + theta) + math.sqrt(2.0 * STEP_SIZE) * noise
    return (theta_next, grad, pressure_out)


LANES = 128
STAT = 3


def chebyshev(rhs, inv, sweep):
    center = 0.5 * (HIGH_EIG + LOW_EIG)
    half = 0.5 * (HIGH_EIG - LOW_EIG)
    sigma = center / half
    resid = [b * v for b, v in zip(rhs, inv)]
    direction = [v * (1.0 / center) for v in resid]
    iterate = None
    rho = 1.0 / sigma
    for _ in range(SWEEPS):
        iterate = direction if iterate is None else [a + b for a, b in zip(iterate, direction)]
        resid = [v - d + s for v, d, s in zip(resid, direction, sweep(direction))]
        rho_next = 1.0 / (2.0 * sigma - rho)
        direction = [
            (rho_next * rho) * d + (2.0 * rho_next / half) * v for d, v in zip(direction, resid)
        ]
        rho = rho_next
    return [a + b for a, b in zip(iterate, direction)]


def chain_physics(nx, rows, logk_of, static_of, fault_row, parts, fault_s, coef, pres_s, before_fields, before_misfit, glogk_s):
    hi_iota = lax.broadcasted_iota(jnp.int32, (rows, LANES), 0)
    lo_iota = lax.broadcasted_iota(jnp.int32, (LANES, LANES), 0)
    for x in range(nx):
        lefts, los = [], []
        for part in range(parts):
            near = fault_row(x, part).astype(jnp.int32)
            shift = fault_row(x, parts + part).astype(jnp.int32) - near - NZ
            los.append((lo_iota == (near & (LANES - 1))).astype(jnp.bfloat16))
            hot = jnp.where(hi_iota == (near >> 7), fault_row(x, 2 * parts + part), 0.0)
            rest = [jnp.where(shift == s, hot, 0.0) for s in (1, 2, 3)]
            pieces = []
            for _ in range(3):
                top = [v.astype(jnp.bfloat16) for v in rest]
                rest = [v - t.astype(jnp.float32) for v, t in zip(rest, top)]
                pieces += top
            lefts.append(jnp.concatenate(pieces, 0))
        got = lax.dot_general(
            jnp.concatenate(lefts, 1), jnp.concatenate(los, 1), (((1,), (1,)), ((), ())),
            preferred_element_type=jnp.float32,
        )
        got = (got[: 3 * rows] + got[3 * rows : 6 * rows]) + got[6 * rows :]
        for s in range(3):
            fault_s[s, pl.ds(x * rows, rows), :] = got[s * rows : (s + 1) * rows]

    before_fields()
    lane = lax.broadcasted_iota(jnp.int32, (nx, LANES), 1)
    xpos = lax.broadcasted_iota(jnp.int32, (nx, LANES), 0)
    low = lane < NZ
    zpos = jnp.where(low, lane, lane - NZ)

    def fwd_lane(v, s):
        return pltpu.roll(v, LANES - s, 1)

    def bwd_lane(v, s):
        return pltpu.roll(v, s, 1)

    fwd_low = [((lane + s) & (LANES - 1)) < NZ for s in range(4)]
    bwd_low = [((lane - s) & (LANES - 1)) < NZ for s in range(4)]

    def up_y(vs, s, hs=None):
        n = len(vs)
        hs = [pltpu.roll(v, NZ - s, 1) for v in vs] if hs is None else hs
        return [jnp.where(fwd_low[s], hs[r], hs[(r + 1) % n]) for r in range(n)]

    def down_y(vs, s, hs=None):
        n = len(vs)
        hs = [pltpu.roll(v, NZ + s, 1) for v in vs] if hs is None else hs
        return [jnp.where(bwd_low[s], hs[r - 1], hs[r]) for r in range(n)]

    def ahead(vs):
        return (
            [pltpu.roll(v, nx - 1, 0) for v in vs],
            up_y(vs, 0),
            [fwd_lane(v, 1) for v in vs],
            up_y(vs, 1),
            up_y(vs, 2),
            up_y(vs, 3),
        )

    def behind_one(kind, vs):
        if kind == 0:
            return [pltpu.roll(v, 1, 0) for v in vs]
        if kind == 2:
            return [bwd_lane(v, 1) for v in vs]
        return down_y(vs, max(kind - 2, 0))

    every = range(rows)
    perm = [jnp.exp(logk_of(r)) for r in every]
    perm_a = ahead(perm)
    zero = jnp.zeros((nx, LANES), jnp.float32)
    diag = [static_of(3, r) for r in every]
    for k in range(6):
        trans = []
        for r in every:
            if k < 3:
                m = static_of(k, r)
            else:
                m = fault_s[k - 3, pl.ds(r, nx, stride=rows), :]
            if k == 0:
                live = xpos < nx - 1
            elif k == 1:
                live = None if r < rows - 1 else low
            elif k == 2:
                live = zpos < NZ - 1
            else:
                live = m > 0.0
            a, b = perm[r], perm_a[k][r]
            total = a + b
            t = 2.0 * a * b / total * m
            if live is not None:
                t = jnp.where(live, t, zero)
            g = t / total
            coef[12 + k, r] = g
            trans.append(t)
        back = behind_one(k, trans)
        for r in every:
            coef[2 * k, r] = trans[r]
            coef[2 * k + 1, r] = back[r]
            diag[r] = diag[r] + trans[r] + back[r]
    inv = [1.0 / v for v in diag]
    for k in range(12):
        for r in every:
            coef[k, r] = coef[k, r] * inv[r]

    def sweep(d):
        hs = [pltpu.roll(v, NZ, 1) for v in d]
        ups = [up_y(d, 0, hs)] + [up_y(d, s) for s in (1, 2, 3)]
        dns = [down_y(d, 0, hs)] + [down_y(d, s) for s in (1, 2, 3)]
        out = []
        for r in every:
            v = d[r]
            acc = coef[0, r] * pltpu.roll(v, nx - 1, 0) + coef[1, r] * pltpu.roll(v, 1, 0)
            acc2 = coef[2, r] * ups[0][r] + coef[3, r] * dns[0][r]
            acc = acc + (coef[4, r] * fwd_lane(v, 1) + coef[5, r] * bwd_lane(v, 1))
            for s in (1, 2, 3):
                acc2 = acc2 + coef[4 + 2 * s, r] * ups[s][r]
                acc = acc + coef[5 + 2 * s, r] * dns[s][r]
            out.append(acc + acc2)
        return out

    pres = chebyshev([static_of(4, r) for r in every], inv, sweep)
    for r in every:
        pres_s[pl.ds(r, nx, stride=rows), :] = pres[r]
    pres_a = ahead(pres)
    perm_a = ahead(perm)
    for k in range(6):
        for r in every:
            drop = (pres[r] - pres_a[k][r]) * coef[12 + k, r]
            coef[12 + k, r] = drop * perm_a[k][r]
            coef[18 + k, r] = drop * perm[r]
    before_misfit()
    misfit = [static_of(6, r) * (pres[r] - static_of(5, r)) for r in every]
    adj = chebyshev(misfit, inv, sweep)
    adj_a = ahead(adj)
    total = [zero for r in every]
    for k in range(6):
        rise = [adj_a[k][r] - adj[r] for r in every]
        back = behind_one(k, [rise[r] * coef[18 + k, r] for r in every])
        for r in every:
            total[r] = total[r] + rise[r] * coef[12 + k, r] + back[r]
    for r in every:
        glogk_s[pl.ds(r, nx, stride=rows), :] = total[r]


def fused_kernel(
    nd, nm, rows, parts, axes,
    theta_hbm, basis_hbm, mean_hbm, face_hbm, storage_hbm, sources_hbm, data_hbm, weight_hbm,
    pairs_hbm, mult_hbm, noise_hbm,
    grad_out, pres_out, drift_out,
    basis, theta_v, noise_v, mean_v, face_v, pairs_v, mult_v, own_stat, own_late, stat, late, part, part_in, mine, field,
    fault_s, coef, pres_s, pres_in, glogk_s, gl_b, gl_all, gl_f, gsend, gin, gfin, gall,
    load_sem, copy_sem, noise_sem, send_sem, recv_sem,
):
    cells_ax, modes_ax = axes
    me, mo = lax.axis_index(cells_ax), lax.axis_index(modes_ax)
    chains, modes_n = theta_v.shape
    cells = rows * LANES
    blk = cells // nd
    pairs_n = nm // 2
    core, group = lax.rem(mo, 2), lax.div(mo, 2)
    high, low = lax.div(me, 2), lax.rem(me, 2)
    srows = STAT * rows
    small = [
        (theta_hbm, theta_v),
        (face_hbm, face_v),
        (storage_hbm, own_stat.at[1, pl.ds(0, rows)]),
        (sources_hbm, own_stat.at[1, pl.ds(rows, rows)]),
        (data_hbm, own_late.at[0]),
        (weight_hbm, own_late.at[1]),
        (pairs_hbm, pairs_v),
        (mult_hbm, mult_v),
        (mean_hbm, mean_v),
    ]
    small = [pltpu.make_async_copy(a, b, load_sem.at[i]) for i, (a, b) in enumerate(small)]
    loads = [
        pltpu.make_async_copy(
            basis_hbm.at[pl.ds(k * blk, blk)], basis.at[pl.ds(k * blk, blk)], copy_sem.at[k]
        )
        for k in range(nd)
    ]
    flight = nd // 2
    for load in small + loads[:flight]:
        load.start()

    def block(i, size):
        return pl.ds(pl.multiple_of(i * size, size), size)

    steps = sorted(
        ((dz, dy) for dz in range(nd // 2) for dy in range(2)),
        key=lambda t: -(min(t[0], nd // 2 - t[0]) + 2 * t[1]),
    )

    def cell_of(step):
        return lax.rem(high + step[0], nd // 2) * 2 + lax.rem(low + step[1], 2)

    near = [t for t in steps if t != (0, 0)]
    wide = sorted(
        ((t, dx) for t in steps for dx in range(pairs_n) if (t, dx) != ((0, 0), 0)),
        key=lambda w: -(min(w[0][0], nd // 2 - w[0][0]) + 2 * w[0][1] + 2 * (w[1] > 0)),
    )
    mate = {modes_ax: group * 2 + 1 - core}

    def group_of(dx):
        return lax.rem(group + dx, pairs_n)

    def wide_peer(t, dx):
        return {cells_ax: cell_of(t), modes_ax: group_of(dx) * 2 + core}

    barrier = pltpu.get_barrier_semaphore()
    for peer in [wide_peer(t, dx) for t, dx in wide] + [mate]:
        pl.semaphore_signal(barrier, inc=1, device_id=peer, device_id_type=pl.DeviceIdType.MESH)
    greeted = len(wide) + 1
    sent = []
    count = [0]

    def send(src, dst, peer):
        slot = count[0]
        count[0] += 1
        copy = pltpu.make_async_remote_copy(
            src_ref=src, dst_ref=dst, send_sem=send_sem.at[slot], recv_sem=recv_sem.at[slot],
            device_id=peer, device_id_type=pl.DeviceIdType.MESH,
        )
        copy.start()
        sent.append(copy)
        return copy

    def cell_peer(t):
        return {cells_ax: cell_of(t)}

    for load in small:
        load.wait()
    for f in range(3):
        own_stat[0, f * rows : (f + 1) * rows, :] = jnp.concatenate(
            [face_v[f : f + 1, r * LANES : (r + 1) * LANES] for r in range(rows)], 0
        )
    pairs = pairs_v[...].astype(jnp.float32)
    spare = rows - 3 * parts
    own_stat[1, 2 * rows :, :] = jnp.concatenate(
        [pairs[e : e + 1, p * LANES : (p + 1) * LANES] for e in range(2) for p in range(parts)]
        + [mult_v[...]]
        + ([jnp.zeros((spare, LANES), jnp.float32)] if spare else []),
        0,
    )
    stat[core, block(me, srows), :] = own_stat[core]
    late[:, block(me, rows), :] = own_late[...]
    share = chains // nm
    theta_b = jnp.concatenate(
        [
            theta_v[(2 * x + c) * share : (2 * x + c + 1) * share, :]
            for c in range(2)
            for x in range(pairs_n)
        ],
        0,
    ).astype(jnp.bfloat16)
    half = rows // 2
    stat_got, part_got = [], []
    for k in range(0, nd, 2):
        for load in (k, k + 1):
            loads[load].wait()
            if load + flight < nd:
                loads[load + flight].start()
        got = lax.dot_general(
            theta_b, basis[k * blk : (k + 2) * blk, :], (((1,), (1,)), ((), ())),
            preferred_element_type=jnp.float32,
        )
        for t in range(2 * blk // LANES):
            r = k * (blk // LANES) + t
            part[r // half, pl.ds(r % half, chains, stride=half), :] = (
                got[:, t * LANES : (t + 1) * LANES]
            )
        if k == 0:
            pl.semaphore_wait(barrier, greeted)
            stat_got = [
                send(own_stat.at[core], stat.at[core, block(me, srows)], cell_peer(t))
                for t in near
            ]
        if (k + 2) % (nd // 2) == 0:
            h = k // (nd // 2)
            part_got.append(
                send(part.at[h, block(1 - core, chains // 2 * half)], part_in.at[h], mate)
            )
    noise_load = pltpu.make_async_copy(noise_hbm, noise_v, noise_sem)
    noise_load.start()
    mean = 1.0 / pairs_n * mean_v[...]
    for h in range(2):
        total = part[h, block(core, chains // 2 * half), :].reshape(chains // 2, half, LANES)
        total = total + mean[h * half : (h + 1) * half][None]
        part_got[h].wait_recv()
        total = total + part_in[h].reshape(chains // 2, half, LANES)
        mine[:, h * half : (h + 1) * half, :] = total
    field_got = [
        send(
            mine.at[group_of(dx) * nd + cell_of(t)], field.at[group, block(me, rows)],
            wide_peer(t, dx),
        )
        for t, dx in wide
    ]
    field[group, block(me, rows), :] = mine[group * nd + me]
    late_got = [
        send(own_late, late.at[:, block(me, rows)], cell_peer(t)) for t in near
    ]
    for copy in stat_got:
        copy.wait_recv()
    send(stat.at[core], stat.at[core], mate).wait_recv()

    def before_fields():
        for copy in field_got:
            copy.wait_recv()

    def static_of(f, r):
        if f > STAT + 1:
            return late[f - STAT - 2, pl.ds(r, nd, stride=rows), :]
        h, f = (0, f) if f < STAT else (1, f - STAT)
        return stat[h, pl.ds(f * rows + r, nd, stride=srows), :]

    def logk_of(r):
        value = field[0, pl.ds(r, nd, stride=rows), :]
        for g in range(1, pairs_n):
            value = value + field[g, pl.ds(r, nd, stride=rows), :]
        return value

    def fault_row(x, k):
        return stat[1, pl.ds(x * srows + 2 * rows + k, 1), :]

    def before_misfit():
        for copy in late_got:
            copy.wait_recv()

    chain_physics(
        nd, rows, logk_of, static_of, fault_row, parts, fault_s, coef, pres_s, before_fields,
        before_misfit, glogk_s,
    )

    gl_b[...] = glogk_s[...].astype(jnp.bfloat16)
    spot = block(group * nd + me, rows)
    gl_got = [
        send(gl_b.at[block(cell_of(t), rows)], gl_all.at[core, spot], wide_peer(t, dx))
        for t, dx in wide
    ]
    gl_all[core, spot, :] = gl_b[block(me, rows), :]
    pres_got = [
        send(pres_s.at[block(cell_of(t), rows)], pres_in.at[block(me, rows)], cell_peer(t))
        for t in near
    ]
    pres_in[block(me, rows), :] = pres_s[block(me, rows), :]
    noise_load.wait()
    drift_out[...] = (1.0 - STEP_SIZE) * theta_v[...] + math.sqrt(2.0 * STEP_SIZE) * noise_v[...]
    mate_got = []
    for dx in range(pairs_n):
        for copy, (_, step) in zip(gl_got, wide):
            if step == dx:
                copy.wait_recv()
        held_rows = block(lax.rem(group + pairs_n - dx, pairs_n), nd * rows)
        mate_got.append(send(gl_all.at[core, held_rows], gl_all.at[core, held_rows], mate))
    for copy in mate_got:
        copy.wait_recv()
    held = chains // 2 * rows
    for c in range(2):
        gl_f[c * held : (c + 1) * held, :] = gl_all[c].astype(jnp.float32)
    glogk = jnp.concatenate(
        [gl_f[pl.ds(r, chains, stride=rows), :] for r in range(rows)], 1
    ).astype(jnp.bfloat16)

    width = modes_n // nd

    def piece(i):
        return jnp.dot(
            glogk, basis[:, block(i, width)], preferred_element_type=jnp.float32
        )

    g_got = []
    for first, last in ((0, 2), (2, 4), (4, nd - 1)):
        for k in range(first, last):
            gsend[k] = piece(cell_of(near[k])).astype(jnp.bfloat16)
        for k in range(first, last):
            g_got.append(send(gsend.at[k], gin.at[k], cell_peer(near[k])))
    grad = piece(me)
    for k, copy in enumerate(g_got):
        copy.wait_recv()
        grad = grad + gin[k].astype(jnp.float32)
    gfin[...] = grad.astype(jnp.bfloat16)
    g_got = [send(gfin, gall.at[me], cell_peer(t)) for t in near]
    gall[me] = gfin[...]
    for copy in pres_got:
        copy.wait_recv()
    pres_out[...] = pres_in[...]
    for copy in sent[: -len(near)]:
        copy.wait_send()
    for copy in g_got:
        copy.wait_recv()
    grad_out[...] = gall[...]
    for copy in sent[-len(near) :]:
        copy.wait_send()


def finish_kernel(
    nm, grad_ref, pres_ref, drift_ref, theta_hbm, grad_hbm, pres_hbm, theta_v, grad_v, pres_v, sems
):
    pieces, chains, width = grad_ref.shape
    share = chains // nm
    order = [x * 2 + c for c in range(2) for x in range(nm // 2)]
    count = pres_v.shape[0]
    rows = pres_v.shape[1] // LANES
    for r in range(rows):
        pres_v[:, r * LANES : (r + 1) * LANES] = pres_ref[pl.ds(r, count, stride=rows), :]
    copies = [pltpu.make_async_copy(pres_v, pres_hbm, sems.at[0])]
    copies[0].start()
    group = pieces // 4
    for q in range(4):
        for p in range(q * group, (q + 1) * group):
            cols = slice(p * width, (p + 1) * width)
            piece = grad_ref[p].astype(jnp.float32)
            g = jnp.concatenate(
                [piece[order.index(n) * share : (order.index(n) + 1) * share] for n in range(nm)],
                0,
            )
            grad_v[:, cols] = g
            theta_v[:, cols] = drift_ref[:, cols] - STEP_SIZE * g
        cols = pl.ds(q * group * width, group * width)
        for i, (src, dst) in enumerate(((grad_v, grad_hbm), (theta_v, theta_hbm))):
            copy = pltpu.make_async_copy(src.at[:, cols], dst.at[:, cols], sems.at[1 + 2 * q + i])
            copy.start()
            copies.append(copy)
    for copy in copies:
        copy.wait()


def fast_body(
    theta, basis, mean_logk, face_mult, storage, sources, obs_data, obs_weight,
    fault_pairs, fault_mult, noise,
):
    nd, nm = lax.axis_size("cells"), lax.axis_size("modes")
    cells, modes_n = basis.shape
    chains = theta.shape[1]
    rows = cells // LANES
    parts = fault_mult.shape[0] // LANES
    f32, bf16 = jnp.float32, jnp.bfloat16
    width = modes_n // nd
    pairs_n = nm // 2
    copies = 5 * (nd - 1) + 2 * (pairs_n * nd - 1) + 3 + pairs_n
    vmem = pl.BlockSpec(memory_space=pltpu.VMEM)
    grad, pressure, drift = pl.pallas_call(
        functools.partial(fused_kernel, nd, nm, rows, parts, ("cells", "modes")),
        out_shape=(
            jax.ShapeDtypeStruct((nd, chains, width), bf16),
            jax.ShapeDtypeStruct((nd * rows, LANES), f32),
            jax.ShapeDtypeStruct((chains, modes_n), f32),
        ),
        in_specs=[pl.BlockSpec(memory_space=pl.ANY)] * 11,
        out_specs=(vmem,) * 3,
        scratch_shapes=[
            pltpu.VMEM((cells, modes_n), bf16),
            pltpu.VMEM((chains, modes_n), f32),
            pltpu.VMEM((chains, modes_n), f32),
            pltpu.VMEM((rows, LANES), f32),
            pltpu.VMEM((3, cells), f32),
            pltpu.VMEM((2, parts * LANES), jnp.int32),
            pltpu.VMEM((parts, LANES), f32),
            pltpu.VMEM((2, STAT * rows, LANES), f32),
            pltpu.VMEM((2, rows, LANES), f32),
            pltpu.VMEM((2, nd * STAT * rows, LANES), f32),
            pltpu.VMEM((2, nd * rows, LANES), f32),
            pltpu.VMEM((2, chains * rows // 2, LANES), f32),
            pltpu.VMEM((2, chains // 2 * rows // 2, LANES), f32),
            pltpu.VMEM((pairs_n * nd, rows, LANES), f32),
            pltpu.VMEM((pairs_n, nd * rows, LANES), f32),
            pltpu.VMEM((3, nd * rows, LANES), f32),
            pltpu.VMEM((24, rows, nd, LANES), f32),
            pltpu.VMEM((nd * rows, LANES), f32),
            pltpu.VMEM((nd * rows, LANES), f32),
            pltpu.VMEM((nd * rows, LANES), f32),
            pltpu.VMEM((nd * rows, LANES), bf16),
            pltpu.VMEM((2, chains // 2 * rows, LANES), bf16),
            pltpu.VMEM((chains * rows, LANES), f32),
            pltpu.VMEM((nd - 1, chains, width), bf16),
            pltpu.VMEM((nd - 1, chains, width), bf16),
            pltpu.VMEM((chains, width), bf16),
            pltpu.VMEM((nd, chains, width), bf16),
            pltpu.SemaphoreType.DMA((9,)),
            pltpu.SemaphoreType.DMA((nd,)),
            pltpu.SemaphoreType.DMA,
            pltpu.SemaphoreType.DMA((copies,)),
            pltpu.SemaphoreType.DMA((copies,)),
        ],
        compiler_params=pltpu.CompilerParams(collective_id=0, has_side_effects=True, vmem_limit_bytes=24 << 20),
    )(
        *[pltpu.with_memory_space_constraint(a, pltpu.HBM) for a in (theta.T, basis, mean_logk.reshape(-1, LANES), face_mult, storage.reshape(-1, LANES),
        sources.reshape(-1, LANES), obs_data.reshape(-1, LANES), obs_weight.reshape(-1, LANES),
        fault_pairs.T, fault_mult.reshape(-1, LANES), noise.T)],
    )
    theta_next, grad, pressure = pl.pallas_call(
        functools.partial(finish_kernel, nm),
        out_shape=(
            jax.ShapeDtypeStruct((chains, modes_n), f32),
            jax.ShapeDtypeStruct((chains, modes_n), f32),
            jax.ShapeDtypeStruct((chains // nm, cells), f32),
        ),
        in_specs=[vmem] * 3,
        out_specs=(pl.BlockSpec(memory_space=pl.ANY),) * 3,
        scratch_shapes=[
            pltpu.VMEM((chains, modes_n), f32),
            pltpu.VMEM((chains, modes_n), f32),
            pltpu.VMEM((chains // nm, cells), f32),
            pltpu.SemaphoreType.DMA((9,)),
        ],
        compiler_params=pltpu.CompilerParams(vmem_limit_bytes=16 << 20),
    )(grad, pressure, drift)
    return (theta_next.T, grad.T, pressure)


def choose_body(theta, basis, *rest):
    share = theta.shape[1] // lax.axis_size("modes")
    nx = lax.axis_size("cells")
    whole = basis.shape[0] == NY * NZ and rest[-2].shape[0] % LANES == 0 and 2 * NZ == LANES
    paired = lax.axis_size("modes") % 2 == 0 and 3 * rest[-2].shape[0] // LANES <= basis.shape[0] // LANES
    if paired and share == nx and nx == 8 and whole and basis.shape[1] % (nx * LANES) == 0:
        return fast_body(theta, basis, *rest)
    return body(theta, basis, *rest)


def solution(mesh):
    return jax.shard_map(
        choose_body,
        mesh=mesh,
        in_specs=(
            P("modes", None),
            P("cells", "modes"),
            P("cells"),
            P(None, "cells"),
            P("cells"),
            P("cells"),
            P("cells"),
            P("cells"),
            P("cells", None),
            P("cells"),
            P("modes", None),
        ),
        out_specs=(P("modes", None), P("modes", None), P("modes", "cells")),
        check_vma=False,
    )
```
